32 devices in a mesh: tx: 8 (over z, x), ty: 4 (over y, core).
Axes of the slice: x: 2, y: 2, z: 4, core: 2. Of those that a mesh axis runs over, the one named last changes fastest.
Arguments:
- dynamics_residual: float32 [6, 48, 48, 16], P(None, 'tx', 'ty'), may hold values from -6 to 6
- density: float32 [6, 48, 48, 16], P(None, 'tx', 'ty'), may hold values from 0.5 to 8
- diagonal_gain: float32 [6, 48, 48, 16], P(None, 'tx', 'ty'), may hold values from 0.05 to 2
- vertical_coupling: float32 [6, 48, 48, 16], P(None, 'tx', 'ty'), may hold values from 0.2 to 8
- edge_panel: int32 [6, 4], replicated, may hold values from 0 to 5, as said below
- edge_side: int32 [6, 4], replicated, may hold values from 0 to 3, as said below
- edge_flip: int32 [6, 4], replicated, may hold values from 0 to 1, as said below
Outputs:
- solution: float32 [6, 48, 48, 16], P(None, 'tx', 'ty')
- coarse_correction: float32 [6, 24, 24, 16], P(None, 'tx', 'ty')
The draws below stay inside these ranges and needn't reach their ends.
Inputs may be any that keep to these rules, and one draw needn't show every extreme that they name: The six panels are the faces of a cube, each with its own orientation and label: side s of panel p borders side edge_side[p, s] of panel edge_panel[p, s], the pairing is mutual, and no side borders a side of its own panel. `edge_side`: see edge_panel. `edge_flip`: equal on both sides of a bordering pair.
All inputs are finite; a program needn't handle non-finite values.
Results may differ from the reference program's by a relative error of at most 0.00005.
Values sent between devices are 32-bit elements; how exact they have to be, the bound alone decides.
A program may use at most 64 MiB of HBM per device.

```python
import math
import jax
import jax.numpy as jnp
import numpy as np

LEV = 16
NSIDE = 48


def frame_tables():
    anchors = np.array([[0, 0, 0], [0, 0, 1], [0, 0, 0], [0, 1, 0], [0, 0, 0], [1, 0, 0]])
    first_dirs = np.array([[1, 0, 0], [0, 1, 0], [0, 0, 1], [1, 0, 0], [0, 1, 0], [0, 0, 1]])
    second_dirs = np.array([[0, 1, 0], [1, 0, 0], [1, 0, 0], [0, 0, 1], [0, 0, 1], [0, 1, 0]])
    all_anchors = []
    all_first = []
    all_second = []
    for turn in range(4):
        all_anchors.append(anchors.copy())
        all_first.append(first_dirs.copy())
        all_second.append(second_dirs.copy())
        anchors, first_dirs, second_dirs = (anchors + first_dirs, second_dirs, -first_dirs)
    return (np.stack(all_anchors), np.stack(all_first), np.stack(all_second))


def edge_pairing(key):
    table_anchor, table_first, table_second = frame_tables()
    turns = jax.random.randint(jax.random.fold_in(key, 7), (6,), 0, 4).astype(jnp.int32)
    faces = jnp.arange(6)
    anchor = jnp.asarray(table_anchor, jnp.int32)[turns, faces]
    first_dir = jnp.asarray(table_first, jnp.int32)[turns, faces]
    second_dir = jnp.asarray(table_second, jnp.int32)[turns, faces]
    starts = jnp.stack([anchor, anchor + first_dir, anchor, anchor + second_dir], axis=1)
    ends = jnp.stack([anchor + second_dir, anchor + first_dir + second_dir, anchor + first_dir, anchor + first_dir + second_dir], axis=1)
    labels = jax.random.permutation(jax.random.fold_in(key, 11), 6).astype(jnp.int32)
    starts = jnp.zeros_like(starts).at[labels].set(starts).reshape(24, 3)
    ends = jnp.zeros_like(ends).at[labels].set(ends).reshape(24, 3)
    same = jnp.all(starts[:, None] == starts[None, :], axis=-1) & jnp.all(ends[:, None] == ends[None, :], axis=-1)
    opposite = jnp.all(starts[:, None] == ends[None, :], axis=-1) & jnp.all(ends[:, None] == starts[None, :], axis=-1)
    others = jnp.arange(24)[:, None] != jnp.arange(24)[None, :]
    matched = ((same | opposite) & others).astype(jnp.int32)
    partner = jnp.argmax(matched, axis=1).astype(jnp.int32)
    flip_codes = jnp.sum(opposite.astype(jnp.int32) * matched, axis=1).astype(jnp.int32)
    return (partner.reshape(6, 4), flip_codes.reshape(6, 4))


def draw_edge_panel(key, part):
    partner, flip_codes = edge_pairing(key)
    return (partner // 4).astype(jnp.int32)


def draw_edge_side(key, part):
    partner, flip_codes = edge_pairing(key)
    return (partner % 4).astype(jnp.int32)


def draw_edge_flip(key, part):
    partner, flip_codes = edge_pairing(key)
    return flip_codes.astype(jnp.int32)


def block_scale(stream_key, dims, shards, smallest, high):
    gain = 1.0
    for dim, shards_of in shards:
        heights = jax.random.uniform(jax.random.fold_in(jax.random.fold_in(stream_key, 6), dim), (shards_of,), jnp.float32, smallest / len(shards), high / len(shards))
        gain = gain * jnp.repeat(jnp.exp(heights), dims[dim] // shards_of).reshape((-1,) + (1,) * (len(dims) - 1 - dim))
    return gain


def centred(stream_key, extent, spread, limit, cuts=(), kind=jnp.bfloat16):
    entries = spread * jax.random.normal(stream_key, extent, jnp.float32)
    if cuts:
        entries = entries * block_scale(stream_key, extent, cuts, -0.22, 0.18)
    return jnp.clip(entries, -limit, limit).astype(kind)


def setup_inputs(seed: int = 0) -> dict:
    key_of = jax.random.split(jax.random.key(seed), 8)
    dynamics_residual = centred(key_of[0], (6, NSIDE, NSIDE, LEV), 1.0, 6.0, ((1, 8), (2, 4)), jnp.float32)
    density = jnp.clip(jnp.exp(math.log(8.0) - 2.7725887 * jax.random.uniform(key_of[1], (6, NSIDE, NSIDE, LEV), jnp.float32) ** block_scale(key_of[1], (6, NSIDE, NSIDE, LEV), ((1, 8), (2, 4)), -0.2, 0.2)), 0.5, 8.0)
    diagonal_gain = jnp.clip(jnp.exp(math.log(2.0) - 3.6888794 * jax.random.uniform(key_of[2], (6, NSIDE, NSIDE, LEV), jnp.float32) ** block_scale(key_of[2], (6, NSIDE, NSIDE, LEV), ((1, 8), (2, 4)), -0.2, 0.2)), 0.05, 2.0)
    vertical_coupling = jnp.clip(jnp.exp(math.log(8.0) - 3.6888794 * jax.random.uniform(key_of[3], (6, NSIDE, NSIDE, LEV), jnp.float32) ** block_scale(key_of[3], (6, NSIDE, NSIDE, LEV), ((1, 8), (2, 4)), -0.2, 0.2)), 0.2, 8.0)
    edge_panel = draw_edge_panel(jax.random.fold_in(key_of[7], 71), 0)
    edge_side = draw_edge_side(jax.random.fold_in(key_of[7], 71), 0)
    edge_flip = draw_edge_flip(jax.random.fold_in(key_of[7], 71), 0)
    return dict(dynamics_residual=dynamics_residual, density=density, diagonal_gain=diagonal_gain, vertical_coupling=vertical_coupling, edge_panel=edge_panel, edge_side=edge_side, edge_flip=edge_flip)


relaxation = 0.8


def lower_levels(values):
    return jnp.concatenate([jnp.zeros_like(values[..., :1]), values[..., :-1]], axis=-1)


def upper_levels(values):
    return jnp.concatenate([values[..., 1:], jnp.zeros_like(values[..., :1])], axis=-1)


def vertical_part(grid_field, vertical):
    return vertical * (grid_field - upper_levels(grid_field)) + lower_levels(vertical) * (grid_field - lower_levels(grid_field))


def diagonal_of(cell_gain, vertical, horizontal):
    return cell_gain + 4.0 * horizontal + vertical + lower_levels(vertical)


def neighbour_sum(padded):
    return padded[:, :-2, 1:-1] + padded[:, 2:, 1:-1] + padded[:, 1:-1, :-2] + padded[:, 1:-1, 2:]


def apply_operator(grid_field, padded, cell_gain, vertical, horizontal):
    return cell_gain * grid_field + horizontal * (4.0 * grid_field - neighbour_sum(padded)) + vertical_part(grid_field, vertical)


def restrict(values):
    shaped = values.reshape(values.shape[0], values.shape[1] // 2, 2, values.shape[2] // 2, 2, values.shape[3])
    return shaped.mean(axis=(2, 4))


def prolong(values):
    return jnp.repeat(jnp.repeat(values, 2, axis=1), 2, axis=2)


def panel_padded(grid_field, edge_panel, edge_side, edge_flip):
    strips = jnp.stack([grid_field[:, 0], grid_field[:, -1], grid_field[:, :, 0], grid_field[:, :, -1]])
    sources = strips[edge_side, edge_panel]
    rim_cells = jnp.where(edge_flip[:, :, None, None] == 1, sources[:, :, ::-1], sources)
    padded = jnp.pad(grid_field, ((0, 0), (1, 1), (1, 1), (0, 0)))
    padded = padded.at[:, 0, 1:-1].set(rim_cells[:, 0])
    padded = padded.at[:, -1, 1:-1].set(rim_cells[:, 1])
    padded = padded.at[:, 1:-1, 0].set(rim_cells[:, 2])
    padded = padded.at[:, 1:-1, -1].set(rim_cells[:, 3])
    return padded


def reference(dynamics_residual, density, diagonal_gain, vertical_coupling, edge_panel, edge_side, edge_flip):
    right_side = density * dynamics_residual
    fine_diagonal = diagonal_of(diagonal_gain, vertical_coupling, 1.0)
    smoothed = relaxation * right_side / fine_diagonal
    applied = apply_operator(smoothed, panel_padded(smoothed, edge_panel, edge_side, edge_flip), diagonal_gain, vertical_coupling, 1.0)
    coarse_rhs = restrict(right_side - applied)
    coarse_gain = restrict(diagonal_gain)
    coarse_vertical = restrict(vertical_coupling)
    coarse_diagonal = diagonal_of(coarse_gain, coarse_vertical, 0.25)
    coarse_guess = relaxation * coarse_rhs / coarse_diagonal
    coarse_applied = apply_operator(coarse_guess, panel_padded(coarse_guess, edge_panel, edge_side, edge_flip), coarse_gain, coarse_vertical, 0.25)
    coarse_correction = coarse_guess + relaxation * (coarse_rhs - coarse_applied) / coarse_diagonal
    corrected = smoothed + prolong(coarse_correction)
    final_applied = apply_operator(corrected, panel_padded(corrected, edge_panel, edge_side, edge_flip), diagonal_gain, vertical_coupling, 1.0)
    solution = corrected + relaxation * (right_side - final_applied) / fine_diagonal
    return solution, coarse_correction
```

```python
import functools

import jax
import jax.numpy as jnp
from jax import lax
from jax.experimental import pallas as pl
from jax.experimental.pallas import tpu as pltpu
from jax.sharding import PartitionSpec as P

MESH = pl.DeviceIdType.MESH
relaxation = 0.8
LANES = 128
TILE = 8


def round_up(value, unit):
    return (value + unit - 1) // unit * unit


def kernel(
    nr,
    nc,
    res_hbm,
    den_hbm,
    gain_hbm,
    vert_hbm,
    panel_ref,
    side_ref,
    flip_ref,
    spread,
    small_ref,
    inp,
    packed,
    st_row,
    st_col,
    ex_row,
    ex_col,
    nb_row,
    nb_col,
    corner,
    rx_row,
    rx_col,
    ry_row,
    ry_col,
    in_sem,
    send_sem,
    nb_sem,
    corner_sem,
    row_sem,
    col_sem,
    row_end_sem,
    col_end_sem,
):
    _, panels, rows, cols, levels = inp.shape
    half_r, half_c = rows // 2, cols // 2
    k = cols // rows
    length = half_r
    last = length - 1
    height = spread.shape[1] // 2
    block = st_row.shape[3]
    r = lax.axis_index("tx")
    c = lax.axis_index("ty")
    is_row = (r == 0) | (r == nr - 1)
    is_col = (c == 0) | (c == nc - 1)
    tr = r // (nr - 1)
    tc = c // (nc - 1)
    row_ok = (r > 0, r < nr - 1)
    col_ok = (c > 0, c < nc - 1)

    def row_segment(f, p):
        return k * c + p if f == 0 else nr - 1 - k * c - p

    def col_segment(f):
        return r if f == 0 else nr - 1 - r

    def clamp(x, n):
        return jnp.minimum(jnp.maximum(x, 0), n - 1)

    def partners():
        found = []
        for f in range(2):
            here = c if f == 0 else nc - 1 - c
            for e in range(2):
                for d in (-1, 0, 1):
                    to = here + d
                    found.append((is_row & (to >= 0) & (to < nc), (e * (nr - 1), clamp(to, nc))))
                low = row_segment(f, 0 if f == 0 else k - 1)
                for d in range(-1, k + 1):
                    to = low + d
                    found.append((is_row & (to >= 0) & (to < nr), (clamp(to, nr), e * (nc - 1))))
                g = col_segment(f)
                for d in (-1, 0, 1):
                    to = g + d
                    inside = is_col & (to >= 0) & (to < nr)
                    found.append((inside, (clamp(to, nr), e * (nc - 1))))
                    if d:
                        inside = inside & (g % k == (k - 1 if d == 1 else 0))
                    found.append((inside, (e * (nr - 1), clamp(g // k + d, nc))))
        for dr in (-1, 0, 1):
            for dc in (-1, 0, 1):
                if dr or dc:
                    ok = True
                    if dr:
                        ok = row_ok[(dr + 1) // 2]
                    if dc:
                        ok = col_ok[(dc + 1) // 2] if ok is True else ok & col_ok[(dc + 1) // 2]
                    found.append((ok, (r + dr, c + dc)))
        return found

    def messages():
        found = []
        src_row = st_row.at[tr]
        for f in range(2):
            slot = 4 * f + tr
            to = c if f == 0 else nc - 1 - c
            for e in range(2):
                found.append((is_row, (e * (nr - 1), to), src_row, rx_row.at[slot], row_sem))
        for f in range(2):
            slot = 4 * f + 2 + tc
            g = col_segment(f)
            for e in range(2):
                found.append(
                    (is_col, (g, e * (nc - 1)), st_col.at[tc], rx_col.at[slot], col_sem)
                )
                found.append(
                    (
                        is_col,
                        (e * (nr - 1), g // k),
                        st_col.at[tc],
                        rx_row.at[slot, r % k],
                        row_sem,
                    )
                )
        for p in range(k):
            for f in range(2):
                slot = 4 * f + tr
                g = row_segment(f, p)
                for e in range(2):
                    found.append(
                        (is_row, (g, e * (nc - 1)), st_row.at[tr, p], rx_col.at[slot], col_sem)
                    )
        for h in range(2):
            for f in range(2):
                d = 1 if h != f else -1
                end = 0 if d == 1 else 1
                for p in range(k):
                    slot = 4 * f + tr
                    src = ex_row.at[tr, p, h]
                    to = row_segment(f, p) + d
                    ok = is_row & (to >= 0) & (to < nr)
                    for e in range(2):
                        found.append(
                            (
                                ok,
                                (clamp(to, nr), e * (nc - 1)),
                                src,
                                ry_col.at[end, slot],
                                col_end_sem.at[end],
                            )
                        )
                    if p == (k - 1 if h == 1 else 0):
                        to = (c if f == 0 else nc - 1 - c) + d
                        ok = is_row & (to >= 0) & (to < nc)
                        for e in range(2):
                            found.append(
                                (
                                    ok,
                                    (e * (nr - 1), clamp(to, nc)),
                                    src,
                                    ry_row.at[end, slot],
                                    row_end_sem.at[end],
                                )
                            )
                slot = 4 * f + 2 + tc
                src = ex_col.at[tc, h]
                g = col_segment(f)
                to = g + d
                ok = is_col & (to >= 0) & (to < nr)
                far = ok & (g % k == (k - 1 if d == 1 else 0))
                for e in range(2):
                    found.append(
                        (ok, (clamp(to, nr), e * (nc - 1)), src, ry_col.at[end, slot], col_end_sem.at[end])
                    )
                    found.append(
                        (
                            far,
                            (e * (nr - 1), clamp(g // k + d, nc)),
                            src,
                            ry_row.at[end, slot],
                            row_end_sem.at[end],
                        )
                    )
        border = len(found)
        for s in range(2):
            found.append(
                (row_ok[s], (r + 2 * s - 1, c), st_row.at[s], nb_row.at[1 - s], nb_sem.at[1 - s])
            )
            found.append(
                (
                    col_ok[s],
                    (r, c + 2 * s - 1),
                    st_col.at[s],
                    nb_col.at[1 - s],
                    nb_sem.at[3 - s],
                )
            )
        for s in range(2):
            for w in range(2):
                at = 2 * (1 - s) + 1 - w
                found.append(
                    (
                        row_ok[s] & col_ok[w],
                        (r + 2 * s - 1, c + 2 * w - 1),
                        ex_row.at[s, w * (k - 1), w],
                        corner.at[at],
                        corner_sem.at[at],
                    )
                )
        return found, border

    def same(dest):
        return (dest[0] == r) & (dest[1] == c)

    loads = [
        pltpu.make_async_copy(source, inp.at[i], in_sem.at[i])
        for i, source in enumerate((gain_hbm, vert_hbm, den_hbm, res_hbm))
    ]
    for load in loads:
        load.start()

    barrier = pltpu.get_barrier_semaphore()
    expected = jnp.int32(0)
    for active, dest in partners():
        go = active & jnp.logical_not(same(dest))
        expected = expected + go.astype(jnp.int32)

        @pl.when(go)
        def _():
            pl.semaphore_signal(barrier, inc=1, device_id=dest, device_id_type=MESH)

    lane = lax.broadcasted_iota(jnp.int32, (TILE, LANES), 1)
    sub = lax.broadcasted_iota(jnp.int32, (height, LANES), 0)
    level = lane[:1] % levels
    first_level = level == 0
    last_level = level == levels - 1

    def lower(x):
        return jnp.where(first_level, 0.0, pltpu.roll(x, 1, 1))

    def upper(x):
        return jnp.where(last_level, 0.0, pltpu.roll(x, LANES - 1, 1))

    def pick_tables(side):
        index = lane
        code = jnp.zeros_like(lane)
        for p in range(panels):
            here = lane // levels == p
            index = jnp.where(here, panel_ref[side, p] * levels + lane % levels, index)
            code = jnp.where(here, flip_ref[side, p] * 4 + side_ref[side, p], code)
        return index, code

    row_pick = pick_tables(tr)
    col_pick = pick_tables(2 + tc)

    def pack(value):
        filler = jnp.zeros((rows, cols, LANES - panels * levels), jnp.float32)
        return jnp.concatenate([value[p] for p in range(panels)] + [filler], axis=-1)

    def split(which, value):
        packed[which, :, :cols, :] = value
        if packed.shape[2] > cols:
            packed[which, :, cols:, :] = jnp.zeros(
                (rows, packed.shape[2] - cols, LANES), jnp.float32
            )
        return [
            [packed[which, y, pl.ds(b, height, stride=2), :] for b in range(2)]
            for y in range(rows)
        ]

    def fine(fun):
        return [[fun(y, b) for b in range(2)] for y in range(rows)]

    small = range(half_r)

    def block_mean(values, i):
        y = 2 * i
        return 0.25 * (values[y][0] + values[y][1] + values[y + 1][0] + values[y + 1][1])

    loads[0].wait()
    gain = split(1, pack(inp[0]))
    loads[1].wait()
    vertical = split(2, pack(inp[1]))
    low_vert = fine(lambda y, b: lower(vertical[y][b]))
    inverse = fine(
        lambda y, b: relaxation / (gain[y][b] + 4.0 + vertical[y][b] + low_vert[y][b])
    )
    c_vert = [block_mean(vertical, i) for i in small]
    c_low = [lower(c_vert[i]) for i in small]
    c_inv = [relaxation / (block_mean(gain, i) + 1.0 + c_vert[i] + c_low[i]) for i in small]
    loads[2].wait()
    loads[3].wait()
    right_side = split(0, pack(inp[2] * inp[3]))
    smoothed = fine(lambda y, b: inverse[y][b] * right_side[y][b])

    def inner(y, b):
        x = smoothed[y][b]
        return vertical[y][b] * upper(x) + low_vert[y][b] * lower(x)

    coupled = fine(inner)
    column = fine(lambda y, b: coupled[y][b] + (1.0 - relaxation) * right_side[y][b])
    north = [smoothed[2 * i][0] + smoothed[2 * i][1] for i in small]
    south = [smoothed[2 * i + 1][0] + smoothed[2 * i + 1][1] for i in small]
    west = [smoothed[2 * i][0] + smoothed[2 * i + 1][0] for i in small]
    east = [smoothed[2 * i][1] + smoothed[2 * i + 1][1] for i in small]
    from_w = [pltpu.roll(east[i], 1, 0) for i in small]
    from_e = [pltpu.roll(west[i], height - 1, 0) for i in small]
    start_w = sub % length == 0
    start_e = sub % length == last
    edge_w = sub == 0
    edge_e = sub == half_c - 1

    def bare(i):
        total = block_mean(column, i) + 0.5 * (north[i] + south[i])
        beside = None
        if i > 0:
            beside = south[i - 1]
        if i < half_r - 1:
            beside = north[i + 1] if beside is None else beside + north[i + 1]
        return total if beside is None else total + 0.25 * beside

    plain = [bare(i) for i in small]

    def partial_guess(i, mask_w, mask_e):
        beside = jnp.where(mask_w, 0.0, from_w[i]) + jnp.where(mask_e, 0.0, from_e[i])
        return c_inv[i] * (plain[i] + 0.25 * beside)

    by_tile = [partial_guess(i, edge_w, edge_e) for i in small]
    by_piece = by_tile if k == 1 else [partial_guess(i, start_w, start_e) for i in small]

    def put(ref, at, value):
        ref[at : at + value.shape[0], :] = value

    for s in range(2):
        y = s * (rows - 1)
        i0, i1 = (0, 1) if s == 0 else (half_r - 1, half_r - 2)
        out = north[0] if s == 0 else south[half_r - 1]
        for p in range(k):
            lo, hi = p * length, p * length + last
            seg = slice(lo, hi + 1)
            one = lambda x, j: x[j : j + 1]
            a, b, g = (st_row.at[s, p, q] for q in range(3))
            put(a, 0, smoothed[y][0][seg])
            put(a, length, smoothed[y][1][seg])
            put(a, 2 * length, one(c_inv[i1], lo))
            put(a, 2 * length + 1, one(c_inv[i1], hi))
            put(b, 0, by_piece[i0][seg])
            put(b, length, by_piece[i1][seg])
            put(b, 2 * length, one(west[i0], lo))
            put(b, 2 * length + 1, one(east[i0], hi))
            put(g, 0, c_inv[i0][seg])
            put(g, length, c_vert[i0][seg])
            put(g, 2 * length, one(west[i1], lo))
            put(g, 2 * length + 1, one(east[i1], hi))
            for h in range(2):
                j, j1 = (lo, lo + 1) if h == 0 else (hi, hi - 1)
                side = west if h == 0 else east
                x = ex_row.at[s, p, h]
                put(x, 0, one(by_piece[i0], j))
                put(x, 1, one(c_inv[i0], j))
                put(x, 2, one(side[i0], j))
                put(x, 3, one(side[i1], j))
                put(x, 4, one(out, j))
                put(x, 5, one(out, j1))
    for s in range(2):
        j0, j1 = (0, 1) if s == 0 else (half_c - 1, half_c - 2)
        out = west if s == 0 else east
        a, b, g = (st_col.at[s, q] for q in range(3))
        at0 = lambda x: x[j0 : j0 + 1]
        at1 = lambda x: x[j1 : j1 + 1]
        for y in range(rows):
            put(a, (y % 2) * length + y // 2, at0(smoothed[y][s]))
        put(a, 2 * length, at1(c_inv[0]))
        put(a, 2 * length + 1, at1(c_inv[half_r - 1]))
        for i in small:
            put(b, i, at0(by_tile[i]))
            put(b, length + i, at1(by_tile[i]))
            put(g, i, at0(c_inv[i]))
            put(g, length + i, at0(c_vert[i]))
        put(b, 2 * length, at0(north[0]))
        put(b, 2 * length + 1, at0(south[half_r - 1]))
        put(g, 2 * length, at1(north[0]))
        put(g, 2 * length + 1, at1(south[half_r - 1]))
        for h in range(2):
            i0, i1 = (0, 1) if h == 0 else (half_r - 1, half_r - 2)
            side = north[0] if h == 0 else south[half_r - 1]
            x = ex_col.at[s, h]
            put(x, 0, at0(by_tile[i0]))
            put(x, 1, at0(c_inv[i0]))
            put(x, 2, at0(side))
            put(x, 3, at1(side))
            put(x, 4, at0(out[i0]))
            put(x, 5, at0(out[i1]))

    sends, border = messages()
    pl.semaphore_wait(barrier, expected)
    for m, (active, dest, src, dst, sem) in enumerate(sends):
        mine = same(dest)

        @pl.when(active & jnp.logical_not(mine) if m < border else active)
        def _():
            pltpu.make_async_remote_copy(
                src_ref=src,
                dst_ref=dst,
                send_sem=send_sem.at[m],
                recv_sem=sem,
                device_id=dest,
                device_id_type=MESH,
            ).start()

        if m < border:

            @pl.when(active & mine)
            def _():
                pltpu.make_async_copy(src, dst, sem).start()

    def beside(y, b):
        x = smoothed[y][b]
        total = coupled[y][b] + smoothed[y][1 - b]
        if y > 0:
            total = total + smoothed[y - 1][b]
        if y < rows - 1:
            total = total + smoothed[y + 1][b]
        return total

    partial = fine(beside)

    def arrived(ref, sem):
        pltpu.make_async_copy(ref, ref, sem).wait()

    for s in range(2):

        @pl.when(row_ok[s])
        def _():
            arrived(nb_row.at[s], nb_sem.at[s])

        @pl.when(col_ok[s])
        def _():
            arrived(nb_col.at[s], nb_sem.at[2 + s])

        for w in range(2):

            @pl.when(row_ok[s] & col_ok[w])
            def _():
                arrived(corner.at[2 * s + w], corner_sem.at[2 * s + w])

    order = list(range(2 * length))[::-1] + [2 * length + 1, 2 * length]
    other = (
        list(range(length))[::-1]
        + list(range(length, 2 * length))[::-1]
        + [2 * length + 1, 2 * length]
    )
    sublane = lax.broadcasted_iota(jnp.int32, (block, LANES), 0)

    def flip_index(perm):
        index = sublane
        for at, source in enumerate(perm):
            index = jnp.where(sublane == at, source, index)
        return index

    flips = [flip_index(order), flip_index(other), flip_index(other)]

    def choose(read, pick, f):
        index, code = pick
        taken = None
        for t in range(4):
            moved = jnp.take_along_axis(read(4 * f + t), index, axis=1, mode="promise_in_bounds")
            taken = moved if taken is None else jnp.where(code == 4 * f + t, moved, taken)
        return taken

    def select(plainly, reverse, pick, group):
        straight = choose(plainly, pick, 0)
        turned = choose(reverse, pick, 1)
        if group is not None:
            turned = jnp.take_along_axis(turned, flips[group], axis=0, mode="promise_in_bounds")
        return jnp.where(pick[1] >= 4, turned, straight)

    @pl.when(is_row)
    def _():
        arrived(rx_row, row_sem)
        for p in range(k):
            for q in range(3):
                nb_row[tr, p, q] = select(
                    lambda s: rx_row[s, p, q], lambda s: rx_row[s, k - 1 - p, q], row_pick, q
                )
        for w in range(2):

            @pl.when(col_ok[w])
            def _():
                arrived(ry_row.at[w], row_end_sem.at[w])
                read = lambda s: ry_row[w, s]
                corner[2 * tr + w] = select(read, read, row_pick, None)

    @pl.when(is_col)
    def _():
        arrived(rx_col, col_sem)
        for q in range(3):
            read = lambda s: rx_col[s, q]
            nb_col[tc, q] = select(read, read, col_pick, q)
        for s in range(2):

            @pl.when(row_ok[s])
            def _():
                arrived(ry_col.at[s], col_end_sem.at[s])
                read = lambda slot: ry_col[s, slot]
                value = select(read, read, col_pick, None)
                corner[2 * s + tc, 0:2, :] = value[0:2]
                corner[2 * s + tc, 2:4, :] = value[4:6]
                corner[2 * s + tc, 4:6, :] = value[2:4]

    @pl.when(is_row & is_col)
    def _():
        at = 2 * tr + tc
        corner[at, 0:2, :] = jnp.zeros((2, LANES), jnp.float32)
        for q in range(2):
            rows_z = nb_col[tc, 1 + q]
            rows_x = nb_row[tr, tc * (k - 1), 1 + q]
            corner[at, 2 + q : 3 + q, :] = jnp.where(
                tr == 0, rows_z[2 * length : 2 * length + 1], rows_z[2 * length + 1 : 2 * length + 2]
            )
            corner[at, 4 + q : 5 + q, :] = jnp.where(
                tc == 0, rows_x[2 * length : 2 * length + 1], rows_x[2 * length + 1 : 2 * length + 2]
            )

    def zeros(count):
        return [jnp.zeros((count, LANES), jnp.float32)] if count else []

    def stack(lines, total):
        used = sum(x.shape[0] for x in lines)
        return jnp.concatenate(list(lines) + zeros(total - used), axis=0)

    tall_z = round_up(half_r, TILE)
    flat = 2 * length

    class Strip:
        pass

    def strip(read, pieces, ends, total, own):
        def gather(q, at):
            return stack([read(p, q, slice(at, at + length)) for p in range(pieces)], total)

        def sides(first, final):
            lines = []
            for p in range(pieces):
                lines += [first(p)] + zeros(length - 2) + [final(p)]
            return stack(lines, total)

        def lateral(q):
            return sides(
                lambda p: ends[0][q] if p == 0 else read(p - 1, 1 + q, slice(flat + 1, flat + 2)),
                lambda p: ends[1][q]
                if p == pieces - 1
                else read(p + 1, 1 + q, slice(flat, flat + 1)),
            )

        x = Strip()
        x.even, x.odd = gather(0, 0), gather(0, length)
        x.pair = x.even + x.odd
        inv1 = sides(
            lambda p: read(p, 0, slice(flat, flat + 1)),
            lambda p: read(p, 0, slice(flat + 1, flat + 2)),
        )
        x.inv, x.vert = gather(2, 0), gather(2, length)
        x.guess = gather(1, 0) + 0.25 * x.inv * (lateral(0) + own)
        x.inside = gather(1, length) + 0.25 * inv1 * lateral(1)
        return x

    def corner_row(s, w, at):
        return corner[2 * s + w, at : at + 1, :]

    row_strip = []
    for s in range(2):
        own = north[0] if s == 0 else south[half_r - 1]
        ends = [[corner_row(s, w, 2 + q) for q in range(2)] for w in range(2)]
        row_strip.append(
            strip(lambda p, q, rows_: nb_row[s, p, q, rows_, :], k, ends, height, own)
        )
    col_strip = []
    for w in range(2):
        j = w * (half_c - 1)
        faces = west if w == 0 else east
        own = stack([faces[i][j : j + 1] for i in small], tall_z)
        ends = [[corner_row(s, w, 4 + q) for q in range(2)] for s in range(2)]
        col_strip.append(
            strip(lambda p, q, rows_: nb_col[w, q, rows_, :], 1, ends, tall_z, own)
        )

    guess = []
    for i in small:
        lateral = jnp.where(edge_w, col_strip[0].pair[i : i + 1], 0.0)
        lateral = lateral + jnp.where(edge_e, col_strip[1].pair[i : i + 1], 0.0)
        if i == 0:
            lateral = lateral + row_strip[0].pair
        if i == half_r - 1:
            lateral = lateral + row_strip[1].pair
        guess.append(by_tile[i] + 0.25 * c_inv[i] * lateral)

    row_side = [[None] * 2 for _ in range(2)]
    col_side = [[None] * 2 for _ in range(2)]
    for s in range(2):
        for w in range(2):
            faces = nb_row[s, w * (k - 1), 1, flat + w : flat + w + 1, :]
            faces = faces + nb_col[w, 1, flat + s : flat + s + 1, :]
            there = corner_row(s, w, 0) + 0.25 * corner_row(s, w, 1) * faces
            tip = (r == s * (nr - 1)) & (c == w * (nc - 1))
            jr, jc = w * (half_c - 1), s * (half_r - 1)
            row_side[s][w] = jnp.where(tip, col_strip[w].guess[jc : jc + 1], there)
            col_side[w][s] = jnp.where(tip, row_strip[s].guess[jr : jr + 1], there)

    def relax(x, ends, own, count):
        total = x.guess.shape[0]
        at = lax.broadcasted_iota(jnp.int32, (total, LANES), 0)
        around = x.inside + own
        around = around + jnp.where(at == 0, ends[0], pltpu.roll(x.guess, 1, 0))
        around = around + jnp.where(at == count - 1, ends[1], pltpu.roll(x.guess, total - 1, 0))
        column = x.vert * upper(x.guess) + lower(x.vert) * lower(x.guess)
        return (2.0 - relaxation) * x.guess + x.inv * (0.25 * around + column)

    row_fix = [
        relax(row_strip[s], row_side[s], guess[s * (half_r - 1)], half_c) for s in range(2)
    ]
    col_fix = []
    for w in range(2):
        j = w * (half_c - 1)
        own = stack([guess[i][j : j + 1] for i in small], tall_z)
        col_fix.append(relax(col_strip[w], col_side[w], own, half_r))

    def from_left(x, line):
        return jnp.where(edge_w, line, pltpu.roll(x, 1, 0))

    def from_right(x, line):
        return jnp.where(edge_e, line, pltpu.roll(x, height - 1, 0))

    correction = []
    for i in small:
        x = guess[i]
        around = from_left(x, col_strip[0].guess[i : i + 1])
        around = around + from_right(x, col_strip[1].guess[i : i + 1])
        around = around + (guess[i - 1] if i > 0 else row_strip[0].guess)
        around = around + (guess[i + 1] if i < half_r - 1 else row_strip[1].guess)
        levels_part = c_vert[i] * upper(x) + c_low[i] * lower(x)
        correction.append((2.0 - relaxation) * x + c_inv[i] * (0.25 * around + levels_part))
        small_ref[i] = correction[i]

    def outer(y, b):
        at = (y % 2) * length + y // 2
        source = col_strip[b]
        line = (source.even if y % 2 == 0 else source.odd)[y // 2 : y // 2 + 1]
        if b == 0:
            total = partial[y][b] + from_left(smoothed[y][1], line)
        else:
            total = partial[y][b] + from_right(smoothed[y][0], line)
        if y == 0:
            total = total + (row_strip[0].even if b == 0 else row_strip[0].odd)
        if y == rows - 1:
            total = total + (row_strip[1].even if b == 0 else row_strip[1].odd)
        return total

    c_up = [upper(x) for x in correction]
    c_down = [lower(x) for x in correction]
    left = [from_left(correction[i], col_fix[0][i : i + 1]) for i in small]
    right = [from_right(correction[i], col_fix[1][i : i + 1]) for i in small]
    for y in range(rows):
        i = y // 2
        next_i = i - 1 if y % 2 == 0 else i + 1
        for b in range(2):
            total = outer(y, b) + 2.0 * correction[i]
            total = total + vertical[y][b] * c_up[i] + low_vert[y][b] * c_down[i]
            if next_i < 0:
                total = total + row_fix[0]
            elif next_i >= half_r:
                total = total + row_fix[1]
            else:
                total = total + correction[next_i]
            total = total + (left if b == 0 else right)[i]
            first = (2.0 - relaxation) * smoothed[y][b] + (1.0 - relaxation) * correction[i]
            spread[y, pl.ds(b, height, stride=2), :] = first + inverse[y][b] * total

    for m, (active, dest, src, dst, sem) in enumerate(sends):

        @pl.when(active & jnp.logical_not(same(dest)) if m < border else active)
        def _():
            pltpu.make_async_copy(src, src, send_sem.at[m]).wait()


def unpack(spread, small_ref, sol_ref, corr_ref):
    panels, _, cols, levels = sol_ref.shape
    half_c = corr_ref.shape[2]
    for p in range(panels):
        lanes = slice(p * levels, (p + 1) * levels)
        sol_ref[p] = spread[:, :cols, lanes]
        corr_ref[p] = small_ref[:, :half_c, lanes]


def solution(mesh):
    nr, nc = mesh.shape["tx"], mesh.shape["ty"]

    def shards(residual, density, gain, vertical, edge_panel, edge_side, edge_flip):
        panels, rows, cols, levels = residual.shape
        k = cols // rows
        assert cols == k * rows and rows % 2 == 0 and panels * levels <= LANES
        assert rows >= 6 and nr > 1 and nc > 1
        block = round_up(rows + 2, TILE)
        height = round_up(cols // 2, TILE)
        tall = 2 * height
        f32 = jnp.float32
        count = 4 + 8 + 4 * k + 8 * k + 8 + 16 + 4 + 4
        spread, small = pl.pallas_call(
            functools.partial(kernel, nr, nc),
            out_shape=(
                jax.ShapeDtypeStruct((rows, tall, LANES), f32),
                jax.ShapeDtypeStruct((rows // 2, height, LANES), f32),
            ),
            in_specs=[pl.BlockSpec(memory_space=pl.ANY)] * 4
            + [pl.BlockSpec(memory_space=pltpu.SMEM)] * 3,
            out_specs=(pl.BlockSpec(memory_space=pltpu.VMEM),) * 2,
            scratch_shapes=[
                pltpu.VMEM((4, panels, rows, cols, levels), f32),
                pltpu.VMEM((3, rows, tall, LANES), f32),
                pltpu.VMEM((3, k, 3, block, LANES), f32),
                pltpu.VMEM((3, 3, block, LANES), f32),
                pltpu.VMEM((3, k, 2, TILE, LANES), f32),
                pltpu.VMEM((3, 2, TILE, LANES), f32),
                pltpu.VMEM((3, k, 3, block, LANES), f32),
                pltpu.VMEM((3, 3, block, LANES), f32),
                pltpu.VMEM((5, TILE, LANES), f32),
                pltpu.VMEM((8, k, 3, block, LANES), f32),
                pltpu.VMEM((8, 3, block, LANES), f32),
                pltpu.VMEM((2, 8, TILE, LANES), f32),
                pltpu.VMEM((2, 8, TILE, LANES), f32),
                pltpu.SemaphoreType.DMA((4,)),
                pltpu.SemaphoreType.DMA((count,)),
                pltpu.SemaphoreType.DMA((4,)),
                pltpu.SemaphoreType.DMA((4,)),
                pltpu.SemaphoreType.DMA,
                pltpu.SemaphoreType.DMA,
                pltpu.SemaphoreType.DMA((2,)),
                pltpu.SemaphoreType.DMA((2,)),
            ],
            compiler_params=pltpu.CompilerParams(collective_id=0, has_side_effects=True),
        )(residual, density, gain, vertical, edge_panel.T, edge_side.T, edge_flip.T)
        return pl.pallas_call(
            unpack,
            out_shape=(
                jax.ShapeDtypeStruct(residual.shape, f32),
                jax.ShapeDtypeStruct((panels, rows // 2, cols // 2, levels), f32),
            ),
            in_specs=[pl.BlockSpec(memory_space=pltpu.VMEM)] * 2,
            out_specs=(pl.BlockSpec(memory_space=pltpu.VMEM),) * 2,
        )(spread, small)

    fields = P(None, "tx", "ty", None)
    return jax.shard_map(
        shards,
        mesh=mesh,
        in_specs=(fields,) * 4 + (P(),) * 3,
        out_specs=(fields, fields),
        check_vma=False,
    )
```

```python
import functools

import jax
import jax.numpy as jnp
from jax import lax
from jax.experimental import pallas as pl
from jax.experimental.pallas import tpu as pltpu
from jax.sharding import PartitionSpec as P

MESH = pl.DeviceIdType.MESH
relaxation = 0.8
LANES = 128
TILE = 8


def round_up(value, unit):
    return (value + unit - 1) // unit * unit


def kernel(
    nr,
    nc,
    res_hbm,
    den_hbm,
    gain_hbm,
    vert_hbm,
    panel_hbm,
    side_hbm,
    flip_hbm,
    spread,
    small_ref,
    inp,
    tables,
    packed,
    st_row,
    st_col,
    ex_row,
    ex_col,
    nb_row,
    nb_col,
    corner,
    rx_row,
    rx_col,
    ry_row,
    ry_col,
    in_sem,
    table_sem,
    send_sem,
    nb_sem,
    corner_sem,
    row_sem,
    col_sem,
    row_end_sem,
    col_end_sem,
):
    _, panels, rows, cols, levels = inp.shape
    half_r, half_c = rows // 2, cols // 2
    k = cols // rows
    length = half_r
    last = length - 1
    height = spread.shape[1] // 2
    block = st_row.shape[3]
    r = lax.axis_index("tx")
    c = lax.axis_index("ty")
    is_row = (r == 0) | (r == nr - 1)
    is_col = (c == 0) | (c == nc - 1)
    tr = r // (nr - 1)
    tc = c // (nc - 1)
    row_ok = (r > 0, r < nr - 1)
    col_ok = (c > 0, c < nc - 1)

    def row_segment(f, p):
        return k * c + p if f == 0 else nr - 1 - k * c - p

    def col_segment(f):
        return r if f == 0 else nr - 1 - r

    def clamp(x, n):
        return jnp.minimum(jnp.maximum(x, 0), n - 1)

    def partners():
        found = []
        for f in range(2):
            here = c if f == 0 else nc - 1 - c
            for e in range(2):
                for d in (-1, 0, 1):
                    to = here + d
                    found.append((is_row & (to >= 0) & (to < nc), (e * (nr - 1), clamp(to, nc))))
                low = row_segment(f, 0 if f == 0 else k - 1)
                for d in range(-1, k + 1):
                    to = low + d
                    found.append((is_row & (to >= 0) & (to < nr), (clamp(to, nr), e * (nc - 1))))
                g = col_segment(f)
                for d in (-1, 0, 1):
                    to = g + d
                    inside = is_col & (to >= 0) & (to < nr)
                    found.append((inside, (clamp(to, nr), e * (nc - 1))))
                    if d:
                        inside = inside & (g % k == (k - 1 if d == 1 else 0))
                    found.append((inside, (e * (nr - 1), clamp(g // k + d, nc))))
        for dr in (-1, 0, 1):
            for dc in (-1, 0, 1):
                if dr or dc:
                    ok = True
                    if dr:
                        ok = row_ok[(dr + 1) // 2]
                    if dc:
                        ok = col_ok[(dc + 1) // 2] if ok is True else ok & col_ok[(dc + 1) // 2]
                    found.append((ok, (r + dr, c + dc)))
        return found

    def messages():
        found = []
        src_row = st_row.at[tr]
        for f in range(2):
            slot = 4 * f + tr
            to = c if f == 0 else nc - 1 - c
            for e in range(2):
                found.append((is_row, (e * (nr - 1), to), src_row, rx_row.at[slot], row_sem))
        for f in range(2):
            slot = 4 * f + 2 + tc
            g = col_segment(f)
            for e in range(2):
                found.append(
                    (is_col, (g, e * (nc - 1)), st_col.at[tc], rx_col.at[slot], col_sem)
                )
                found.append(
                    (
                        is_col,
                        (e * (nr - 1), g // k),
                        st_col.at[tc],
                        rx_row.at[slot, r % k],
                        row_sem,
                    )
                )
        for p in range(k):
            for f in range(2):
                slot = 4 * f + tr
                g = row_segment(f, p)
                for e in range(2):
                    found.append(
                        (is_row, (g, e * (nc - 1)), st_row.at[tr, p], rx_col.at[slot], col_sem)
                    )
        for h in range(2):
            for f in range(2):
                d = 1 if h != f else -1
                end = 0 if d == 1 else 1
                for p in range(k):
                    slot = 4 * f + tr
                    src = ex_row.at[tr, p, h]
                    to = row_segment(f, p) + d
                    ok = is_row & (to >= 0) & (to < nr)
                    for e in range(2):
                        found.append(
                            (
                                ok,
                                (clamp(to, nr), e * (nc - 1)),
                                src,
                                ry_col.at[end, slot],
                                col_end_sem.at[end],
                            )
                        )
                    if p == (k - 1 if h == 1 else 0):
                        to = (c if f == 0 else nc - 1 - c) + d
                        ok = is_row & (to >= 0) & (to < nc)
                        for e in range(2):
                            found.append(
                                (
                                    ok,
                                    (e * (nr - 1), clamp(to, nc)),
                                    src,
                                    ry_row.at[end, slot],
                                    row_end_sem.at[end],
                                )
                            )
                slot = 4 * f + 2 + tc
                src = ex_col.at[tc, h]
                g = col_segment(f)
                to = g + d
                ok = is_col & (to >= 0) & (to < nr)
                far = ok & (g % k == (k - 1 if d == 1 else 0))
                for e in range(2):
                    found.append(
                        (ok, (clamp(to, nr), e * (nc - 1)), src, ry_col.at[end, slot], col_end_sem.at[end])
                    )
                    found.append(
                        (
                            far,
                            (e * (nr - 1), clamp(g // k + d, nc)),
                            src,
                            ry_row.at[end, slot],
                            row_end_sem.at[end],
                        )
                    )
        border = len(found)
        for s in range(2):
            found.append(
                (row_ok[s], (r + 2 * s - 1, c), st_row.at[s], nb_row.at[1 - s], nb_sem.at[1 - s])
            )
            found.append(
                (
                    col_ok[s],
                    (r, c + 2 * s - 1),
                    st_col.at[s],
                    nb_col.at[1 - s],
                    nb_sem.at[3 - s],
                )
            )
        for s in range(2):
            for w in range(2):
                at = 2 * (1 - s) + 1 - w
                found.append(
                    (
                        row_ok[s] & col_ok[w],
                        (r + 2 * s - 1, c + 2 * w - 1),
                        ex_row.at[s, w * (k - 1), w],
                        corner.at[at],
                        corner_sem.at[at],
                    )
                )
        return found, border

    def same(dest):
        return (dest[0] == r) & (dest[1] == c)

    loads = [
        pltpu.make_async_copy(source, inp.at[i], in_sem.at[i])
        for i, source in enumerate((gain_hbm, vert_hbm, den_hbm, res_hbm))
    ]
    for load in loads:
        load.start()
    table_loads = [
        pltpu.make_async_copy(source, tables.at[i], table_sem.at[i])
        for i, source in enumerate((panel_hbm, side_hbm, flip_hbm))
    ]
    for load in table_loads:
        load.start()

    barrier = pltpu.get_barrier_semaphore()
    expected = jnp.int32(0)
    for active, dest in partners():
        go = active & jnp.logical_not(same(dest))
        expected = expected + go.astype(jnp.int32)

        @pl.when(go)
        def _():
            pl.semaphore_signal(barrier, inc=1, device_id=dest, device_id_type=MESH)

    lane = lax.broadcasted_iota(jnp.int32, (TILE, LANES), 1)
    sub = lax.broadcasted_iota(jnp.int32, (height, LANES), 0)
    level = lane[:1] % levels
    first_level = level == 0
    last_level = level == levels - 1

    def lower(x):
        return jnp.where(first_level, 0.0, pltpu.roll(x, 1, 1))

    def upper(x):
        return jnp.where(last_level, 0.0, pltpu.roll(x, LANES - 1, 1))

    def pick_tables(side):
        index = lane
        code = jnp.zeros_like(lane)
        for p in range(panels):
            here = lane // levels == p
            index = jnp.where(here, tables[0, side, p] * levels + lane % levels, index)
            code = jnp.where(here, tables[2, side, p] * 4 + tables[1, side, p], code)
        return index, code

    def pack(value):
        filler = jnp.zeros((rows, cols, LANES - panels * levels), jnp.float32)
        return jnp.concatenate([value[p] for p in range(panels)] + [filler], axis=-1)

    def split(which, value):
        packed[which, :, :cols, :] = value
        if packed.shape[2] > cols:
            packed[which, :, cols:, :] = jnp.zeros(
                (rows, packed.shape[2] - cols, LANES), jnp.float32
            )
        return [
            [packed[which, y, pl.ds(b, height, stride=2), :] for b in range(2)]
            for y in range(rows)
        ]

    def fine(fun):
        return [[fun(y, b) for b in range(2)] for y in range(rows)]

    small = range(half_r)

    def block_mean(values, i):
        y = 2 * i
        return 0.25 * (values[y][0] + values[y][1] + values[y + 1][0] + values[y + 1][1])

    loads[0].wait()
    gain = split(1, pack(inp[0]))
    loads[1].wait()
    vertical = split(2, pack(inp[1]))
    low_vert = fine(lambda y, b: lower(vertical[y][b]))
    inverse = fine(
        lambda y, b: relaxation / (gain[y][b] + 4.0 + vertical[y][b] + low_vert[y][b])
    )
    c_vert = [block_mean(vertical, i) for i in small]
    c_low = [lower(c_vert[i]) for i in small]
    c_inv = [relaxation / (block_mean(gain, i) + 1.0 + c_vert[i] + c_low[i]) for i in small]
    loads[2].wait()
    loads[3].wait()
    right_side = split(0, pack(inp[2] * inp[3]))
    smoothed = fine(lambda y, b: inverse[y][b] * right_side[y][b])

    def inner(y, b):
        x = smoothed[y][b]
        return vertical[y][b] * upper(x) + low_vert[y][b] * lower(x)

    coupled = fine(inner)
    column = fine(lambda y, b: coupled[y][b] + (1.0 - relaxation) * right_side[y][b])
    north = [smoothed[2 * i][0] + smoothed[2 * i][1] for i in small]
    south = [smoothed[2 * i + 1][0] + smoothed[2 * i + 1][1] for i in small]
    west = [smoothed[2 * i][0] + smoothed[2 * i + 1][0] for i in small]
    east = [smoothed[2 * i][1] + smoothed[2 * i + 1][1] for i in small]
    from_w = [pltpu.roll(east[i], 1, 0) for i in small]
    from_e = [pltpu.roll(west[i], height - 1, 0) for i in small]
    start_w = sub % length == 0
    start_e = sub % length == last
    edge_w = sub == 0
    edge_e = sub == half_c - 1

    def bare(i):
        total = block_mean(column, i) + 0.5 * (north[i] + south[i])
        beside = None
        if i > 0:
            beside = south[i - 1]
        if i < half_r - 1:
            beside = north[i + 1] if beside is None else beside + north[i + 1]
        return total if beside is None else total + 0.25 * beside

    plain = [bare(i) for i in small]

    def partial_guess(i, mask_w, mask_e):
        beside = jnp.where(mask_w, 0.0, from_w[i]) + jnp.where(mask_e, 0.0, from_e[i])
        return c_inv[i] * (plain[i] + 0.25 * beside)

    by_tile = [partial_guess(i, edge_w, edge_e) for i in small]
    by_piece = by_tile if k == 1 else [partial_guess(i, start_w, start_e) for i in small]

    def put(ref, at, value):
        ref[at : at + value.shape[0], :] = value

    for s in range(2):
        y = s * (rows - 1)
        i0, i1 = (0, 1) if s == 0 else (half_r - 1, half_r - 2)
        out = north[0] if s == 0 else south[half_r - 1]
        for p in range(k):
            lo, hi = p * length, p * length + last
            seg = slice(lo, hi + 1)
            one = lambda x, j: x[j : j + 1]
            a, b, g = (st_row.at[s, p, q] for q in range(3))
            put(a, 0, smoothed[y][0][seg])
            put(a, length, smoothed[y][1][seg])
            put(a, 2 * length, one(c_inv[i1], lo))
            put(a, 2 * length + 1, one(c_inv[i1], hi))
            put(b, 0, by_piece[i0][seg])
            put(b, length, by_piece[i1][seg])
            put(b, 2 * length, one(west[i0], lo))
            put(b, 2 * length + 1, one(east[i0], hi))
            put(g, 0, c_inv[i0][seg])
            put(g, length, c_vert[i0][seg])
            put(g, 2 * length, one(west[i1], lo))
            put(g, 2 * length + 1, one(east[i1], hi))
            for h in range(2):
                j, j1 = (lo, lo + 1) if h == 0 else (hi, hi - 1)
                side = west if h == 0 else east
                x = ex_row.at[s, p, h]
                put(x, 0, one(by_piece[i0], j))
                put(x, 1, one(c_inv[i0], j))
                put(x, 2, one(side[i0], j))
                put(x, 3, one(side[i1], j))
                put(x, 4, one(out, j))
                put(x, 5, one(out, j1))
    for s in range(2):
        j0, j1 = (0, 1) if s == 0 else (half_c - 1, half_c - 2)
        out = west if s == 0 else east
        a, b, g = (st_col.at[s, q] for q in range(3))
        at0 = lambda x: x[j0 : j0 + 1]
        at1 = lambda x: x[j1 : j1 + 1]
        for y in range(rows):
            put(a, (y % 2) * length + y // 2, at0(smoothed[y][s]))
        put(a, 2 * length, at1(c_inv[0]))
        put(a, 2 * length + 1, at1(c_inv[half_r - 1]))
        for i in small:
            put(b, i, at0(by_tile[i]))
            put(b, length + i, at1(by_tile[i]))
            put(g, i, at0(c_inv[i]))
            put(g, length + i, at0(c_vert[i]))
        put(b, 2 * length, at0(north[0]))
        put(b, 2 * length + 1, at0(south[half_r - 1]))
        put(g, 2 * length, at1(north[0]))
        put(g, 2 * length + 1, at1(south[half_r - 1]))
        for h in range(2):
            i0, i1 = (0, 1) if h == 0 else (half_r - 1, half_r - 2)
            side = north[0] if h == 0 else south[half_r - 1]
            x = ex_col.at[s, h]
            put(x, 0, at0(by_tile[i0]))
            put(x, 1, at0(c_inv[i0]))
            put(x, 2, at0(side))
            put(x, 3, at1(side))
            put(x, 4, at0(out[i0]))
            put(x, 5, at0(out[i1]))

    sends, border = messages()
    pl.semaphore_wait(barrier, expected)
    for m, (active, dest, src, dst, sem) in enumerate(sends):
        mine = same(dest)

        @pl.when(active & jnp.logical_not(mine) if m < border else active)
        def _():
            pltpu.make_async_remote_copy(
                src_ref=src,
                dst_ref=dst,
                send_sem=send_sem.at[m],
                recv_sem=sem,
                device_id=dest,
                device_id_type=MESH,
            ).start()

        if m < border:

            @pl.when(active & mine)
            def _():
                pltpu.make_async_copy(src, dst, sem).start()

    def beside(y, b):
        x = smoothed[y][b]
        total = coupled[y][b] + smoothed[y][1 - b]
        if y > 0:
            total = total + smoothed[y - 1][b]
        if y < rows - 1:
            total = total + smoothed[y + 1][b]
        return total

    partial = fine(beside)

    for load in table_loads:
        load.wait()
    row_pick = pick_tables(tr)
    col_pick = pick_tables(2 + tc)

    def arrived(ref, sem):
        pltpu.make_async_copy(ref, ref, sem).wait()

    for s in range(2):

        @pl.when(row_ok[s])
        def _():
            arrived(nb_row.at[s], nb_sem.at[s])

        @pl.when(col_ok[s])
        def _():
            arrived(nb_col.at[s], nb_sem.at[2 + s])

        for w in range(2):

            @pl.when(row_ok[s] & col_ok[w])
            def _():
                arrived(corner.at[2 * s + w], corner_sem.at[2 * s + w])

    order = list(range(2 * length))[::-1] + [2 * length + 1, 2 * length]
    other = (
        list(range(length))[::-1]
        + list(range(length, 2 * length))[::-1]
        + [2 * length + 1, 2 * length]
    )
    sublane = lax.broadcasted_iota(jnp.int32, (block, LANES), 0)

    def flip_index(perm):
        index = sublane
        for at, source in enumerate(perm):
            index = jnp.where(sublane == at, source, index)
        return index

    flips = [flip_index(order), flip_index(other), flip_index(other)]

    def choose(read, pick, f):
        index, code = pick
        taken = None
        for t in range(4):
            moved = jnp.take_along_axis(read(4 * f + t), index, axis=1, mode="promise_in_bounds")
            taken = moved if taken is None else jnp.where(code == 4 * f + t, moved, taken)
        return taken

    def select(plainly, reverse, pick, group):
        straight = choose(plainly, pick, 0)
        turned = choose(reverse, pick, 1)
        if group is not None:
            turned = jnp.take_along_axis(turned, flips[group], axis=0, mode="promise_in_bounds")
        return jnp.where(pick[1] >= 4, turned, straight)

    @pl.when(is_row)
    def _():
        arrived(rx_row, row_sem)
        for p in range(k):
            for q in range(3):
                nb_row[tr, p, q] = select(
                    lambda s: rx_row[s, p, q], lambda s: rx_row[s, k - 1 - p, q], row_pick, q
                )
        for w in range(2):

            @pl.when(col_ok[w])
            def _():
                arrived(ry_row.at[w], row_end_sem.at[w])
                read = lambda s: ry_row[w, s]
                corner[2 * tr + w] = select(read, read, row_pick, None)

    @pl.when(is_col)
    def _():
        arrived(rx_col, col_sem)
        for q in range(3):
            read = lambda s: rx_col[s, q]
            nb_col[tc, q] = select(read, read, col_pick, q)
        for s in range(2):

            @pl.when(row_ok[s])
            def _():
                arrived(ry_col.at[s], col_end_sem.at[s])
                read = lambda slot: ry_col[s, slot]
                value = select(read, read, col_pick, None)
                corner[2 * s + tc, 0:2, :] = value[0:2]
                corner[2 * s + tc, 2:4, :] = value[4:6]
                corner[2 * s + tc, 4:6, :] = value[2:4]

    @pl.when(is_row & is_col)
    def _():
        at = 2 * tr + tc
        corner[at, 0:2, :] = jnp.zeros((2, LANES), jnp.float32)
        for q in range(2):
            rows_z = nb_col[tc, 1 + q]
            rows_x = nb_row[tr, tc * (k - 1), 1 + q]
            corner[at, 2 + q : 3 + q, :] = jnp.where(
                tr == 0, rows_z[2 * length : 2 * length + 1], rows_z[2 * length + 1 : 2 * length + 2]
            )
            corner[at, 4 + q : 5 + q, :] = jnp.where(
                tc == 0, rows_x[2 * length : 2 * length + 1], rows_x[2 * length + 1 : 2 * length + 2]
            )

    def zeros(count):
        return [jnp.zeros((count, LANES), jnp.float32)] if count else []

    def stack(lines, total):
        used = sum(x.shape[0] for x in lines)
        return jnp.concatenate(list(lines) + zeros(total - used), axis=0)

    tall_z = round_up(half_r, TILE)
    flat = 2 * length

    class Strip:
        pass

    def strip(read, pieces, ends, total, own):
        def gather(q, at):
            return stack([read(p, q, slice(at, at + length)) for p in range(pieces)], total)

        def sides(first, final):
            lines = []
            for p in range(pieces):
                lines += [first(p)] + zeros(length - 2) + [final(p)]
            return stack(lines, total)

        def lateral(q):
            return sides(
                lambda p: ends[0][q] if p == 0 else read(p - 1, 1 + q, slice(flat + 1, flat + 2)),
                lambda p: ends[1][q]
                if p == pieces - 1
                else read(p + 1, 1 + q, slice(flat, flat + 1)),
            )

        x = Strip()
        x.even, x.odd = gather(0, 0), gather(0, length)
        x.pair = x.even + x.odd
        inv1 = sides(
            lambda p: read(p, 0, slice(flat, flat + 1)),
            lambda p: read(p, 0, slice(flat + 1, flat + 2)),
        )
        x.inv, x.vert = gather(2, 0), gather(2, length)
        x.guess = gather(1, 0) + 0.25 * x.inv * (lateral(0) + own)
        x.inside = gather(1, length) + 0.25 * inv1 * lateral(1)
        return x

    def corner_row(s, w, at):
        return corner[2 * s + w, at : at + 1, :]

    row_strip = []
    for s in range(2):
        own = north[0] if s == 0 else south[half_r - 1]
        ends = [[corner_row(s, w, 2 + q) for q in range(2)] for w in range(2)]
        row_strip.append(
            strip(lambda p, q, rows_: nb_row[s, p, q, rows_, :], k, ends, height, own)
        )
    col_strip = []
    for w in range(2):
        j = w * (half_c - 1)
        faces = west if w == 0 else east
        own = stack([faces[i][j : j + 1] for i in small], tall_z)
        ends = [[corner_row(s, w, 4 + q) for q in range(2)] for s in range(2)]
        col_strip.append(
            strip(lambda p, q, rows_: nb_col[w, q, rows_, :], 1, ends, tall_z, own)
        )

    guess = []
    for i in small:
        lateral = jnp.where(edge_w, col_strip[0].pair[i : i + 1], 0.0)
        lateral = lateral + jnp.where(edge_e, col_strip[1].pair[i : i + 1], 0.0)
        if i == 0:
            lateral = lateral + row_strip[0].pair
        if i == half_r - 1:
            lateral = lateral + row_strip[1].pair
        guess.append(by_tile[i] + 0.25 * c_inv[i] * lateral)

    row_side = [[None] * 2 for _ in range(2)]
    col_side = [[None] * 2 for _ in range(2)]
    for s in range(2):
        for w in range(2):
            faces = nb_row[s, w * (k - 1), 1, flat + w : flat + w + 1, :]
            faces = faces + nb_col[w, 1, flat + s : flat + s + 1, :]
            there = corner_row(s, w, 0) + 0.25 * corner_row(s, w, 1) * faces
            tip = (r == s * (nr - 1)) & (c == w * (nc - 1))
            jr, jc = w * (half_c - 1), s * (half_r - 1)
            row_side[s][w] = jnp.where(tip, col_strip[w].guess[jc : jc + 1], there)
            col_side[w][s] = jnp.where(tip, row_strip[s].guess[jr : jr + 1], there)

    def relax(x, ends, own, count):
        total = x.guess.shape[0]
        at = lax.broadcasted_iota(jnp.int32, (total, LANES), 0)
        around = x.inside + own
        around = around + jnp.where(at == 0, ends[0], pltpu.roll(x.guess, 1, 0))
        around = around + jnp.where(at == count - 1, ends[1], pltpu.roll(x.guess, total - 1, 0))
        column = x.vert * upper(x.guess) + lower(x.vert) * lower(x.guess)
        return (2.0 - relaxation) * x.guess + x.inv * (0.25 * around + column)

    row_fix = [
        relax(row_strip[s], row_side[s], guess[s * (half_r - 1)], half_c) for s in range(2)
    ]
    col_fix = []
    for w in range(2):
        j = w * (half_c - 1)
        own = stack([guess[i][j : j + 1] for i in small], tall_z)
        col_fix.append(relax(col_strip[w], col_side[w], own, half_r))

    def from_left(x, line):
        return jnp.where(edge_w, line, pltpu.roll(x, 1, 0))

    def from_right(x, line):
        return jnp.where(edge_e, line, pltpu.roll(x, height - 1, 0))

    correction = []
    for i in small:
        x = guess[i]
        around = from_left(x, col_strip[0].guess[i : i + 1])
        around = around + from_right(x, col_strip[1].guess[i : i + 1])
        around = around + (guess[i - 1] if i > 0 else row_strip[0].guess)
        around = around + (guess[i + 1] if i < half_r - 1 else row_strip[1].guess)
        levels_part = c_vert[i] * upper(x) + c_low[i] * lower(x)
        correction.append((2.0 - relaxation) * x + c_inv[i] * (0.25 * around + levels_part))
        small_ref[i] = correction[i]

    def outer(y, b):
        at = (y % 2) * length + y // 2
        source = col_strip[b]
        line = (source.even if y % 2 == 0 else source.odd)[y // 2 : y // 2 + 1]
        if b == 0:
            total = partial[y][b] + from_left(smoothed[y][1], line)
        else:
            total = partial[y][b] + from_right(smoothed[y][0], line)
        if y == 0:
            total = total + (row_strip[0].even if b == 0 else row_strip[0].odd)
        if y == rows - 1:
            total = total + (row_strip[1].even if b == 0 else row_strip[1].odd)
        return total

    c_up = [upper(x) for x in correction]
    c_down = [lower(x) for x in correction]
    left = [from_left(correction[i], col_fix[0][i : i + 1]) for i in small]
    right = [from_right(correction[i], col_fix[1][i : i + 1]) for i in small]
    for y in range(rows):
        i = y // 2
        next_i = i - 1 if y % 2 == 0 else i + 1
        for b in range(2):
            total = outer(y, b) + 2.0 * correction[i]
            total = total + vertical[y][b] * c_up[i] + low_vert[y][b] * c_down[i]
            if next_i < 0:
                total = total + row_fix[0]
            elif next_i >= half_r:
                total = total + row_fix[1]
            else:
                total = total + correction[next_i]
            total = total + (left if b == 0 else right)[i]
            first = (2.0 - relaxation) * smoothed[y][b] + (1.0 - relaxation) * correction[i]
            spread[y, pl.ds(b, height, stride=2), :] = first + inverse[y][b] * total

    for m, (active, dest, src, dst, sem) in enumerate(sends):

        @pl.when(active & jnp.logical_not(same(dest)) if m < border else active)
        def _():
            pltpu.make_async_copy(src, src, send_sem.at[m]).wait()


def unpack(spread, small_ref, sol_ref, corr_ref):
    panels, _, cols, levels = sol_ref.shape
    half_c = corr_ref.shape[2]
    for p in range(panels):
        lanes = slice(p * levels, (p + 1) * levels)
        sol_ref[p] = spread[:, :cols, lanes]
        corr_ref[p] = small_ref[:, :half_c, lanes]


def solution(mesh):
    nr, nc = mesh.shape["tx"], mesh.shape["ty"]

    def shards(residual, density, gain, vertical, edge_panel, edge_side, edge_flip):
        panels, rows, cols, levels = residual.shape
        k = cols // rows
        assert cols == k * rows and rows % 2 == 0 and panels * levels <= LANES
        assert rows >= 6 and nr > 1 and nc > 1
        block = round_up(rows + 2, TILE)
        height = round_up(cols // 2, TILE)
        tall = 2 * height
        f32 = jnp.float32
        count = 4 + 8 + 4 * k + 8 * k + 8 + 16 + 4 + 4
        spread, small = pl.pallas_call(
            functools.partial(kernel, nr, nc),
            out_shape=(
                pltpu.VMEM((rows, tall, LANES), f32),
                pltpu.VMEM((rows // 2, height, LANES), f32),
            ),
            in_specs=[pl.BlockSpec(memory_space=pl.ANY)] * 7,
            out_specs=(pl.BlockSpec(memory_space=pltpu.VMEM),) * 2,
            scratch_shapes=[
                pltpu.VMEM((4, panels, rows, cols, levels), f32),
                pltpu.SMEM((3,) + edge_panel.T.shape, jnp.int32),
                pltpu.VMEM((3, rows, tall, LANES), f32),
                pltpu.VMEM((3, k, 3, block, LANES), f32),
                pltpu.VMEM((3, 3, block, LANES), f32),
                pltpu.VMEM((3, k, 2, TILE, LANES), f32),
                pltpu.VMEM((3, 2, TILE, LANES), f32),
                pltpu.VMEM((3, k, 3, block, LANES), f32),
                pltpu.VMEM((3, 3, block, LANES), f32),
                pltpu.VMEM((5, TILE, LANES), f32),
                pltpu.VMEM((8, k, 3, block, LANES), f32),
                pltpu.VMEM((8, 3, block, LANES), f32),
                pltpu.VMEM((2, 8, TILE, LANES), f32),
                pltpu.VMEM((2, 8, TILE, LANES), f32),
                pltpu.SemaphoreType.DMA((4,)),
                pltpu.SemaphoreType.DMA((3,)),
                pltpu.SemaphoreType.DMA((count,)),
                pltpu.SemaphoreType.DMA((4,)),
                pltpu.SemaphoreType.DMA((4,)),
                pltpu.SemaphoreType.DMA,
                pltpu.SemaphoreType.DMA,
                pltpu.SemaphoreType.DMA((2,)),
                pltpu.SemaphoreType.DMA((2,)),
            ],
            compiler_params=pltpu.CompilerParams(collective_id=0, has_side_effects=True),
        )(residual, density, gain, vertical, edge_panel.T, edge_side.T, edge_flip.T)
        spread = pltpu.with_memory_space_constraint(spread, pltpu.VMEM)
        small = pltpu.with_memory_space_constraint(small, pltpu.VMEM)
        return pl.pallas_call(
            unpack,
            out_shape=(
                jax.ShapeDtypeStruct(residual.shape, f32),
                jax.ShapeDtypeStruct((panels, rows // 2, cols // 2, levels), f32),
            ),
            in_specs=[pl.BlockSpec(memory_space=pltpu.VMEM)] * 2,
            out_specs=(pl.BlockSpec(memory_space=pltpu.VMEM),) * 2,
        )(spread, small)

    fields = P(None, "tx", "ty", None)
    return jax.shard_map(
        shards,
        mesh=mesh,
        in_specs=(fields,) * 4 + (P(),) * 3,
        out_specs=(fields, fields),
        check_vma=False,
    )
```

```python
import functools

import jax
import jax.numpy as jnp
from jax import lax
from jax.experimental import pallas as pl
from jax.experimental.pallas import tpu as pltpu
from jax.sharding import PartitionSpec as P

MESH = pl.DeviceIdType.MESH
relaxation = 0.8
LANES = 128
TILE = 8


def round_up(value, unit):
    return (value + unit - 1) // unit * unit


def kernel(
    nr,
    nc,
    res_hbm,
    den_hbm,
    gain_hbm,
    vert_hbm,
    panel_hbm,
    side_hbm,
    flip_hbm,
    spread,
    small_ref,
    inp,
    tables,
    packed,
    st_row,
    st_col,
    ex_row,
    ex_col,
    nb_row,
    nb_col,
    corner,
    rx_row,
    rx_col,
    ry_row,
    ry_col,
    in_sem,
    table_sem,
    send_sem,
    nb_sem,
    corner_sem,
    row_sem,
    col_sem,
    row_end_sem,
    col_end_sem,
):
    _, panels, rows, cols, levels = inp.shape
    half_r, half_c = rows // 2, cols // 2
    k = cols // rows
    length = half_r
    last = length - 1
    height = spread.shape[1] // 2
    block = st_row.shape[3]
    r = lax.axis_index("tx")
    c = lax.axis_index("ty")
    is_row = (r == 0) | (r == nr - 1)
    is_col = (c == 0) | (c == nc - 1)
    tr = r // (nr - 1)
    tc = c // (nc - 1)
    row_ok = (r > 0, r < nr - 1)
    col_ok = (c > 0, c < nc - 1)

    def row_segment(f, p):
        return k * c + p if f == 0 else nr - 1 - k * c - p

    def col_segment(f):
        return r if f == 0 else nr - 1 - r

    def clamp(x, n):
        return jnp.minimum(jnp.maximum(x, 0), n - 1)

    def partners():
        found = []
        for f in range(2):
            here = c if f == 0 else nc - 1 - c
            for e in range(2):
                for d in (-1, 0, 1):
                    to = here + d
                    found.append((is_row & (to >= 0) & (to < nc), (e * (nr - 1), clamp(to, nc))))
                low = row_segment(f, 0 if f == 0 else k - 1)
                for d in range(-1, k + 1):
                    to = low + d
                    found.append((is_row & (to >= 0) & (to < nr), (clamp(to, nr), e * (nc - 1))))
                g = col_segment(f)
                for d in (-1, 0, 1):
                    to = g + d
                    inside = is_col & (to >= 0) & (to < nr)
                    found.append((inside, (clamp(to, nr), e * (nc - 1))))
                    if d:
                        inside = inside & (g % k == (k - 1 if d == 1 else 0))
                    found.append((inside, (e * (nr - 1), clamp(g // k + d, nc))))
        for dr in (-1, 0, 1):
            for dc in (-1, 0, 1):
                if dr or dc:
                    ok = True
                    if dr:
                        ok = row_ok[(dr + 1) // 2]
                    if dc:
                        ok = col_ok[(dc + 1) // 2] if ok is True else ok & col_ok[(dc + 1) // 2]
                    found.append((ok, (r + dr, c + dc)))
        return found

    far_r, near_r = (1 - tr) * (nr - 1), tr * (nr - 1)
    far_c, near_c = (1 - tc) * (nc - 1), tc * (nc - 1)
    used = 6

    def traffic(sending):
        count = [0]

        def remote(src, dst, sem, dest):
            m = count[0]
            count[0] += 1
            if sending:
                pltpu.make_async_remote_copy(
                    src_ref=src,
                    dst_ref=dst,
                    send_sem=send_sem.at[m],
                    recv_sem=sem,
                    device_id=dest,
                    device_id_type=MESH,
                ).start()
            else:
                pltpu.make_async_copy(src, src, send_sem.at[m]).wait()

        def local(src, dst, sem):
            if sending:
                pltpu.make_async_copy(src, dst, sem).start()

        def either(src, dst, sem, dest, mine):
            @pl.when(jnp.logical_not(mine))
            def _():
                remote(src, dst, sem, dest)

            @pl.when(mine)
            def _():
                local(src, dst, sem)

        @pl.when(is_row)
        def _():
            src = st_row.at[tr]
            other = nc - 1 - c
            remote(src, rx_row.at[4 + tr], row_sem, (far_r, other))
            remote(src, rx_row.at[tr], row_sem, (far_r, c))
            for p in range(k):
                extreme = (c == 0) if p == 0 else (c == nc - 1)
                if k == 1:
                    extreme = extreme | (c == nc - 1)

                def to_columns(p=p):
                    for f in (1, 0):
                        for ec in (far_c, near_c):
                            remote(
                                st_row.at[tr, p],
                                rx_col.at[4 * f + tr],
                                col_sem,
                                (row_segment(f, p), ec),
                            )

                if 0 < p < k - 1:
                    to_columns()
                else:
                    pl.when(jnp.logical_not(extreme))(to_columns)
            remote(src, rx_row.at[4 + tr], row_sem, (near_r, other))
            local(src, rx_row.at[tr], row_sem)

        @pl.when(is_col)
        def _():
            src = st_col.at[tc]
            for f in (1, 0):
                dst = rx_row.at[4 * f + 2 + tc, r % k]
                remote(src, dst, row_sem, (far_r, col_segment(f) // k))

            @pl.when(jnp.logical_not(is_row))
            def _():
                remote(src, rx_col.at[6 + tc], col_sem, (nr - 1 - r, far_c))
                remote(src, rx_col.at[6 + tc], col_sem, (nr - 1 - r, near_c))
                remote(src, rx_col.at[2 + tc], col_sem, (r, far_c))
                local(src, rx_col.at[2 + tc], col_sem)

            for f in (1, 0):
                dst = rx_row.at[4 * f + 2 + tc, r % k]
                to = col_segment(f) // k
                either(src, dst, row_sem, (near_r, to), is_row & (to == c))

        for f in (1, 0):
            for h in range(2):
                d = 1 if h != f else -1
                end = 0 if d == 1 else 1

                @pl.when(is_row)
                def _():
                    slot = 4 * f + tr
                    for p in range(k):
                        outer_end = p == (k - 1 if h == 1 else 0)

                        def ends(p=p, outer_end=outer_end):
                            src = ex_row.at[tr, p, h, 0:used]
                            to = clamp(row_segment(f, p) + d, nr)
                            dst = ry_col.at[end, slot, 0:used]
                            sem = col_end_sem.at[end]
                            remote(src, dst, sem, (to, far_c))
                            either(src, dst, sem, (to, near_c), is_col & (to == r))
                            if outer_end:
                                to = clamp((c if f == 0 else nc - 1 - c) + d, nc)
                                dst = ry_row.at[end, slot, 0:used]
                                sem = row_end_sem.at[end]
                                remote(src, dst, sem, (far_r, to))
                                if f == 0:
                                    remote(src, dst, sem, (near_r, to))
                                else:
                                    either(src, dst, sem, (near_r, to), to == c)

                        if outer_end:
                            pl.when(col_ok[h])(ends)
                        else:
                            ends()

                @pl.when(is_col & row_ok[h])
                def _():
                    slot = 4 * f + 2 + tc
                    src = ex_col.at[tc, h, 0:used]
                    g = col_segment(f)
                    to = clamp(g + d, nr)
                    dst = ry_col.at[end, slot, 0:used]
                    sem = col_end_sem.at[end]
                    remote(src, dst, sem, (to, far_c))
                    if f == 0:
                        remote(src, dst, sem, (to, near_c))
                    else:
                        either(src, dst, sem, (to, near_c), to == r)

                    def crossing():
                        to = clamp(g // k + d, nc)
                        dst = ry_row.at[end, slot, 0:used]
                        sem = row_end_sem.at[end]
                        remote(src, dst, sem, (far_r, to))
                        either(src, dst, sem, (near_r, to), is_row & (to == c))

                    if k == 1:
                        crossing()
                    else:
                        pl.when(g % k == (k - 1 if d == 1 else 0))(crossing)

        for s in range(2):

            @pl.when(row_ok[s])
            def _():
                remote(st_row.at[s], nb_row.at[1 - s], nb_sem.at[1 - s], (r + 2 * s - 1, c))

            @pl.when(col_ok[s])
            def _():
                remote(st_col.at[s], nb_col.at[1 - s], nb_sem.at[3 - s], (r, c + 2 * s - 1))

        for s in range(2):
            for w in range(2):
                at = 2 * (1 - s) + 1 - w

                @pl.when(row_ok[s] & col_ok[w])
                def _():
                    remote(
                        ex_row.at[s, w * (k - 1), w, 0:used],
                        corner.at[at, 0:used],
                        corner_sem.at[at],
                        (r + 2 * s - 1, c + 2 * w - 1),
                    )

    def same(dest):
        return (dest[0] == r) & (dest[1] == c)

    loads = [
        pltpu.make_async_copy(source, inp.at[i], in_sem.at[i])
        for i, source in enumerate((gain_hbm, vert_hbm, den_hbm, res_hbm))
    ]
    for load in loads:
        load.start()
    table_loads = [
        pltpu.make_async_copy(source, tables.at[i], table_sem.at[i])
        for i, source in enumerate((panel_hbm, side_hbm, flip_hbm))
    ]
    for load in table_loads:
        load.start()

    barrier = pltpu.get_barrier_semaphore()
    expected = jnp.int32(0)
    for active, dest in partners():
        go = active & jnp.logical_not(same(dest))
        expected = expected + go.astype(jnp.int32)

        @pl.when(go)
        def _():
            pl.semaphore_signal(barrier, inc=1, device_id=dest, device_id_type=MESH)

    lane = lax.broadcasted_iota(jnp.int32, (TILE, LANES), 1)
    sub = lax.broadcasted_iota(jnp.int32, (height, LANES), 0)
    level = lane[:1] % levels
    first_level = level == 0
    last_level = level == levels - 1

    def lower(x):
        return jnp.where(first_level, 0.0, pltpu.roll(x, 1, 1))

    def upper(x):
        return jnp.where(last_level, 0.0, pltpu.roll(x, LANES - 1, 1))

    def pick_tables(side):
        index = lane
        code = jnp.zeros_like(lane)
        for p in range(panels):
            here = lane // levels == p
            index = jnp.where(here, tables[0, side, p] * levels + lane % levels, index)
            code = jnp.where(here, tables[2, side, p] * 4 + tables[1, side, p], code)
        return index, code

    def pack(value):
        filler = jnp.zeros((rows, cols, LANES - panels * levels), jnp.float32)
        return jnp.concatenate([value[p] for p in range(panels)] + [filler], axis=-1)

    def split(which, value):
        packed[which, :, :cols, :] = value
        if packed.shape[2] > cols:
            packed[which, :, cols:, :] = jnp.zeros(
                (rows, packed.shape[2] - cols, LANES), jnp.float32
            )
        return [
            [packed[which, y, pl.ds(b, height, stride=2), :] for b in range(2)]
            for y in range(rows)
        ]

    def fine(fun):
        return [[fun(y, b) for b in range(2)] for y in range(rows)]

    small = range(half_r)

    def block_mean(values, i):
        y = 2 * i
        return 0.25 * (values[y][0] + values[y][1] + values[y + 1][0] + values[y + 1][1])

    loads[0].wait()
    gain = split(1, pack(inp[0]))
    loads[1].wait()
    vertical = split(2, pack(inp[1]))
    low_vert = fine(lambda y, b: lower(vertical[y][b]))
    inverse = fine(
        lambda y, b: relaxation / (gain[y][b] + 4.0 + vertical[y][b] + low_vert[y][b])
    )
    c_vert = [block_mean(vertical, i) for i in small]
    c_low = [lower(c_vert[i]) for i in small]
    c_inv = [relaxation / (block_mean(gain, i) + 1.0 + c_vert[i] + c_low[i]) for i in small]
    loads[2].wait()
    loads[3].wait()
    right_side = split(0, pack(inp[2] * inp[3]))
    smoothed = fine(lambda y, b: inverse[y][b] * right_side[y][b])

    def inner(y, b):
        x = smoothed[y][b]
        return vertical[y][b] * upper(x) + low_vert[y][b] * lower(x)

    coupled = fine(inner)
    column = fine(lambda y, b: coupled[y][b] + (1.0 - relaxation) * right_side[y][b])
    north = [smoothed[2 * i][0] + smoothed[2 * i][1] for i in small]
    south = [smoothed[2 * i + 1][0] + smoothed[2 * i + 1][1] for i in small]
    west = [smoothed[2 * i][0] + smoothed[2 * i + 1][0] for i in small]
    east = [smoothed[2 * i][1] + smoothed[2 * i + 1][1] for i in small]
    from_w = [pltpu.roll(east[i], 1, 0) for i in small]
    from_e = [pltpu.roll(west[i], height - 1, 0) for i in small]
    start_w = sub % length == 0
    start_e = sub % length == last
    edge_w = sub == 0
    edge_e = sub == half_c - 1

    def bare(i):
        total = block_mean(column, i) + 0.5 * (north[i] + south[i])
        beside = None
        if i > 0:
            beside = south[i - 1]
        if i < half_r - 1:
            beside = north[i + 1] if beside is None else beside + north[i + 1]
        return total if beside is None else total + 0.25 * beside

    plain = [bare(i) for i in small]

    def partial_guess(i, mask_w, mask_e):
        beside = jnp.where(mask_w, 0.0, from_w[i]) + jnp.where(mask_e, 0.0, from_e[i])
        return c_inv[i] * (plain[i] + 0.25 * beside)

    by_tile = [partial_guess(i, edge_w, edge_e) for i in small]
    by_piece = by_tile if k == 1 else [partial_guess(i, start_w, start_e) for i in small]

    def put(ref, at, value):
        ref[at : at + value.shape[0], :] = value

    for s in range(2):
        y = s * (rows - 1)
        i0, i1 = (0, 1) if s == 0 else (half_r - 1, half_r - 2)
        out = north[0] if s == 0 else south[half_r - 1]
        for p in range(k):
            lo, hi = p * length, p * length + last
            seg = slice(lo, hi + 1)
            one = lambda x, j: x[j : j + 1]
            a, b, g = (st_row.at[s, p, q] for q in range(3))
            put(a, 0, smoothed[y][0][seg])
            put(a, length, smoothed[y][1][seg])
            put(a, 2 * length, one(c_inv[i1], lo))
            put(a, 2 * length + 1, one(c_inv[i1], hi))
            put(b, 0, by_piece[i0][seg])
            put(b, length, by_piece[i1][seg])
            put(b, 2 * length, one(west[i0], lo))
            put(b, 2 * length + 1, one(east[i0], hi))
            put(g, 0, c_inv[i0][seg])
            put(g, length, c_vert[i0][seg])
            put(g, 2 * length, one(west[i1], lo))
            put(g, 2 * length + 1, one(east[i1], hi))
            for h in range(2):
                j, j1 = (lo, lo + 1) if h == 0 else (hi, hi - 1)
                side = west if h == 0 else east
                x = ex_row.at[s, p, h]
                put(x, 0, one(by_piece[i0], j))
                put(x, 1, one(c_inv[i0], j))
                put(x, 2, one(side[i0], j))
                put(x, 3, one(side[i1], j))
                put(x, 4, one(out, j))
                put(x, 5, one(out, j1))
    for s in range(2):
        j0, j1 = (0, 1) if s == 0 else (half_c - 1, half_c - 2)
        out = west if s == 0 else east
        a, b, g = (st_col.at[s, q] for q in range(3))
        at0 = lambda x: x[j0 : j0 + 1]
        at1 = lambda x: x[j1 : j1 + 1]
        for y in range(rows):
            put(a, (y % 2) * length + y // 2, at0(smoothed[y][s]))
        put(a, 2 * length, at1(c_inv[0]))
        put(a, 2 * length + 1, at1(c_inv[half_r - 1]))
        for i in small:
            put(b, i, at0(by_tile[i]))
            put(b, length + i, at1(by_tile[i]))
            put(g, i, at0(c_inv[i]))
            put(g, length + i, at0(c_vert[i]))
        put(b, 2 * length, at0(north[0]))
        put(b, 2 * length + 1, at0(south[half_r - 1]))
        put(g, 2 * length, at1(north[0]))
        put(g, 2 * length + 1, at1(south[half_r - 1]))
        for h in range(2):
            i0, i1 = (0, 1) if h == 0 else (half_r - 1, half_r - 2)
            side = north[0] if h == 0 else south[half_r - 1]
            x = ex_col.at[s, h]
            put(x, 0, at0(by_tile[i0]))
            put(x, 1, at0(c_inv[i0]))
            put(x, 2, at0(side))
            put(x, 3, at1(side))
            put(x, 4, at0(out[i0]))
            put(x, 5, at0(out[i1]))

    pl.semaphore_wait(barrier, expected)
    traffic(True)

    def beside(y, b):
        x = smoothed[y][b]
        total = coupled[y][b] + smoothed[y][1 - b]
        if y > 0:
            total = total + smoothed[y - 1][b]
        if y < rows - 1:
            total = total + smoothed[y + 1][b]
        return total

    partial = fine(beside)

    for load in table_loads:
        load.wait()
    row_pick = pick_tables(tr)
    col_pick = pick_tables(2 + tc)

    def arrived(ref, sem):
        pltpu.make_async_copy(ref, ref, sem).wait()

    for s in range(2):

        @pl.when(row_ok[s])
        def _():
            arrived(nb_row.at[s], nb_sem.at[s])

        @pl.when(col_ok[s])
        def _():
            arrived(nb_col.at[s], nb_sem.at[2 + s])

        for w in range(2):

            @pl.when(row_ok[s] & col_ok[w])
            def _():
                arrived(corner.at[2 * s + w, 0:used], corner_sem.at[2 * s + w])

    order = list(range(2 * length))[::-1] + [2 * length + 1, 2 * length]
    other = (
        list(range(length))[::-1]
        + list(range(length, 2 * length))[::-1]
        + [2 * length + 1, 2 * length]
    )
    sublane = lax.broadcasted_iota(jnp.int32, (block, LANES), 0)

    def flip_index(perm):
        index = sublane
        for at, source in enumerate(perm):
            index = jnp.where(sublane == at, source, index)
        return index

    flips = [flip_index(order), flip_index(other), flip_index(other)]

    def choose(read, pick, f):
        index, code = pick
        taken = None
        for t in range(4):
            moved = jnp.take_along_axis(read(4 * f + t), index, axis=1, mode="promise_in_bounds")
            taken = moved if taken is None else jnp.where(code == 4 * f + t, moved, taken)
        return taken

    def select(plainly, reverse, pick, group):
        straight = choose(plainly, pick, 0)
        turned = choose(reverse, pick, 1)
        if group is not None:
            turned = jnp.take_along_axis(turned, flips[group], axis=0, mode="promise_in_bounds")
        return jnp.where(pick[1] >= 4, turned, straight)

    @pl.when(is_row)
    def _():
        arrived(rx_row, row_sem)
        for p in range(k):
            for q in range(3):
                nb_row[tr, p, q] = select(
                    lambda s: rx_row[s, p, q], lambda s: rx_row[s, k - 1 - p, q], row_pick, q
                )
        for w in range(2):

            @pl.when(col_ok[w])
            def _():
                arrived(ry_row.at[w, :, 0:used], row_end_sem.at[w])
                read = lambda s: ry_row[w, s]
                corner[2 * tr + w] = select(read, read, row_pick, None)

    @pl.when(is_col & jnp.logical_not(is_row))
    def _():
        arrived(rx_col, col_sem)
        for q in range(3):
            read = lambda s: rx_col[s, q]
            nb_col[tc, q] = select(read, read, col_pick, q)

    @pl.when(is_col & is_row)
    def _():
        swap = (tr + tc) % 2
        for q in range(3):

            def read(s, q=q):
                f, t = s // 4, s % 4
                at = 4 * (1 - swap) + t if f == 1 else 4 * swap + t
                return rx_row[at, (tr if f == 0 else 1 - tr) * (k - 1), q]

            nb_col[tc, q] = select(read, read, col_pick, q)

    @pl.when(is_col)
    def _():
        for s in range(2):

            @pl.when(row_ok[s])
            def _():
                arrived(ry_col.at[s, :, 0:used], col_end_sem.at[s])
                read = lambda slot: ry_col[s, slot]
                value = select(read, read, col_pick, None)
                corner[2 * s + tc, 0:2, :] = value[0:2]
                corner[2 * s + tc, 2:4, :] = value[4:6]
                corner[2 * s + tc, 4:6, :] = value[2:4]

    @pl.when(is_row & is_col)
    def _():
        at = 2 * tr + tc
        corner[at, 0:2, :] = jnp.zeros((2, LANES), jnp.float32)
        for q in range(2):
            rows_z = nb_col[tc, 1 + q]
            rows_x = nb_row[tr, tc * (k - 1), 1 + q]
            corner[at, 2 + q : 3 + q, :] = jnp.where(
                tr == 0, rows_z[2 * length : 2 * length + 1], rows_z[2 * length + 1 : 2 * length + 2]
            )
            corner[at, 4 + q : 5 + q, :] = jnp.where(
                tc == 0, rows_x[2 * length : 2 * length + 1], rows_x[2 * length + 1 : 2 * length + 2]
            )

    def zeros(count):
        return [jnp.zeros((count, LANES), jnp.float32)] if count else []

    def stack(lines, total):
        used = sum(x.shape[0] for x in lines)
        return jnp.concatenate(list(lines) + zeros(total - used), axis=0)

    tall_z = round_up(half_r, TILE)
    flat = 2 * length

    class Strip:
        pass

    def strip(read, pieces, ends, total, own):
        def gather(q, at):
            return stack([read(p, q, slice(at, at + length)) for p in range(pieces)], total)

        def sides(first, final):
            lines = []
            for p in range(pieces):
                lines += [first(p)] + zeros(length - 2) + [final(p)]
            return stack(lines, total)

        def lateral(q):
            return sides(
                lambda p: ends[0][q] if p == 0 else read(p - 1, 1 + q, slice(flat + 1, flat + 2)),
                lambda p: ends[1][q]
                if p == pieces - 1
                else read(p + 1, 1 + q, slice(flat, flat + 1)),
            )

        x = Strip()
        x.even, x.odd = gather(0, 0), gather(0, length)
        x.pair = x.even + x.odd
        inv1 = sides(
            lambda p: read(p, 0, slice(flat, flat + 1)),
            lambda p: read(p, 0, slice(flat + 1, flat + 2)),
        )
        x.inv, x.vert = gather(2, 0), gather(2, length)
        x.guess = gather(1, 0) + 0.25 * x.inv * (lateral(0) + own)
        x.inside = gather(1, length) + 0.25 * inv1 * lateral(1)
        return x

    def corner_row(s, w, at):
        return corner[2 * s + w, at : at + 1, :]

    row_strip = []
    for s in range(2):
        own = north[0] if s == 0 else south[half_r - 1]
        ends = [[corner_row(s, w, 2 + q) for q in range(2)] for w in range(2)]
        row_strip.append(
            strip(lambda p, q, rows_: nb_row[s, p, q, rows_, :], k, ends, height, own)
        )
    col_strip = []
    for w in range(2):
        j = w * (half_c - 1)
        faces = west if w == 0 else east
        own = stack([faces[i][j : j + 1] for i in small], tall_z)
        ends = [[corner_row(s, w, 4 + q) for q in range(2)] for s in range(2)]
        col_strip.append(
            strip(lambda p, q, rows_: nb_col[w, q, rows_, :], 1, ends, tall_z, own)
        )

    guess = []
    for i in small:
        lateral = jnp.where(edge_w, col_strip[0].pair[i : i + 1], 0.0)
        lateral = lateral + jnp.where(edge_e, col_strip[1].pair[i : i + 1], 0.0)
        if i == 0:
            lateral = lateral + row_strip[0].pair
        if i == half_r - 1:
            lateral = lateral + row_strip[1].pair
        guess.append(by_tile[i] + 0.25 * c_inv[i] * lateral)

    row_side = [[None] * 2 for _ in range(2)]
    col_side = [[None] * 2 for _ in range(2)]
    for s in range(2):
        for w in range(2):
            faces = nb_row[s, w * (k - 1), 1, flat + w : flat + w + 1, :]
            faces = faces + nb_col[w, 1, flat + s : flat + s + 1, :]
            there = corner_row(s, w, 0) + 0.25 * corner_row(s, w, 1) * faces
            tip = (r == s * (nr - 1)) & (c == w * (nc - 1))
            jr, jc = w * (half_c - 1), s * (half_r - 1)
            row_side[s][w] = jnp.where(tip, col_strip[w].guess[jc : jc + 1], there)
            col_side[w][s] = jnp.where(tip, row_strip[s].guess[jr : jr + 1], there)

    def relax(x, ends, own, count):
        total = x.guess.shape[0]
        at = lax.broadcasted_iota(jnp.int32, (total, LANES), 0)
        around = x.inside + own
        around = around + jnp.where(at == 0, ends[0], pltpu.roll(x.guess, 1, 0))
        around = around + jnp.where(at == count - 1, ends[1], pltpu.roll(x.guess, total - 1, 0))
        column = x.vert * upper(x.guess) + lower(x.vert) * lower(x.guess)
        return (2.0 - relaxation) * x.guess + x.inv * (0.25 * around + column)

    row_fix = [
        relax(row_strip[s], row_side[s], guess[s * (half_r - 1)], half_c) for s in range(2)
    ]
    col_fix = []
    for w in range(2):
        j = w * (half_c - 1)
        own = stack([guess[i][j : j + 1] for i in small], tall_z)
        col_fix.append(relax(col_strip[w], col_side[w], own, half_r))

    def from_left(x, line):
        return jnp.where(edge_w, line, pltpu.roll(x, 1, 0))

    def from_right(x, line):
        return jnp.where(edge_e, line, pltpu.roll(x, height - 1, 0))

    correction = []
    for i in small:
        x = guess[i]
        around = from_left(x, col_strip[0].guess[i : i + 1])
        around = around + from_right(x, col_strip[1].guess[i : i + 1])
        around = around + (guess[i - 1] if i > 0 else row_strip[0].guess)
        around = around + (guess[i + 1] if i < half_r - 1 else row_strip[1].guess)
        levels_part = c_vert[i] * upper(x) + c_low[i] * lower(x)
        correction.append((2.0 - relaxation) * x + c_inv[i] * (0.25 * around + levels_part))
        small_ref[i] = correction[i]

    def outer(y, b):
        at = (y % 2) * length + y // 2
        source = col_strip[b]
        line = (source.even if y % 2 == 0 else source.odd)[y // 2 : y // 2 + 1]
        if b == 0:
            total = partial[y][b] + from_left(smoothed[y][1], line)
        else:
            total = partial[y][b] + from_right(smoothed[y][0], line)
        if y == 0:
            total = total + (row_strip[0].even if b == 0 else row_strip[0].odd)
        if y == rows - 1:
            total = total + (row_strip[1].even if b == 0 else row_strip[1].odd)
        return total

    c_up = [upper(x) for x in correction]
    c_down = [lower(x) for x in correction]
    left = [from_left(correction[i], col_fix[0][i : i + 1]) for i in small]
    right = [from_right(correction[i], col_fix[1][i : i + 1]) for i in small]
    for y in range(rows):
        i = y // 2
        next_i = i - 1 if y % 2 == 0 else i + 1
        for b in range(2):
            total = outer(y, b) + 2.0 * correction[i]
            total = total + vertical[y][b] * c_up[i] + low_vert[y][b] * c_down[i]
            if next_i < 0:
                total = total + row_fix[0]
            elif next_i >= half_r:
                total = total + row_fix[1]
            else:
                total = total + correction[next_i]
            total = total + (left if b == 0 else right)[i]
            first = (2.0 - relaxation) * smoothed[y][b] + (1.0 - relaxation) * correction[i]
            spread[y, pl.ds(b, height, stride=2), :] = first + inverse[y][b] * total

    traffic(False)


def unpack(spread, small_ref, sol_ref, corr_ref):
    panels, _, cols, levels = sol_ref.shape
    half_c = corr_ref.shape[2]
    for p in range(panels):
        lanes = slice(p * levels, (p + 1) * levels)
        sol_ref[p] = spread[:, :cols, lanes]
        corr_ref[p] = small_ref[:, :half_c, lanes]


def solution(mesh):
    nr, nc = mesh.shape["tx"], mesh.shape["ty"]

    def shards(residual, density, gain, vertical, edge_panel, edge_side, edge_flip):
        panels, rows, cols, levels = residual.shape
        k = cols // rows
        assert cols == k * rows and rows % 2 == 0 and panels * levels <= LANES
        assert rows >= 6 and nr > 1 and nc > 1
        block = round_up(rows + 2, TILE)
        height = round_up(cols // 2, TILE)
        tall = 2 * height
        f32 = jnp.float32
        count = 4 + 8 + 4 * k + 8 * k + 8 + 16 + 4 + 4
        spread, small = pl.pallas_call(
            functools.partial(kernel, nr, nc),
            out_shape=(
                pltpu.VMEM((rows, tall, LANES), f32),
                pltpu.VMEM((rows // 2, height, LANES), f32),
            ),
            in_specs=[pl.BlockSpec(memory_space=pl.ANY)] * 7,
            out_specs=(pl.BlockSpec(memory_space=pltpu.VMEM),) * 2,
            scratch_shapes=[
                pltpu.VMEM((4, panels, rows, cols, levels), f32),
                pltpu.SMEM((3,) + edge_panel.T.shape, jnp.int32),
                pltpu.VMEM((3, rows, tall, LANES), f32),
                pltpu.VMEM((3, k, 3, block, LANES), f32),
                pltpu.VMEM((3, 3, block, LANES), f32),
                pltpu.VMEM((3, k, 2, TILE, LANES), f32),
                pltpu.VMEM((3, 2, TILE, LANES), f32),
                pltpu.VMEM((3, k, 3, block, LANES), f32),
                pltpu.VMEM((3, 3, block, LANES), f32),
                pltpu.VMEM((5, TILE, LANES), f32),
                pltpu.VMEM((8, k, 3, block, LANES), f32),
                pltpu.VMEM((8, 3, block, LANES), f32),
                pltpu.VMEM((2, 8, TILE, LANES), f32),
                pltpu.VMEM((2, 8, TILE, LANES), f32),
                pltpu.SemaphoreType.DMA((4,)),
                pltpu.SemaphoreType.DMA((3,)),
                pltpu.SemaphoreType.DMA((count,)),
                pltpu.SemaphoreType.DMA((4,)),
                pltpu.SemaphoreType.DMA((4,)),
                pltpu.SemaphoreType.DMA,
                pltpu.SemaphoreType.DMA,
                pltpu.SemaphoreType.DMA((2,)),
                pltpu.SemaphoreType.DMA((2,)),
            ],
            compiler_params=pltpu.CompilerParams(collective_id=0, has_side_effects=True),
        )(residual, density, gain, vertical, edge_panel.T, edge_side.T, edge_flip.T)
        spread = pltpu.with_memory_space_constraint(spread, pltpu.VMEM)
        small = pltpu.with_memory_space_constraint(small, pltpu.VMEM)
        return pl.pallas_call(
            unpack,
            out_shape=(
                jax.ShapeDtypeStruct(residual.shape, f32),
                jax.ShapeDtypeStruct((panels, rows // 2, cols // 2, levels), f32),
            ),
            in_specs=[pl.BlockSpec(memory_space=pltpu.VMEM)] * 2,
            out_specs=(pl.BlockSpec(memory_space=pltpu.VMEM),) * 2,
        )(spread, small)

    fields = P(None, "tx", "ty", None)
    return jax.shard_map(
        shards,
        mesh=mesh,
        in_specs=(fields,) * 4 + (P(),) * 3,
        out_specs=(fields, fields),
        check_vma=False,
    )
```

```python
import functools

import jax
import jax.numpy as jnp
from jax import lax
from jax.experimental import pallas as pl
from jax.experimental.pallas import tpu as pltpu
from jax.sharding import PartitionSpec as P

MESH = pl.DeviceIdType.MESH
relaxation = 0.8
LANES = 128
TILE = 8


def round_up(value, unit):
    return (value + unit - 1) // unit * unit


def kernel(
    nr,
    nc,
    res_hbm,
    den_hbm,
    gain_hbm,
    vert_hbm,
    panel_hbm,
    side_hbm,
    flip_hbm,
    spread,
    small_ref,
    inp,
    tables,
    packed,
    st_row,
    st_col,
    ex_row,
    ex_col,
    nb_row,
    nb_col,
    corner,
    rx_row,
    rx_col,
    ry_row,
    ry_col,
    in_sem,
    table_sem,
    send_sem,
    nb_sem,
    corner_sem,
    row_sem,
    col_sem,
    row_end_sem,
    col_end_sem,
):
    _, panels, rows, cols, levels = inp.shape
    half_r, half_c = rows // 2, cols // 2
    k = cols // rows
    length = half_r
    last = length - 1
    height = spread.shape[1] // 2
    block = st_row.shape[3]
    r = lax.axis_index("tx")
    c = lax.axis_index("ty")
    is_row = (r == 0) | (r == nr - 1)
    is_col = (c == 0) | (c == nc - 1)
    tr = (r == nr - 1).astype(jnp.int32)
    tc = (c == nc - 1).astype(jnp.int32)
    row_ok = (r > 0, r < nr - 1)
    col_ok = (c > 0, c < nc - 1)

    def row_segment(f, p):
        return k * c + p if f == 0 else nr - 1 - k * c - p

    def col_segment(f):
        return r if f == 0 else nr - 1 - r

    def clamp(x, n):
        return jnp.minimum(jnp.maximum(x, 0), n - 1)

    used = 6

    def traffic(sending):
        count = [0]

        def remote(src, dst, sem, dest):
            m = count[0]
            count[0] += 1
            if sending:
                pltpu.make_async_remote_copy(
                    src_ref=src,
                    dst_ref=dst,
                    send_sem=send_sem.at[m],
                    recv_sem=sem,
                    device_id=dest,
                    device_id_type=MESH,
                ).start()
            else:
                pltpu.make_async_copy(src, src, send_sem.at[m]).wait()

        def local(src, dst, sem):
            if sending:
                pltpu.make_async_copy(src, dst, sem).start()

        def either(src, dst, sem, dest, mine):
            @pl.when(jnp.logical_not(mine))
            def _():
                remote(src, dst, sem, dest)

            @pl.when(mine)
            def _():
                local(src, dst, sem)

        def at_row(e):
            return r == e * (nr - 1)

        def at_col(e):
            return c == e * (nc - 1)

        def strips_to_rows(e):
            row = e * (nr - 1)

            @pl.when(is_row)
            def _():
                src = st_row.at[tr]
                remote(src, rx_row.at[4 + tr], row_sem, (row, nc - 1 - c))
                either(src, rx_row.at[tr], row_sem, (row, c), at_row(e))

            @pl.when(is_col)
            def _():
                for f in (1, 0):
                    dst = rx_row.at[4 * f + 2 + tc, lax.rem(r, k)]
                    to = lax.div(col_segment(f), k)
                    either(st_col.at[tc], dst, row_sem, (row, to), at_row(e) & (to == c))

        def strips_to_columns(e):
            col = e * (nc - 1)

            @pl.when(is_row)
            def _():
                for p in range(k):
                    extreme = (c == 0) if p == 0 else (c == nc - 1)
                    if k == 1:
                        extreme = extreme | (c == nc - 1)

                    def to_columns(p=p):
                        for f in (1, 0):
                            to = row_segment(f, p)
                            remote(st_row.at[tr, p], rx_col.at[4 * f + tr], col_sem, (to, col))

                    if 0 < p < k - 1:
                        to_columns()
                    else:
                        pl.when(jnp.logical_not(extreme))(to_columns)

            @pl.when(is_col & jnp.logical_not(is_row))
            def _():
                src = st_col.at[tc]
                remote(src, rx_col.at[6 + tc], col_sem, (nr - 1 - r, col))
                either(src, rx_col.at[2 + tc], col_sem, (r, col), at_col(e))

        def ends(e):
            row, col = e * (nr - 1), e * (nc - 1)
            for f in (1, 0):
                for h in range(2):
                    d = 1 if h != f else -1
                    end = 0 if d == 1 else 1

                    @pl.when(is_row)
                    def _():
                        slot = 4 * f + tr
                        for p in range(k):
                            outer_end = p == (k - 1 if h == 1 else 0)

                            def one_end(p=p, outer_end=outer_end):
                                src = ex_row.at[tr, p, h, 0:used]
                                if outer_end:
                                    to = clamp((c if f == 0 else nc - 1 - c) + d, nc)
                                    dst = ry_row.at[end, slot, 0:used]
                                    sem = row_end_sem.at[end]
                                    if f == 0:
                                        remote(src, dst, sem, (row, to))
                                    else:
                                        either(src, dst, sem, (row, to), at_row(e) & (to == c))
                                to = clamp(row_segment(f, p) + d, nr)
                                dst = ry_col.at[end, slot, 0:used]
                                sem = col_end_sem.at[end]
                                either(src, dst, sem, (to, col), at_col(e) & (to == r))

                            if outer_end:
                                pl.when(col_ok[h])(one_end)
                            else:
                                one_end()

                    @pl.when(is_col & row_ok[h])
                    def _():
                        slot = 4 * f + 2 + tc
                        src = ex_col.at[tc, h, 0:used]
                        g = col_segment(f)

                        def crossing():
                            to = clamp(lax.div(g, k) + d, nc)
                            dst = ry_row.at[end, slot, 0:used]
                            sem = row_end_sem.at[end]
                            either(src, dst, sem, (row, to), at_row(e) & (to == c))

                        if k == 1:
                            crossing()
                        else:
                            pl.when(lax.rem(g, k) == (k - 1 if d == 1 else 0))(crossing)
                        to = clamp(g + d, nr)
                        dst = ry_col.at[end, slot, 0:used]
                        sem = col_end_sem.at[end]
                        if f == 0:
                            remote(src, dst, sem, (to, col))
                        else:
                            either(src, dst, sem, (to, col), at_col(e) & (to == r))

        def within(s):
            @pl.when(row_ok[s])
            def _():
                remote(st_row.at[s], nb_row.at[1 - s], nb_sem.at[1 - s], (r + 2 * s - 1, c))

            @pl.when(col_ok[s])
            def _():
                remote(st_col.at[s], nb_col.at[1 - s], nb_sem.at[3 - s], (r, c + 2 * s - 1))

            for w in range(2):
                at = 2 * (1 - s) + 1 - w

                @pl.when(row_ok[s] & col_ok[w])
                def _():
                    remote(
                        ex_row.at[s, w * (k - 1), w, 0:used],
                        corner.at[at, 0:used],
                        corner_sem.at[at],
                        (r + 2 * s - 1, c + 2 * w - 1),
                    )

        within(0)
        strips_to_rows(0)
        ends(0)
        strips_to_columns(0)
        strips_to_rows(1)
        ends(1)
        strips_to_columns(1)
        within(1)

    loads = [
        pltpu.make_async_copy(source, inp.at[i], in_sem.at[i])
        for i, source in enumerate((gain_hbm, vert_hbm, den_hbm, res_hbm))
    ]
    for load in loads:
        load.start()
    table_loads = [
        pltpu.make_async_copy(source, tables.at[i], table_sem.at[i])
        for i, source in enumerate((panel_hbm, side_hbm, flip_hbm))
    ]
    for load in table_loads:
        load.start()

    barrier = pltpu.get_barrier_semaphore()
    far_r, near_r = (1 - tr) * (nr - 1), tr * (nr - 1)
    far_c, near_c = (1 - tc) * (nc - 1), tc * (nc - 1)

    def greet(dest):
        pl.semaphore_signal(barrier, inc=1, device_id=dest, device_id_type=MESH)

    def number(flag):
        return flag.astype(jnp.int32)

    def row_greetings():
        found = []
        for near in (False, True):
            for f in (1, 0):
                here = c if f == 0 else nc - 1 - c
                for d in (0, -1, 1):
                    if near and f == 0 and d == 0:
                        continue
                    ok = None if d == 0 else (here > 0) if d == -1 else (here < nc - 1)
                    mine = (here + d == c) if near and f == 1 and d else None
                    found.append((ok, mine, (near_r if near else far_r, clamp(here + d, nc))))
        for near in (False, True):
            for f in (1, 0):
                low = row_segment(f, 0 if f == 0 else k - 1)
                for d in range(-1, k + 1):
                    ok = None if 0 <= d < k else (low > 0) if d == -1 else (low + d < nr)
                    mine = (is_col & (low + d == r)) if near else None
                    found.append((ok, mine, (clamp(low + d, nr), near_c if near else far_c)))
        return found

    def col_greetings():
        found = []
        for near in (False, True):
            for f in (1, 0):
                g = col_segment(f)
                for d in (0, -1, 1):
                    inside = None if d == 0 else (g > 0) if d == -1 else (g < nr - 1)
                    if not (near and f == 0 and d == 0):
                        mine = (g + d == r) if near and f == 1 and d else None
                        found.append((inside, mine, (clamp(g + d, nr), near_c if near else far_c)))
                    cross = inside
                    if d and k > 1:
                        cross = inside & (lax.rem(g, k) == (k - 1 if d == 1 else 0))
                    to = lax.div(g, k) + d
                    mine = (is_row & (to == c)) if near else None
                    found.append((cross, mine, (near_r if near else far_r, clamp(to, nc))))
        return found

    def near_greetings():
        found = []
        for dr in (-1, 0, 1):
            for dc in (-1, 0, 1):
                if dr or dc:
                    ok = row_ok[(dr + 1) // 2] if dr else None
                    if dc:
                        side = col_ok[(dc + 1) // 2]
                        ok = side if ok is None else ok & side
                    found.append((ok, None, (r + dr, c + dc)))
        return found

    def announce(found):
        total = jnp.int32(0)
        for ok, mine, dest in found:
            go = ok
            if mine is not None:
                go = jnp.logical_not(mine) if go is None else go & jnp.logical_not(mine)
            if go is None:
                total = total + 1
            else:
                total = total + number(go)
        return total

    def tell(found):
        for ok, mine, dest in found:
            go = ok
            if mine is not None:
                go = jnp.logical_not(mine) if go is None else go & jnp.logical_not(mine)
            if go is None:
                greet(dest)
            else:
                pl.when(go)(functools.partial(greet, dest))

    pl.when(is_row)(lambda: tell(row_greetings()))
    pl.when(is_col)(lambda: tell(col_greetings()))
    tell(near_greetings())
    expected = announce(near_greetings())
    expected = expected + jnp.where(is_row, announce(row_greetings()), 0)
    expected = expected + jnp.where(is_col, announce(col_greetings()), 0)

    lane = lax.broadcasted_iota(jnp.int32, (TILE, LANES), 1)
    sub = lax.broadcasted_iota(jnp.int32, (height, LANES), 0)
    level = lane[:1] % levels
    first_level = level == 0
    last_level = level == levels - 1

    def lower(x):
        return jnp.where(first_level, 0.0, pltpu.roll(x, 1, 1))

    def upper(x):
        return jnp.where(last_level, 0.0, pltpu.roll(x, LANES - 1, 1))

    def pick_tables(side):
        index = lane
        code = jnp.zeros_like(lane)
        for p in range(panels):
            here = lane // levels == p
            index = jnp.where(here, tables[0, side, p] * levels + lane % levels, index)
            code = jnp.where(here, tables[2, side, p] * 4 + tables[1, side, p], code)
        return index, code

    def pack(value):
        filler = jnp.zeros((rows, cols, LANES - panels * levels), jnp.float32)
        return jnp.concatenate([value[p] for p in range(panels)] + [filler], axis=-1)

    def split(which, value):
        packed[which, :, :cols, :] = value
        if packed.shape[2] > cols:
            packed[which, :, cols:, :] = jnp.zeros(
                (rows, packed.shape[2] - cols, LANES), jnp.float32
            )
        return [
            [packed[which, y, pl.ds(b, height, stride=2), :] for b in range(2)]
            for y in range(rows)
        ]

    def fine(fun):
        return [[fun(y, b) for b in range(2)] for y in range(rows)]

    small = range(half_r)

    def block_mean(values, i):
        y = 2 * i
        return 0.25 * (values[y][0] + values[y][1] + values[y + 1][0] + values[y + 1][1])

    loads[0].wait()
    gain = split(1, pack(inp[0]))
    loads[1].wait()
    vertical = split(2, pack(inp[1]))
    low_vert = fine(lambda y, b: lower(vertical[y][b]))
    inverse = fine(
        lambda y, b: relaxation / (gain[y][b] + 4.0 + vertical[y][b] + low_vert[y][b])
    )
    c_vert = [block_mean(vertical, i) for i in small]
    c_low = [lower(c_vert[i]) for i in small]
    c_inv = [relaxation / (block_mean(gain, i) + 1.0 + c_vert[i] + c_low[i]) for i in small]
    loads[2].wait()
    loads[3].wait()
    right_side = split(0, pack(inp[2] * inp[3]))
    smoothed = fine(lambda y, b: inverse[y][b] * right_side[y][b])

    def inner(y, b):
        x = smoothed[y][b]
        return vertical[y][b] * upper(x) + low_vert[y][b] * lower(x)

    coupled = fine(inner)
    column = fine(lambda y, b: coupled[y][b] + (1.0 - relaxation) * right_side[y][b])
    north = [smoothed[2 * i][0] + smoothed[2 * i][1] for i in small]
    south = [smoothed[2 * i + 1][0] + smoothed[2 * i + 1][1] for i in small]
    west = [smoothed[2 * i][0] + smoothed[2 * i + 1][0] for i in small]
    east = [smoothed[2 * i][1] + smoothed[2 * i + 1][1] for i in small]
    from_w = [pltpu.roll(east[i], 1, 0) for i in small]
    from_e = [pltpu.roll(west[i], height - 1, 0) for i in small]
    start_w = sub % length == 0
    start_e = sub % length == last
    edge_w = sub == 0
    edge_e = sub == half_c - 1

    def bare(i):
        total = block_mean(column, i) + 0.5 * (north[i] + south[i])
        beside = None
        if i > 0:
            beside = south[i - 1]
        if i < half_r - 1:
            beside = north[i + 1] if beside is None else beside + north[i + 1]
        return total if beside is None else total + 0.25 * beside

    plain = [bare(i) for i in small]

    def partial_guess(i, mask_w, mask_e):
        beside = jnp.where(mask_w, 0.0, from_w[i]) + jnp.where(mask_e, 0.0, from_e[i])
        return c_inv[i] * (plain[i] + 0.25 * beside)

    by_tile = [partial_guess(i, edge_w, edge_e) for i in small]
    by_piece = by_tile if k == 1 else [partial_guess(i, start_w, start_e) for i in small]

    def put(ref, at, value):
        ref[at : at + value.shape[0], :] = value

    for s in range(2):
        y = s * (rows - 1)
        i0, i1 = (0, 1) if s == 0 else (half_r - 1, half_r - 2)
        out = north[0] if s == 0 else south[half_r - 1]
        for p in range(k):
            lo, hi = p * length, p * length + last
            seg = slice(lo, hi + 1)
            one = lambda x, j: x[j : j + 1]
            a, b, g = (st_row.at[s, p, q] for q in range(3))
            put(a, 0, smoothed[y][0][seg])
            put(a, length, smoothed[y][1][seg])
            put(a, 2 * length, one(c_inv[i1], lo))
            put(a, 2 * length + 1, one(c_inv[i1], hi))
            put(b, 0, by_piece[i0][seg])
            put(b, length, by_piece[i1][seg])
            put(b, 2 * length, one(west[i0], lo))
            put(b, 2 * length + 1, one(east[i0], hi))
            put(g, 0, c_inv[i0][seg])
            put(g, length, c_vert[i0][seg])
            put(g, 2 * length, one(west[i1], lo))
            put(g, 2 * length + 1, one(east[i1], hi))
            for h in range(2):
                j, j1 = (lo, lo + 1) if h == 0 else (hi, hi - 1)
                side = west if h == 0 else east
                x = ex_row.at[s, p, h]
                put(x, 0, one(by_piece[i0], j))
                put(x, 1, one(c_inv[i0], j))
                put(x, 2, one(side[i0], j))
                put(x, 3, one(side[i1], j))
                put(x, 4, one(out, j))
                put(x, 5, one(out, j1))
    for s in range(2):
        j0, j1 = (0, 1) if s == 0 else (half_c - 1, half_c - 2)
        out = west if s == 0 else east
        a, b, g = (st_col.at[s, q] for q in range(3))
        at0 = lambda x: x[j0 : j0 + 1]
        at1 = lambda x: x[j1 : j1 + 1]
        for y in range(rows):
            put(a, (y % 2) * length + y // 2, at0(smoothed[y][s]))
        put(a, 2 * length, at1(c_inv[0]))
        put(a, 2 * length + 1, at1(c_inv[half_r - 1]))
        for i in small:
            put(b, i, at0(by_tile[i]))
            put(b, length + i, at1(by_tile[i]))
            put(g, i, at0(c_inv[i]))
            put(g, length + i, at0(c_vert[i]))
        put(b, 2 * length, at0(north[0]))
        put(b, 2 * length + 1, at0(south[half_r - 1]))
        put(g, 2 * length, at1(north[0]))
        put(g, 2 * length + 1, at1(south[half_r - 1]))
        for h in range(2):
            i0, i1 = (0, 1) if h == 0 else (half_r - 1, half_r - 2)
            side = north[0] if h == 0 else south[half_r - 1]
            x = ex_col.at[s, h]
            put(x, 0, at0(by_tile[i0]))
            put(x, 1, at0(c_inv[i0]))
            put(x, 2, at0(side))
            put(x, 3, at1(side))
            put(x, 4, at0(out[i0]))
            put(x, 5, at0(out[i1]))

    pl.semaphore_wait(barrier, expected)
    traffic(True)

    def beside(y, b):
        x = smoothed[y][b]
        total = coupled[y][b] + smoothed[y][1 - b]
        if y > 0:
            total = total + smoothed[y - 1][b]
        if y < rows - 1:
            total = total + smoothed[y + 1][b]
        return total

    partial = fine(beside)
    traffic(False)

    for load in table_loads:
        load.wait()
    row_pick = pick_tables(tr)
    col_pick = pick_tables(2 + tc)

    def arrived(ref, sem):
        pltpu.make_async_copy(ref, ref, sem).wait()

    for s in range(2):

        @pl.when(row_ok[s])
        def _():
            arrived(nb_row.at[s], nb_sem.at[s])

        @pl.when(col_ok[s])
        def _():
            arrived(nb_col.at[s], nb_sem.at[2 + s])

        for w in range(2):

            @pl.when(row_ok[s] & col_ok[w])
            def _():
                arrived(corner.at[2 * s + w, 0:used], corner_sem.at[2 * s + w])

    order = list(range(2 * length))[::-1] + [2 * length + 1, 2 * length]
    other = (
        list(range(length))[::-1]
        + list(range(length, 2 * length))[::-1]
        + [2 * length + 1, 2 * length]
    )
    sublane = lax.broadcasted_iota(jnp.int32, (block, LANES), 0)

    def flip_index(perm):
        index = sublane
        for at, source in enumerate(perm):
            index = jnp.where(sublane == at, source, index)
        return index

    flips = [flip_index(order), flip_index(other), flip_index(other)]

    def choose(read, pick, f):
        index, code = pick
        taken = None
        for t in range(4):
            moved = jnp.take_along_axis(read(4 * f + t), index, axis=1, mode="promise_in_bounds")
            taken = moved if taken is None else jnp.where(code == 4 * f + t, moved, taken)
        return taken

    def select(plainly, reverse, pick, group):
        straight = choose(plainly, pick, 0)
        turned = choose(reverse, pick, 1)
        if group is not None:
            turned = jnp.take_along_axis(turned, flips[group], axis=0, mode="promise_in_bounds")
        return jnp.where(pick[1] >= 4, turned, straight)

    @pl.when(is_row)
    def _():
        arrived(rx_row, row_sem)
        for p in range(k):
            for q in range(3):
                nb_row[tr, p, q] = select(
                    lambda s: rx_row[s, p, q], lambda s: rx_row[s, k - 1 - p, q], row_pick, q
                )
        for w in range(2):

            @pl.when(col_ok[w])
            def _():
                arrived(ry_row.at[w, :, 0:used], row_end_sem.at[w])
                read = lambda s: ry_row[w, s]
                corner[2 * tr + w] = select(read, read, row_pick, None)

    @pl.when(is_col & jnp.logical_not(is_row))
    def _():
        arrived(rx_col, col_sem)
        for q in range(3):
            read = lambda s: rx_col[s, q]
            nb_col[tc, q] = select(read, read, col_pick, q)

    @pl.when(is_col & is_row)
    def _():
        swap = (tr != tc).astype(jnp.int32)
        for q in range(3):

            def read(s, q=q):
                f, t = s // 4, s % 4
                at = 4 * (1 - swap) + t if f == 1 else 4 * swap + t
                return rx_row[at, (tr if f == 0 else 1 - tr) * (k - 1), q]

            nb_col[tc, q] = select(read, read, col_pick, q)

    @pl.when(is_col)
    def _():
        for s in range(2):

            @pl.when(row_ok[s])
            def _():
                arrived(ry_col.at[s, :, 0:used], col_end_sem.at[s])
                read = lambda slot: ry_col[s, slot]
                value = select(read, read, col_pick, None)
                corner[2 * s + tc, 0:2, :] = value[0:2]
                corner[2 * s + tc, 2:4, :] = value[4:6]
                corner[2 * s + tc, 4:6, :] = value[2:4]

    @pl.when(is_row & is_col)
    def _():
        at = 2 * tr + tc
        corner[at, 0:2, :] = jnp.zeros((2, LANES), jnp.float32)
        for q in range(2):
            rows_z = nb_col[tc, 1 + q]
            rows_x = nb_row[tr, tc * (k - 1), 1 + q]
            corner[at, 2 + q : 3 + q, :] = jnp.where(
                tr == 0, rows_z[2 * length : 2 * length + 1], rows_z[2 * length + 1 : 2 * length + 2]
            )
            corner[at, 4 + q : 5 + q, :] = jnp.where(
                tc == 0, rows_x[2 * length : 2 * length + 1], rows_x[2 * length + 1 : 2 * length + 2]
            )

    def zeros(count):
        return [jnp.zeros((count, LANES), jnp.float32)] if count else []

    def stack(lines, total):
        used = sum(x.shape[0] for x in lines)
        return jnp.concatenate(list(lines) + zeros(total - used), axis=0)

    tall_z = round_up(half_r, TILE)
    flat = 2 * length

    class Strip:
        pass

    def strip(read, pieces, ends, total, own):
        def gather(q, at):
            return stack([read(p, q, slice(at, at + length)) for p in range(pieces)], total)

        def sides(first, final):
            lines = []
            for p in range(pieces):
                lines += [first(p)] + zeros(length - 2) + [final(p)]
            return stack(lines, total)

        def lateral(q):
            return sides(
                lambda p: ends[0][q] if p == 0 else read(p - 1, 1 + q, slice(flat + 1, flat + 2)),
                lambda p: ends[1][q]
                if p == pieces - 1
                else read(p + 1, 1 + q, slice(flat, flat + 1)),
            )

        x = Strip()
        x.even, x.odd = gather(0, 0), gather(0, length)
        x.pair = x.even + x.odd
        inv1 = sides(
            lambda p: read(p, 0, slice(flat, flat + 1)),
            lambda p: read(p, 0, slice(flat + 1, flat + 2)),
        )
        x.inv, x.vert = gather(2, 0), gather(2, length)
        x.guess = gather(1, 0) + 0.25 * x.inv * (lateral(0) + own)
        x.inside = gather(1, length) + 0.25 * inv1 * lateral(1)
        return x

    def corner_row(s, w, at):
        return corner[2 * s + w, at : at + 1, :]

    row_strip = []
    for s in range(2):
        own = north[0] if s == 0 else south[half_r - 1]
        ends = [[corner_row(s, w, 2 + q) for q in range(2)] for w in range(2)]
        row_strip.append(
            strip(lambda p, q, rows_: nb_row[s, p, q, rows_, :], k, ends, height, own)
        )
    col_strip = []
    for w in range(2):
        j = w * (half_c - 1)
        faces = west if w == 0 else east
        own = stack([faces[i][j : j + 1] for i in small], tall_z)
        ends = [[corner_row(s, w, 4 + q) for q in range(2)] for s in range(2)]
        col_strip.append(
            strip(lambda p, q, rows_: nb_col[w, q, rows_, :], 1, ends, tall_z, own)
        )

    guess = []
    for i in small:
        lateral = jnp.where(edge_w, col_strip[0].pair[i : i + 1], 0.0)
        lateral = lateral + jnp.where(edge_e, col_strip[1].pair[i : i + 1], 0.0)
        if i == 0:
            lateral = lateral + row_strip[0].pair
        if i == half_r - 1:
            lateral = lateral + row_strip[1].pair
        guess.append(by_tile[i] + 0.25 * c_inv[i] * lateral)

    row_side = [[None] * 2 for _ in range(2)]
    col_side = [[None] * 2 for _ in range(2)]
    for s in range(2):
        for w in range(2):
            faces = nb_row[s, w * (k - 1), 1, flat + w : flat + w + 1, :]
            faces = faces + nb_col[w, 1, flat + s : flat + s + 1, :]
            there = corner_row(s, w, 0) + 0.25 * corner_row(s, w, 1) * faces
            tip = (r == s * (nr - 1)) & (c == w * (nc - 1))
            jr, jc = w * (half_c - 1), s * (half_r - 1)
            row_side[s][w] = jnp.where(tip, col_strip[w].guess[jc : jc + 1], there)
            col_side[w][s] = jnp.where(tip, row_strip[s].guess[jr : jr + 1], there)

    def relax(x, ends, own, count):
        total = x.guess.shape[0]
        at = lax.broadcasted_iota(jnp.int32, (total, LANES), 0)
        around = x.inside + own
        around = around + jnp.where(at == 0, ends[0], pltpu.roll(x.guess, 1, 0))
        around = around + jnp.where(at == count - 1, ends[1], pltpu.roll(x.guess, total - 1, 0))
        column = x.vert * upper(x.guess) + lower(x.vert) * lower(x.guess)
        return (2.0 - relaxation) * x.guess + x.inv * (0.25 * around + column)

    row_fix = [
        relax(row_strip[s], row_side[s], guess[s * (half_r - 1)], half_c) for s in range(2)
    ]
    col_fix = []
    for w in range(2):
        j = w * (half_c - 1)
        own = stack([guess[i][j : j + 1] for i in small], tall_z)
        col_fix.append(relax(col_strip[w], col_side[w], own, half_r))

    def from_left(x, line):
        return jnp.where(edge_w, line, pltpu.roll(x, 1, 0))

    def from_right(x, line):
        return jnp.where(edge_e, line, pltpu.roll(x, height - 1, 0))

    correction = []
    for i in small:
        x = guess[i]
        around = from_left(x, col_strip[0].guess[i : i + 1])
        around = around + from_right(x, col_strip[1].guess[i : i + 1])
        around = around + (guess[i - 1] if i > 0 else row_strip[0].guess)
        around = around + (guess[i + 1] if i < half_r - 1 else row_strip[1].guess)
        levels_part = c_vert[i] * upper(x) + c_low[i] * lower(x)
        correction.append((2.0 - relaxation) * x + c_inv[i] * (0.25 * around + levels_part))
        small_ref[i] = correction[i]

    def outer(y, b):
        at = (y % 2) * length + y // 2
        source = col_strip[b]
        line = (source.even if y % 2 == 0 else source.odd)[y // 2 : y // 2 + 1]
        if b == 0:
            total = partial[y][b] + from_left(smoothed[y][1], line)
        else:
            total = partial[y][b] + from_right(smoothed[y][0], line)
        if y == 0:
            total = total + (row_strip[0].even if b == 0 else row_strip[0].odd)
        if y == rows - 1:
            total = total + (row_strip[1].even if b == 0 else row_strip[1].odd)
        return total

    c_up = [upper(x) for x in correction]
    c_down = [lower(x) for x in correction]
    left = [from_left(correction[i], col_fix[0][i : i + 1]) for i in small]
    right = [from_right(correction[i], col_fix[1][i : i + 1]) for i in small]
    for y in range(rows):
        i = y // 2
        next_i = i - 1 if y % 2 == 0 else i + 1
        for b in range(2):
            total = outer(y, b) + 2.0 * correction[i]
            total = total + vertical[y][b] * c_up[i] + low_vert[y][b] * c_down[i]
            if next_i < 0:
                total = total + row_fix[0]
            elif next_i >= half_r:
                total = total + row_fix[1]
            else:
                total = total + correction[next_i]
            total = total + (left if b == 0 else right)[i]
            first = (2.0 - relaxation) * smoothed[y][b] + (1.0 - relaxation) * correction[i]
            spread[y, pl.ds(b, height, stride=2), :] = first + inverse[y][b] * total


def unpack(spread, small_ref, sol_ref, corr_ref):
    panels, _, cols, levels = sol_ref.shape
    half_c = corr_ref.shape[2]
    for p in range(panels):
        lanes = slice(p * levels, (p + 1) * levels)
        sol_ref[p] = spread[:, :cols, lanes]
        corr_ref[p] = small_ref[:, :half_c, lanes]


def solution(mesh):
    nr, nc = mesh.shape["tx"], mesh.shape["ty"]

    def shards(residual, density, gain, vertical, edge_panel, edge_side, edge_flip):
        panels, rows, cols, levels = residual.shape
        k = cols // rows
        assert cols == k * rows and rows % 2 == 0 and panels * levels <= LANES
        assert rows >= 6 and nr > 1 and nc > 1
        block = round_up(rows + 2, TILE)
        height = round_up(cols // 2, TILE)
        tall = 2 * height
        f32 = jnp.float32
        count = 4 + 8 + 4 * k + 8 * k + 8 + 16 + 4 + 4
        spread, small = pl.pallas_call(
            functools.partial(kernel, nr, nc),
            out_shape=(
                pltpu.VMEM((rows, tall, LANES), f32),
                pltpu.VMEM((rows // 2, height, LANES), f32),
            ),
            in_specs=[pl.BlockSpec(memory_space=pl.ANY)] * 7,
            out_specs=(pl.BlockSpec(memory_space=pltpu.VMEM),) * 2,
            scratch_shapes=[
                pltpu.VMEM((4, panels, rows, cols, levels), f32),
                pltpu.SMEM((3,) + edge_panel.T.shape, jnp.int32),
                pltpu.VMEM((3, rows, tall, LANES), f32),
                pltpu.VMEM((3, k, 3, block, LANES), f32),
                pltpu.VMEM((3, 3, block, LANES), f32),
                pltpu.VMEM((3, k, 2, TILE, LANES), f32),
                pltpu.VMEM((3, 2, TILE, LANES), f32),
                pltpu.VMEM((3, k, 3, block, LANES), f32),
                pltpu.VMEM((3, 3, block, LANES), f32),
                pltpu.VMEM((5, TILE, LANES), f32),
                pltpu.VMEM((8, k, 3, block, LANES), f32),
                pltpu.VMEM((8, 3, block, LANES), f32),
                pltpu.VMEM((2, 8, TILE, LANES), f32),
                pltpu.VMEM((2, 8, TILE, LANES), f32),
                pltpu.SemaphoreType.DMA((4,)),
                pltpu.SemaphoreType.DMA((3,)),
                pltpu.SemaphoreType.DMA((count,)),
                pltpu.SemaphoreType.DMA((4,)),
                pltpu.SemaphoreType.DMA((4,)),
                pltpu.SemaphoreType.DMA,
                pltpu.SemaphoreType.DMA,
                pltpu.SemaphoreType.DMA((2,)),
                pltpu.SemaphoreType.DMA((2,)),
            ],
            compiler_params=pltpu.CompilerParams(collective_id=0, has_side_effects=True),
        )(residual, density, gain, vertical, edge_panel.T, edge_side.T, edge_flip.T)
        spread = pltpu.with_memory_space_constraint(spread, pltpu.VMEM)
        small = pltpu.with_memory_space_constraint(small, pltpu.VMEM)
        return pl.pallas_call(
            unpack,
            out_shape=(
                jax.ShapeDtypeStruct(residual.shape, f32),
                jax.ShapeDtypeStruct((panels, rows // 2, cols // 2, levels), f32),
            ),
            in_specs=[pl.BlockSpec(memory_space=pltpu.VMEM)] * 2,
            out_specs=(pl.BlockSpec(memory_space=pltpu.VMEM),) * 2,
        )(spread, small)

    fields = P(None, "tx", "ty", None)
    return jax.shard_map(
        shards,
        mesh=mesh,
        in_specs=(fields,) * 4 + (P(),) * 3,
        out_specs=(fields, fields),
        check_vma=False,
    )
```

```python
import functools

import jax
import jax.numpy as jnp
from jax import lax
from jax.experimental import pallas as pl
from jax.experimental.pallas import tpu as pltpu
from jax.sharding import PartitionSpec as P

MESH = pl.DeviceIdType.MESH
relaxation = 0.8
LANES = 128
TILE = 8


def round_up(value, unit):
    return (value + unit - 1) // unit * unit


def kernel(
    nr,
    nc,
    res_hbm,
    den_hbm,
    gain_hbm,
    vert_hbm,
    panel_hbm,
    side_hbm,
    flip_hbm,
    spread,
    small_ref,
    inp,
    tables,
    packed,
    st_row,
    st_col,
    ex_row,
    ex_col,
    nb_row,
    nb_col,
    corner,
    rx_row,
    rx_col,
    ry_row,
    ry_col,
    in_sem,
    table_sem,
    send_sem,
    nb_sem,
    corner_sem,
    row_sem,
    col_sem,
    row_end_sem,
    col_end_sem,
):
    _, panels, rows, cols, levels = inp.shape
    half_r, half_c = rows // 2, cols // 2
    k = cols // rows
    length = half_r
    last = length - 1
    height = spread.shape[1] // 2
    block = st_row.shape[3]
    r = lax.axis_index("tx")
    c = lax.axis_index("ty")
    is_row = (r == 0) | (r == nr - 1)
    is_col = (c == 0) | (c == nc - 1)
    tr = (r == nr - 1).astype(jnp.int32)
    tc = (c == nc - 1).astype(jnp.int32)
    row_ok = (r > 0, r < nr - 1)
    col_ok = (c > 0, c < nc - 1)

    def row_segment(f, p):
        return k * c + p if f == 0 else nr - 1 - k * c - p

    def col_segment(f):
        return r if f == 0 else nr - 1 - r

    def clamp(x, n):
        return jnp.minimum(jnp.maximum(x, 0), n - 1)

    used = 6

    def traffic(sending):
        def remote(src, dst, sem, dest):
            if sending:
                pltpu.make_async_remote_copy(
                    src_ref=src,
                    dst_ref=dst,
                    send_sem=send_sem.at[0],
                    recv_sem=sem,
                    device_id=dest,
                    device_id_type=MESH,
                ).start()
            else:
                pltpu.make_async_copy(src, src, send_sem.at[0]).wait()

        def local(src, dst, sem):
            if sending:
                pltpu.make_async_copy(src, dst, sem).start()

        def either(src, dst, sem, dest, mine):
            @pl.when(jnp.logical_not(mine))
            def _():
                remote(src, dst, sem, dest)

            @pl.when(mine)
            def _():
                local(src, dst, sem)

        def at_row(e):
            return r == e * (nr - 1)

        def at_col(e):
            return c == e * (nc - 1)

        def strips_to_rows(e):
            row = e * (nr - 1)

            @pl.when(is_row)
            def _():
                src = st_row.at[tr]
                remote(src, rx_row.at[4 + tr], row_sem, (row, nc - 1 - c))
                either(src, rx_row.at[tr], row_sem, (row, c), at_row(e))

            @pl.when(is_col)
            def _():
                for f in (1, 0):
                    dst = rx_row.at[4 * f + 2 + tc, lax.rem(r, k)]
                    to = lax.div(col_segment(f), k)
                    either(st_col.at[tc], dst, row_sem, (row, to), at_row(e) & (to == c))

        def strips_to_columns(e):
            col = e * (nc - 1)

            @pl.when(is_row)
            def _():
                for p in range(k):
                    extreme = (c == 0) if p == 0 else (c == nc - 1)
                    if k == 1:
                        extreme = extreme | (c == nc - 1)

                    def to_columns(p=p):
                        for f in (1, 0):
                            to = row_segment(f, p)
                            remote(st_row.at[tr, p], rx_col.at[4 * f + tr], col_sem, (to, col))

                    if 0 < p < k - 1:
                        to_columns()
                    else:
                        pl.when(jnp.logical_not(extreme))(to_columns)

            @pl.when(is_col & jnp.logical_not(is_row))
            def _():
                src = st_col.at[tc]
                remote(src, rx_col.at[6 + tc], col_sem, (nr - 1 - r, col))
                either(src, rx_col.at[2 + tc], col_sem, (r, col), at_col(e))

        def ends(e):
            row, col = e * (nr - 1), e * (nc - 1)
            for f in (1, 0):
                for h in range(2):
                    d = 1 if h != f else -1
                    end = 0 if d == 1 else 1

                    @pl.when(is_row)
                    def _():
                        slot = 4 * f + tr
                        for p in range(k):
                            outer_end = p == (k - 1 if h == 1 else 0)

                            def one_end(p=p, outer_end=outer_end):
                                src = ex_row.at[tr, p, h, 0:used]
                                if outer_end:
                                    to = clamp((c if f == 0 else nc - 1 - c) + d, nc)
                                    dst = ry_row.at[end, slot, 0:used]
                                    sem = row_end_sem.at[end]
                                    if f == 0:
                                        remote(src, dst, sem, (row, to))
                                    else:
                                        either(src, dst, sem, (row, to), at_row(e) & (to == c))
                                to = clamp(row_segment(f, p) + d, nr)
                                dst = ry_col.at[end, slot, 0:used]
                                sem = col_end_sem.at[end]
                                either(src, dst, sem, (to, col), at_col(e) & (to == r))

                            if outer_end:
                                pl.when(col_ok[h])(one_end)
                            else:
                                one_end()

                    @pl.when(is_col & row_ok[h])
                    def _():
                        slot = 4 * f + 2 + tc
                        src = ex_col.at[tc, h, 0:used]
                        g = col_segment(f)

                        def crossing():
                            to = clamp(lax.div(g, k) + d, nc)
                            dst = ry_row.at[end, slot, 0:used]
                            sem = row_end_sem.at[end]
                            either(src, dst, sem, (row, to), at_row(e) & (to == c))

                        if k == 1:
                            crossing()
                        else:
                            pl.when(lax.rem(g, k) == (k - 1 if d == 1 else 0))(crossing)
                        to = clamp(g + d, nr)
                        dst = ry_col.at[end, slot, 0:used]
                        sem = col_end_sem.at[end]
                        if f == 0:
                            remote(src, dst, sem, (to, col))
                        else:
                            either(src, dst, sem, (to, col), at_col(e) & (to == r))

        def within(s):
            @pl.when(row_ok[s])
            def _():
                remote(st_row.at[s], nb_row.at[1 - s], nb_sem.at[1 - s], (r + 2 * s - 1, c))

            @pl.when(col_ok[s])
            def _():
                remote(st_col.at[s], nb_col.at[1 - s], nb_sem.at[3 - s], (r, c + 2 * s - 1))

            for w in range(2):
                at = 2 * (1 - s) + 1 - w

                @pl.when(row_ok[s] & col_ok[w])
                def _():
                    remote(
                        ex_row.at[s, w * (k - 1), w, 0:used],
                        corner.at[at, 0:used],
                        corner_sem.at[at],
                        (r + 2 * s - 1, c + 2 * w - 1),
                    )

        strips_to_rows(0)
        within(0)
        ends(0)
        strips_to_rows(1)
        strips_to_columns(0)
        strips_to_columns(1)
        ends(1)
        within(1)

    loads = [
        pltpu.make_async_copy(source, inp.at[i], in_sem.at[i // 2])
        for i, source in enumerate((gain_hbm, vert_hbm, den_hbm, res_hbm))
    ]
    for load in loads:
        load.start()
    table_loads = [
        pltpu.make_async_copy(source, tables.at[i], table_sem.at[i])
        for i, source in enumerate((panel_hbm, side_hbm, flip_hbm))
    ]
    for load in table_loads:
        load.start()

    barrier = pltpu.get_barrier_semaphore()
    far_r, near_r = (1 - tr) * (nr - 1), tr * (nr - 1)
    far_c, near_c = (1 - tc) * (nc - 1), tc * (nc - 1)

    def greet(dest):
        pl.semaphore_signal(barrier, inc=1, device_id=dest, device_id_type=MESH)

    def number(flag):
        return flag.astype(jnp.int32)

    def row_greetings():
        found = []
        for near in (False, True):
            for f in (1, 0):
                here = c if f == 0 else nc - 1 - c
                for d in (0, -1, 1):
                    if near and f == 0 and d == 0:
                        continue
                    ok = None if d == 0 else (here > 0) if d == -1 else (here < nc - 1)
                    mine = (here + d == c) if near and f == 1 and d else None
                    found.append((ok, mine, (near_r if near else far_r, clamp(here + d, nc))))
        for near in (False, True):
            for f in (1, 0):
                low = row_segment(f, 0 if f == 0 else k - 1)
                for d in range(-1, k + 1):
                    ok = None if 0 <= d < k else (low > 0) if d == -1 else (low + d < nr)
                    mine = (is_col & (low + d == r)) if near else None
                    found.append((ok, mine, (clamp(low + d, nr), near_c if near else far_c)))
        return found

    def col_greetings():
        found = []
        for near in (False, True):
            for f in (1, 0):
                g = col_segment(f)
                for d in (0, -1, 1):
                    inside = None if d == 0 else (g > 0) if d == -1 else (g < nr - 1)
                    if not (near and f == 0 and d == 0):
                        mine = (g + d == r) if near and f == 1 and d else None
                        found.append((inside, mine, (clamp(g + d, nr), near_c if near else far_c)))
                    cross = inside
                    if d and k > 1:
                        cross = inside & (lax.rem(g, k) == (k - 1 if d == 1 else 0))
                    to = lax.div(g, k) + d
                    mine = (is_row & (to == c)) if near else None
                    found.append((cross, mine, (near_r if near else far_r, clamp(to, nc))))
        return found

    def near_greetings():
        found = []
        for dr in (-1, 0, 1):
            for dc in (-1, 0, 1):
                if dr or dc:
                    ok = row_ok[(dr + 1) // 2] if dr else None
                    if dc:
                        side = col_ok[(dc + 1) // 2]
                        ok = side if ok is None else ok & side
                    found.append((ok, None, (r + dr, c + dc)))
        return found

    def announce(found):
        total = jnp.int32(0)
        for ok, mine, dest in found:
            go = ok
            if mine is not None:
                go = jnp.logical_not(mine) if go is None else go & jnp.logical_not(mine)
            if go is None:
                total = total + 1
            else:
                total = total + number(go)
        return total

    def tell(found):
        for ok, mine, dest in found:
            go = ok
            if mine is not None:
                go = jnp.logical_not(mine) if go is None else go & jnp.logical_not(mine)
            if go is None:
                greet(dest)
            else:
                pl.when(go)(functools.partial(greet, dest))

    pl.when(is_row)(lambda: tell(row_greetings()))
    pl.when(is_col)(lambda: tell(col_greetings()))
    tell(near_greetings())
    expected = announce(near_greetings())
    expected = expected + jnp.where(is_row, announce(row_greetings()), 0)
    expected = expected + jnp.where(is_col, announce(col_greetings()), 0)

    lane = lax.broadcasted_iota(jnp.int32, (TILE, LANES), 1)
    sub = lax.broadcasted_iota(jnp.int32, (height, LANES), 0)
    level = lane[:1] % levels
    first_level = level == 0
    last_level = level == levels - 1

    def lower(x):
        return jnp.where(first_level, 0.0, pltpu.roll(x, 1, 1))

    def upper(x):
        return jnp.where(last_level, 0.0, pltpu.roll(x, LANES - 1, 1))

    def pick_tables(side):
        index = lane
        code = jnp.zeros_like(lane)
        for p in range(panels):
            here = lane // levels == p
            index = jnp.where(here, tables[0, side, p] * levels + lane % levels, index)
            code = jnp.where(here, tables[2, side, p] * 4 + tables[1, side, p], code)
        return index, code

    def pack(value):
        filler = jnp.zeros((rows, cols, LANES - panels * levels), jnp.float32)
        return jnp.concatenate([value[p] for p in range(panels)] + [filler], axis=-1)

    def split(which, value):
        packed[which, :, :cols, :] = value
        if packed.shape[2] > cols:
            packed[which, :, cols:, :] = jnp.zeros(
                (rows, packed.shape[2] - cols, LANES), jnp.float32
            )
        return [
            [packed[which, y, pl.ds(b, height, stride=2), :] for b in range(2)]
            for y in range(rows)
        ]

    def fine(fun):
        return [[fun(y, b) for b in range(2)] for y in range(rows)]

    small = range(half_r)

    def block_mean(values, i):
        y = 2 * i
        return 0.25 * (values[y][0] + values[y][1] + values[y + 1][0] + values[y + 1][1])

    pltpu.make_async_copy(inp.at[0:2], inp.at[0:2], in_sem.at[0]).wait()
    gain = split(1, pack(inp[0]))
    vertical = split(2, pack(inp[1]))
    low_vert = fine(lambda y, b: lower(vertical[y][b]))
    inverse = fine(
        lambda y, b: relaxation / (gain[y][b] + 4.0 + vertical[y][b] + low_vert[y][b])
    )
    c_vert = [block_mean(vertical, i) for i in small]
    c_low = [lower(c_vert[i]) for i in small]
    c_inv = [relaxation / (block_mean(gain, i) + 1.0 + c_vert[i] + c_low[i]) for i in small]
    pltpu.make_async_copy(inp.at[2:4], inp.at[2:4], in_sem.at[1]).wait()
    right_side = split(0, pack(inp[2] * inp[3]))
    smoothed = fine(lambda y, b: inverse[y][b] * right_side[y][b])

    def inner(y, b):
        x = smoothed[y][b]
        return vertical[y][b] * upper(x) + low_vert[y][b] * lower(x)

    coupled = fine(inner)
    column = fine(lambda y, b: coupled[y][b] + (1.0 - relaxation) * right_side[y][b])
    north = [smoothed[2 * i][0] + smoothed[2 * i][1] for i in small]
    south = [smoothed[2 * i + 1][0] + smoothed[2 * i + 1][1] for i in small]
    west = [smoothed[2 * i][0] + smoothed[2 * i + 1][0] for i in small]
    east = [smoothed[2 * i][1] + smoothed[2 * i + 1][1] for i in small]
    from_w = [pltpu.roll(east[i], 1, 0) for i in small]
    from_e = [pltpu.roll(west[i], height - 1, 0) for i in small]
    start_w = sub % length == 0
    start_e = sub % length == last
    edge_w = sub == 0
    edge_e = sub == half_c - 1

    def bare(i):
        total = block_mean(column, i) + 0.5 * (north[i] + south[i])
        beside = None
        if i > 0:
            beside = south[i - 1]
        if i < half_r - 1:
            beside = north[i + 1] if beside is None else beside + north[i + 1]
        return total if beside is None else total + 0.25 * beside

    plain = [bare(i) for i in small]

    def partial_guess(i, mask_w, mask_e):
        beside = jnp.where(mask_w, 0.0, from_w[i]) + jnp.where(mask_e, 0.0, from_e[i])
        return c_inv[i] * (plain[i] + 0.25 * beside)

    by_tile = [partial_guess(i, edge_w, edge_e) for i in small]
    by_piece = by_tile if k == 1 else [partial_guess(i, start_w, start_e) for i in small]

    def put(ref, at, value):
        ref[at : at + value.shape[0], :] = value

    for s in range(2):
        y = s * (rows - 1)
        i0, i1 = (0, 1) if s == 0 else (half_r - 1, half_r - 2)
        out = north[0] if s == 0 else south[half_r - 1]
        for p in range(k):
            lo, hi = p * length, p * length + last
            seg = slice(lo, hi + 1)
            one = lambda x, j: x[j : j + 1]
            a, b, g = (st_row.at[s, p, q] for q in range(3))
            put(a, 0, smoothed[y][0][seg])
            put(a, length, smoothed[y][1][seg])
            put(a, 2 * length, one(c_inv[i1], lo))
            put(a, 2 * length + 1, one(c_inv[i1], hi))
            put(b, 0, by_piece[i0][seg])
            put(b, length, by_piece[i1][seg])
            put(b, 2 * length, one(west[i0], lo))
            put(b, 2 * length + 1, one(east[i0], hi))
            put(g, 0, c_inv[i0][seg])
            put(g, length, c_vert[i0][seg])
            put(g, 2 * length, one(west[i1], lo))
            put(g, 2 * length + 1, one(east[i1], hi))
            for h in range(2):
                j, j1 = (lo, lo + 1) if h == 0 else (hi, hi - 1)
                side = west if h == 0 else east
                x = ex_row.at[s, p, h]
                put(x, 0, one(by_piece[i0], j))
                put(x, 1, one(c_inv[i0], j))
                put(x, 2, one(side[i0], j))
                put(x, 3, one(side[i1], j))
                put(x, 4, one(out, j))
                put(x, 5, one(out, j1))
    for s in range(2):
        j0, j1 = (0, 1) if s == 0 else (half_c - 1, half_c - 2)
        out = west if s == 0 else east
        a, b, g = (st_col.at[s, q] for q in range(3))
        at0 = lambda x: x[j0 : j0 + 1]
        at1 = lambda x: x[j1 : j1 + 1]
        for y in range(rows):
            put(a, (y % 2) * length + y // 2, at0(smoothed[y][s]))
        put(a, 2 * length, at1(c_inv[0]))
        put(a, 2 * length + 1, at1(c_inv[half_r - 1]))
        for i in small:
            put(b, i, at0(by_tile[i]))
            put(b, length + i, at1(by_tile[i]))
            put(g, i, at0(c_inv[i]))
            put(g, length + i, at0(c_vert[i]))
        put(b, 2 * length, at0(north[0]))
        put(b, 2 * length + 1, at0(south[half_r - 1]))
        put(g, 2 * length, at1(north[0]))
        put(g, 2 * length + 1, at1(south[half_r - 1]))
        for h in range(2):
            i0, i1 = (0, 1) if h == 0 else (half_r - 1, half_r - 2)
            side = north[0] if h == 0 else south[half_r - 1]
            x = ex_col.at[s, h]
            put(x, 0, at0(by_tile[i0]))
            put(x, 1, at0(c_inv[i0]))
            put(x, 2, at0(side))
            put(x, 3, at1(side))
            put(x, 4, at0(out[i0]))
            put(x, 5, at0(out[i1]))

    pl.semaphore_wait(barrier, expected)
    traffic(True)

    def beside(y, b):
        x = smoothed[y][b]
        total = coupled[y][b] + smoothed[y][1 - b]
        if y > 0:
            total = total + smoothed[y - 1][b]
        if y < rows - 1:
            total = total + smoothed[y + 1][b]
        return total

    partial = fine(beside)
    traffic(False)

    for load in table_loads:
        load.wait()
    row_pick = pick_tables(tr)
    col_pick = pick_tables(2 + tc)

    def arrived(ref, sem):
        pltpu.make_async_copy(ref, ref, sem).wait()

    for s in range(2):

        @pl.when(row_ok[s])
        def _():
            arrived(nb_row.at[s], nb_sem.at[s])

        @pl.when(col_ok[s])
        def _():
            arrived(nb_col.at[s], nb_sem.at[2 + s])

        for w in range(2):

            @pl.when(row_ok[s] & col_ok[w])
            def _():
                arrived(corner.at[2 * s + w, 0:used], corner_sem.at[2 * s + w])

    order = list(range(2 * length))[::-1] + [2 * length + 1, 2 * length]
    other = (
        list(range(length))[::-1]
        + list(range(length, 2 * length))[::-1]
        + [2 * length + 1, 2 * length]
    )
    sublane = lax.broadcasted_iota(jnp.int32, (block, LANES), 0)

    def flip_index(perm):
        index = sublane
        for at, source in enumerate(perm):
            index = jnp.where(sublane == at, source, index)
        return index

    flips = [flip_index(order), flip_index(other), flip_index(other)]

    def choose(read, pick, f):
        index, code = pick
        taken = None
        for t in range(4):
            moved = jnp.take_along_axis(read(4 * f + t), index, axis=1, mode="promise_in_bounds")
            taken = moved if taken is None else jnp.where(code == 4 * f + t, moved, taken)
        return taken

    def select(plainly, reverse, pick, group):
        straight = choose(plainly, pick, 0)
        turned = choose(reverse, pick, 1)
        if group is not None:
            turned = jnp.take_along_axis(turned, flips[group], axis=0, mode="promise_in_bounds")
        return jnp.where(pick[1] >= 4, turned, straight)

    @pl.when(is_row)
    def _():
        arrived(rx_row, row_sem)
        for p in range(k):
            for q in range(3):
                nb_row[tr, p, q] = select(
                    lambda s: rx_row[s, p, q], lambda s: rx_row[s, k - 1 - p, q], row_pick, q
                )
        for w in range(2):

            @pl.when(col_ok[w])
            def _():
                arrived(ry_row.at[w, :, 0:used], row_end_sem.at[w])
                read = lambda s: ry_row[w, s]
                corner[2 * tr + w] = select(read, read, row_pick, None)

    @pl.when(is_col & jnp.logical_not(is_row))
    def _():
        arrived(rx_col, col_sem)
        for q in range(3):
            read = lambda s: rx_col[s, q]
            nb_col[tc, q] = select(read, read, col_pick, q)

    @pl.when(is_col & is_row)
    def _():
        swap = (tr != tc).astype(jnp.int32)
        for q in range(3):

            def read(s, q=q):
                f, t = s // 4, s % 4
                at = 4 * (1 - swap) + t if f == 1 else 4 * swap + t
                return rx_row[at, (tr if f == 0 else 1 - tr) * (k - 1), q]

            nb_col[tc, q] = select(read, read, col_pick, q)

    @pl.when(is_col)
    def _():
        for s in range(2):

            @pl.when(row_ok[s])
            def _():
                arrived(ry_col.at[s, :, 0:used], col_end_sem.at[s])
                read = lambda slot: ry_col[s, slot]
                value = select(read, read, col_pick, None)
                corner[2 * s + tc, 0:2, :] = value[0:2]
                corner[2 * s + tc, 2:4, :] = value[4:6]
                corner[2 * s + tc, 4:6, :] = value[2:4]

    @pl.when(is_row & is_col)
    def _():
        at = 2 * tr + tc
        corner[at, 0:2, :] = jnp.zeros((2, LANES), jnp.float32)
        for q in range(2):
            rows_z = nb_col[tc, 1 + q]
            rows_x = nb_row[tr, tc * (k - 1), 1 + q]
            corner[at, 2 + q : 3 + q, :] = jnp.where(
                tr == 0, rows_z[2 * length : 2 * length + 1], rows_z[2 * length + 1 : 2 * length + 2]
            )
            corner[at, 4 + q : 5 + q, :] = jnp.where(
                tc == 0, rows_x[2 * length : 2 * length + 1], rows_x[2 * length + 1 : 2 * length + 2]
            )

    def zeros(count):
        return [jnp.zeros((count, LANES), jnp.float32)] if count else []

    def stack(lines, total):
        used = sum(x.shape[0] for x in lines)
        return jnp.concatenate(list(lines) + zeros(total - used), axis=0)

    tall_z = round_up(half_r, TILE)
    flat = 2 * length

    class Strip:
        pass

    def strip(read, pieces, ends, total, own):
        def gather(q, at):
            return stack([read(p, q, slice(at, at + length)) for p in range(pieces)], total)

        def sides(first, final):
            lines = []
            for p in range(pieces):
                lines += [first(p)] + zeros(length - 2) + [final(p)]
            return stack(lines, total)

        def lateral(q):
            return sides(
                lambda p: ends[0][q] if p == 0 else read(p - 1, 1 + q, slice(flat + 1, flat + 2)),
                lambda p: ends[1][q]
                if p == pieces - 1
                else read(p + 1, 1 + q, slice(flat, flat + 1)),
            )

        x = Strip()
        x.even, x.odd = gather(0, 0), gather(0, length)
        x.pair = x.even + x.odd
        inv1 = sides(
            lambda p: read(p, 0, slice(flat, flat + 1)),
            lambda p: read(p, 0, slice(flat + 1, flat + 2)),
        )
        x.inv, x.vert = gather(2, 0), gather(2, length)
        x.guess = gather(1, 0) + 0.25 * x.inv * (lateral(0) + own)
        x.inside = gather(1, length) + 0.25 * inv1 * lateral(1)
        return x

    def corner_row(s, w, at):
        return corner[2 * s + w, at : at + 1, :]

    row_strip = []
    for s in range(2):
        own = north[0] if s == 0 else south[half_r - 1]
        ends = [[corner_row(s, w, 2 + q) for q in range(2)] for w in range(2)]
        row_strip.append(
            strip(lambda p, q, rows_: nb_row[s, p, q, rows_, :], k, ends, height, own)
        )
    col_strip = []
    for w in range(2):
        j = w * (half_c - 1)
        faces = west if w == 0 else east
        own = stack([faces[i][j : j + 1] for i in small], tall_z)
        ends = [[corner_row(s, w, 4 + q) for q in range(2)] for s in range(2)]
        col_strip.append(
            strip(lambda p, q, rows_: nb_col[w, q, rows_, :], 1, ends, tall_z, own)
        )

    guess = []
    for i in small:
        lateral = jnp.where(edge_w, col_strip[0].pair[i : i + 1], 0.0)
        lateral = lateral + jnp.where(edge_e, col_strip[1].pair[i : i + 1], 0.0)
        if i == 0:
            lateral = lateral + row_strip[0].pair
        if i == half_r - 1:
            lateral = lateral + row_strip[1].pair
        guess.append(by_tile[i] + 0.25 * c_inv[i] * lateral)

    row_side = [[None] * 2 for _ in range(2)]
    col_side = [[None] * 2 for _ in range(2)]
    for s in range(2):
        for w in range(2):
            faces = nb_row[s, w * (k - 1), 1, flat + w : flat + w + 1, :]
            faces = faces + nb_col[w, 1, flat + s : flat + s + 1, :]
            there = corner_row(s, w, 0) + 0.25 * corner_row(s, w, 1) * faces
            tip = (r == s * (nr - 1)) & (c == w * (nc - 1))
            jr, jc = w * (half_c - 1), s * (half_r - 1)
            row_side[s][w] = jnp.where(tip, col_strip[w].guess[jc : jc + 1], there)
            col_side[w][s] = jnp.where(tip, row_strip[s].guess[jr : jr + 1], there)

    def relax(x, ends, own, count):
        total = x.guess.shape[0]
        at = lax.broadcasted_iota(jnp.int32, (total, LANES), 0)
        around = x.inside + own
        around = around + jnp.where(at == 0, ends[0], pltpu.roll(x.guess, 1, 0))
        around = around + jnp.where(at == count - 1, ends[1], pltpu.roll(x.guess, total - 1, 0))
        column = x.vert * upper(x.guess) + lower(x.vert) * lower(x.guess)
        return (2.0 - relaxation) * x.guess + x.inv * (0.25 * around + column)

    row_fix = [
        relax(row_strip[s], row_side[s], guess[s * (half_r - 1)], half_c) for s in range(2)
    ]
    col_fix = []
    for w in range(2):
        j = w * (half_c - 1)
        own = stack([guess[i][j : j + 1] for i in small], tall_z)
        col_fix.append(relax(col_strip[w], col_side[w], own, half_r))

    def from_left(x, line):
        return jnp.where(edge_w, line, pltpu.roll(x, 1, 0))

    def from_right(x, line):
        return jnp.where(edge_e, line, pltpu.roll(x, height - 1, 0))

    correction = []
    for i in small:
        x = guess[i]
        around = from_left(x, col_strip[0].guess[i : i + 1])
        around = around + from_right(x, col_strip[1].guess[i : i + 1])
        around = around + (guess[i - 1] if i > 0 else row_strip[0].guess)
        around = around + (guess[i + 1] if i < half_r - 1 else row_strip[1].guess)
        levels_part = c_vert[i] * upper(x) + c_low[i] * lower(x)
        correction.append((2.0 - relaxation) * x + c_inv[i] * (0.25 * around + levels_part))
        small_ref[i] = correction[i]

    def outer(y, b):
        at = (y % 2) * length + y // 2
        source = col_strip[b]
        line = (source.even if y % 2 == 0 else source.odd)[y // 2 : y // 2 + 1]
        if b == 0:
            total = partial[y][b] + from_left(smoothed[y][1], line)
        else:
            total = partial[y][b] + from_right(smoothed[y][0], line)
        if y == 0:
            total = total + (row_strip[0].even if b == 0 else row_strip[0].odd)
        if y == rows - 1:
            total = total + (row_strip[1].even if b == 0 else row_strip[1].odd)
        return total

    c_up = [upper(x) for x in correction]
    c_down = [lower(x) for x in correction]
    left = [from_left(correction[i], col_fix[0][i : i + 1]) for i in small]
    right = [from_right(correction[i], col_fix[1][i : i + 1]) for i in small]
    for y in range(rows):
        i = y // 2
        next_i = i - 1 if y % 2 == 0 else i + 1
        for b in range(2):
            total = outer(y, b) + 2.0 * correction[i]
            total = total + vertical[y][b] * c_up[i] + low_vert[y][b] * c_down[i]
            if next_i < 0:
                total = total + row_fix[0]
            elif next_i >= half_r:
                total = total + row_fix[1]
            else:
                total = total + correction[next_i]
            total = total + (left if b == 0 else right)[i]
            first = (2.0 - relaxation) * smoothed[y][b] + (1.0 - relaxation) * correction[i]
            spread[y, pl.ds(b, height, stride=2), :] = first + inverse[y][b] * total


def unpack(spread, small_ref, sol_hbm, corr_hbm, sol, corr, sem):
    panels, _, cols, levels = sol.shape
    half_c = corr.shape[2]
    copies = []
    for p in range(panels):
        lanes = slice(p * levels, (p + 1) * levels)
        sol[p] = spread[:, :cols, lanes]
        copies.append(pltpu.make_async_copy(sol.at[p], sol_hbm.at[p], sem.at[p]))
        copies[-1].start()
    for p in range(panels):
        lanes = slice(p * levels, (p + 1) * levels)
        corr[p] = small_ref[:, :half_c, lanes]
    copies.append(pltpu.make_async_copy(corr, corr_hbm, sem.at[panels]))
    copies[-1].start()
    for copy in copies:
        copy.wait()


def solution(mesh):
    nr, nc = mesh.shape["tx"], mesh.shape["ty"]

    def shards(residual, density, gain, vertical, edge_panel, edge_side, edge_flip):
        panels, rows, cols, levels = residual.shape
        k = cols // rows
        assert cols == k * rows and rows % 2 == 0 and panels * levels <= LANES
        assert rows >= 6 and nr > 1 and nc > 1
        block = round_up(rows + 2, TILE)
        height = round_up(cols // 2, TILE)
        tall = 2 * height
        f32 = jnp.float32
        spread, small = pl.pallas_call(
            functools.partial(kernel, nr, nc),
            out_shape=(
                pltpu.VMEM((rows, tall, LANES), f32),
                pltpu.VMEM((rows // 2, height, LANES), f32),
            ),
            in_specs=[pl.BlockSpec(memory_space=pl.ANY)] * 7,
            out_specs=(pl.BlockSpec(memory_space=pltpu.VMEM),) * 2,
            scratch_shapes=[
                pltpu.VMEM((4, panels, rows, cols, levels), f32),
                pltpu.SMEM((3,) + edge_panel.T.shape, jnp.int32),
                pltpu.VMEM((3, rows, tall, LANES), f32),
                pltpu.VMEM((3, k, 3, block, LANES), f32),
                pltpu.VMEM((3, 3, block, LANES), f32),
                pltpu.VMEM((3, k, 2, TILE, LANES), f32),
                pltpu.VMEM((3, 2, TILE, LANES), f32),
                pltpu.VMEM((3, k, 3, block, LANES), f32),
                pltpu.VMEM((3, 3, block, LANES), f32),
                pltpu.VMEM((5, TILE, LANES), f32),
                pltpu.VMEM((8, k, 3, block, LANES), f32),
                pltpu.VMEM((8, 3, block, LANES), f32),
                pltpu.VMEM((2, 8, TILE, LANES), f32),
                pltpu.VMEM((2, 8, TILE, LANES), f32),
                pltpu.SemaphoreType.DMA((2,)),
                pltpu.SemaphoreType.DMA((3,)),
                pltpu.SemaphoreType.DMA((1,)),
                pltpu.SemaphoreType.DMA((4,)),
                pltpu.SemaphoreType.DMA((4,)),
                pltpu.SemaphoreType.DMA,
                pltpu.SemaphoreType.DMA,
                pltpu.SemaphoreType.DMA((2,)),
                pltpu.SemaphoreType.DMA((2,)),
            ],
            compiler_params=pltpu.CompilerParams(collective_id=0, has_side_effects=True),
        )(residual, density, gain, vertical, edge_panel.T, edge_side.T, edge_flip.T)
        spread = pltpu.with_memory_space_constraint(spread, pltpu.VMEM)
        small = pltpu.with_memory_space_constraint(small, pltpu.VMEM)
        return pl.pallas_call(
            unpack,
            out_shape=(
                jax.ShapeDtypeStruct(residual.shape, f32),
                jax.ShapeDtypeStruct((panels, rows // 2, cols // 2, levels), f32),
            ),
            in_specs=[pl.BlockSpec(memory_space=pltpu.VMEM)] * 2,
            out_specs=(pl.BlockSpec(memory_space=pl.ANY),) * 2,
            scratch_shapes=[
                pltpu.VMEM(residual.shape, f32),
                pltpu.VMEM((panels, rows // 2, cols // 2, levels), f32),
                pltpu.SemaphoreType.DMA((panels + 1,)),
            ],
        )(spread, small)

    fields = P(None, "tx", "ty", None)
    return jax.shard_map(
        shards,
        mesh=mesh,
        in_specs=(fields,) * 4 + (P(),) * 3,
        out_specs=(fields, fields),
        check_vma=False,
    )
```

```python
import functools

import jax
import jax.numpy as jnp
from jax import lax
from jax.experimental import pallas as pl
from jax.experimental.pallas import tpu as pltpu
from jax.sharding import PartitionSpec as P

MESH = pl.DeviceIdType.MESH
relaxation = 0.8
LANES = 128
TILE = 8


def round_up(value, unit):
    return (value + unit - 1) // unit * unit


def kernel(
    nr,
    nc,
    res_hbm,
    den_hbm,
    gain_hbm,
    vert_hbm,
    panel_hbm,
    side_hbm,
    flip_hbm,
    spread,
    small_ref,
    inp,
    tables,
    packed,
    st_row,
    st_col,
    sp_row,
    sp_col,
    ex_row,
    ex_col,
    nb_row,
    nb_col,
    corner,
    rx_row,
    rx_col,
    ry_row,
    ry_col,
    in_sem,
    table_sem,
    send_sem,
    nb_sem,
    corner_sem,
    row_sem,
    col_sem,
    row_end_sem,
    col_end_sem,
):
    _, panels, rows, cols, levels = inp.shape
    half_r, half_c = rows // 2, cols // 2
    k = cols // rows
    length = half_r
    last = length - 1
    height = spread.shape[1] // 2
    block = st_row.shape[3]
    r = lax.axis_index("tx")
    c = lax.axis_index("ty")
    is_row = (r == 0) | (r == nr - 1)
    is_col = (c == 0) | (c == nc - 1)
    tr = (r == nr - 1).astype(jnp.int32)
    tc = (c == nc - 1).astype(jnp.int32)
    row_ok = (r > 0, r < nr - 1)
    col_ok = (c > 0, c < nc - 1)

    def row_segment(f, p):
        return k * c + p if f == 0 else nr - 1 - k * c - p

    def col_segment(f):
        return r if f == 0 else nr - 1 - r

    def clamp(x, n):
        return jnp.minimum(jnp.maximum(x, 0), n - 1)

    used = 6
    full = panels * levels
    spare = LANES - full
    packed_rows = 3 * rows

    def traffic(sending):
        def remote(src, dst, sem, dest):
            if sending:
                pltpu.make_async_remote_copy(
                    src_ref=src,
                    dst_ref=dst,
                    send_sem=send_sem.at[0],
                    recv_sem=sem,
                    device_id=dest,
                    device_id_type=MESH,
                ).start()
            else:
                pltpu.make_async_copy(src, src, send_sem.at[0]).wait()

        def local(src, dst, sem):
            if sending:
                pltpu.make_async_copy(src, dst, sem).start()

        def either(src, dst, sem, dest, mine):
            @pl.when(jnp.logical_not(mine))
            def _():
                remote(src, dst, sem, dest)

            @pl.when(mine)
            def _():
                local(src, dst, sem)

        def at_row(e):
            return r == e * (nr - 1)

        def at_col(e):
            return c == e * (nc - 1)

        def strips_to_rows(e):
            row = e * (nr - 1)

            @pl.when(is_row)
            def _():
                src = sp_row.at[tr, :, 0:packed_rows]
                to = jnp.minimum(c, nc - 1 - c)
                f = (c > to).astype(jnp.int32)
                for to, f in ((to, f), (nc - 1 - to, 1 - f)):
                    either(src, rx_row.at[4 * f + tr, :, 0:packed_rows], row_sem, (row, to), at_row(e) & (to == c))

            @pl.when(is_col)
            def _():
                g = jnp.minimum(r, nr - 1 - r)
                f = (r > g).astype(jnp.int32)
                for g, f in ((g, f), (nr - 1 - g, 1 - f)):
                    dst = rx_row.at[4 * f + 2 + tc, lax.rem(r, k), 0:packed_rows]
                    to = lax.div(g, k)
                    either(sp_col.at[tc, 0:packed_rows], dst, row_sem, (row, to), at_row(e) & (to == c))

        def strips_to_columns(e):
            col = e * (nc - 1)

            @pl.when(is_row)
            def _():
                for p in range(k):
                    extreme = (c == 0) if p == 0 else (c == nc - 1)
                    if k == 1:
                        extreme = extreme | (c == nc - 1)

                    def to_columns(p=p):
                        for f in (1, 0):
                            to = row_segment(f, p)
                            remote(st_row.at[tr, p], rx_col.at[4 * f + tr], col_sem, (to, col))

                    if 0 < p < k - 1:
                        to_columns()
                    else:
                        pl.when(jnp.logical_not(extreme))(to_columns)

            @pl.when(is_col & jnp.logical_not(is_row))
            def _():
                src = st_col.at[tc]
                remote(src, rx_col.at[6 + tc], col_sem, (nr - 1 - r, col))
                either(src, rx_col.at[2 + tc], col_sem, (r, col), at_col(e))

        def ends(e):
            row, col = e * (nr - 1), e * (nc - 1)
            for f in (1, 0):
                for h in range(2):
                    d = 1 if h != f else -1
                    end = 0 if d == 1 else 1

                    @pl.when(is_row)
                    def _():
                        slot = 4 * f + tr
                        for p in range(k):
                            outer_end = p == (k - 1 if h == 1 else 0)

                            def one_end(p=p, outer_end=outer_end):
                                src = ex_row.at[tr, p, h, 0:used]
                                if outer_end:
                                    to = clamp((c if f == 0 else nc - 1 - c) + d, nc)
                                    dst = ry_row.at[end, slot, 0:used]
                                    sem = row_end_sem.at[end]
                                    if f == 0:
                                        remote(src, dst, sem, (row, to))
                                    else:
                                        either(src, dst, sem, (row, to), at_row(e) & (to == c))
                                to = clamp(row_segment(f, p) + d, nr)
                                dst = ry_col.at[end, slot, 0:used]
                                sem = col_end_sem.at[end]
                                either(src, dst, sem, (to, col), at_col(e) & (to == r))

                            if outer_end:
                                pl.when(col_ok[h])(one_end)
                            else:
                                one_end()

                    @pl.when(is_col & row_ok[h])
                    def _():
                        slot = 4 * f + 2 + tc
                        src = ex_col.at[tc, h, 0:used]
                        g = col_segment(f)

                        def crossing():
                            to = clamp(lax.div(g, k) + d, nc)
                            dst = ry_row.at[end, slot, 0:used]
                            sem = row_end_sem.at[end]
                            either(src, dst, sem, (row, to), at_row(e) & (to == c))

                        if k == 1:
                            crossing()
                        else:
                            pl.when(lax.rem(g, k) == (k - 1 if d == 1 else 0))(crossing)
                        to = clamp(g + d, nr)
                        dst = ry_col.at[end, slot, 0:used]
                        sem = col_end_sem.at[end]
                        if f == 0:
                            remote(src, dst, sem, (to, col))
                        else:
                            either(src, dst, sem, (to, col), at_col(e) & (to == r))

        def within(s):
            @pl.when(row_ok[s])
            def _():
                remote(st_row.at[s], nb_row.at[1 - s], nb_sem.at[1 - s], (r + 2 * s - 1, c))

            @pl.when(col_ok[s])
            def _():
                remote(st_col.at[s], nb_col.at[1 - s], nb_sem.at[3 - s], (r, c + 2 * s - 1))

            for w in range(2):
                at = 2 * (1 - s) + 1 - w

                @pl.when(row_ok[s] & col_ok[w])
                def _():
                    remote(
                        ex_row.at[s, w * (k - 1), w, 0:used],
                        corner.at[at, 0:used],
                        corner_sem.at[at],
                        (r + 2 * s - 1, c + 2 * w - 1),
                    )

        strips_to_rows(0)
        if sending:
            stage_ends()
        within(0)
        ends(0)
        strips_to_rows(1)
        strips_to_columns(0)
        strips_to_columns(1)
        ends(1)
        within(1)

    fields = (gain_hbm, vert_hbm, den_hbm, res_hbm)
    for pair in range(2):
        for p in range(panels):
            for i in (2 * pair, 2 * pair + 1):
                pltpu.make_async_copy(fields[i].at[p], inp.at[i, p], in_sem.at[pair]).start()
    table_loads = [
        pltpu.make_async_copy(source, tables.at[i], table_sem.at[0])
        for i, source in enumerate((panel_hbm, side_hbm, flip_hbm))
    ]
    for load in table_loads:
        load.start()

    barrier = pltpu.get_barrier_semaphore()
    far_r, near_r = (1 - tr) * (nr - 1), tr * (nr - 1)
    far_c, near_c = (1 - tc) * (nc - 1), tc * (nc - 1)

    def greet(dest):
        pl.semaphore_signal(barrier, inc=1, device_id=dest, device_id_type=MESH)

    def number(flag):
        return flag.astype(jnp.int32)

    def row_greetings():
        found = []
        for near in (False, True):
            for f in (1, 0):
                here = c if f == 0 else nc - 1 - c
                for d in (0, -1, 1):
                    if near and f == 0 and d == 0:
                        continue
                    ok = None if d == 0 else (here > 0) if d == -1 else (here < nc - 1)
                    mine = (here + d == c) if near and f == 1 and d else None
                    found.append((ok, mine, (near_r if near else far_r, clamp(here + d, nc))))
        for near in (False, True):
            for f in (1, 0):
                low = row_segment(f, 0 if f == 0 else k - 1)
                for d in range(-1, k + 1):
                    ok = None if 0 <= d < k else (low > 0) if d == -1 else (low + d < nr)
                    mine = (is_col & (low + d == r)) if near else None
                    found.append((ok, mine, (clamp(low + d, nr), near_c if near else far_c)))
        return found

    def col_greetings():
        found = []
        for near in (False, True):
            for f in (1, 0):
                g = col_segment(f)
                for d in (0, -1, 1):
                    inside = None if d == 0 else (g > 0) if d == -1 else (g < nr - 1)
                    if not (near and f == 0 and d == 0):
                        mine = (g + d == r) if near and f == 1 and d else None
                        found.append((inside, mine, (clamp(g + d, nr), near_c if near else far_c)))
                    cross = inside
                    if d and k > 1:
                        cross = inside & (lax.rem(g, k) == (k - 1 if d == 1 else 0))
                    to = lax.div(g, k) + d
                    mine = (is_row & (to == c)) if near else None
                    found.append((cross, mine, (near_r if near else far_r, clamp(to, nc))))
        return found

    def near_greetings():
        found = []
        for dr in (-1, 0, 1):
            for dc in (-1, 0, 1):
                if dr or dc:
                    ok = row_ok[(dr + 1) // 2] if dr else None
                    if dc:
                        side = col_ok[(dc + 1) // 2]
                        ok = side if ok is None else ok & side
                    found.append((ok, None, (r + dr, c + dc)))
        return found

    def announce(found):
        total = jnp.int32(0)
        for ok, mine, dest in found:
            go = ok
            if mine is not None:
                go = jnp.logical_not(mine) if go is None else go & jnp.logical_not(mine)
            if go is None:
                total = total + 1
            else:
                total = total + number(go)
        return total

    def tell(found):
        for ok, mine, dest in found:
            go = ok
            if mine is not None:
                go = jnp.logical_not(mine) if go is None else go & jnp.logical_not(mine)
            if go is None:
                greet(dest)
            else:
                pl.when(go)(functools.partial(greet, dest))

    pl.when(is_row)(lambda: tell(row_greetings()))
    pl.when(is_col)(lambda: tell(col_greetings()))
    tell(near_greetings())
    expected = announce(near_greetings())
    expected = expected + jnp.where(is_row, announce(row_greetings()), 0)
    expected = expected + jnp.where(is_col, announce(col_greetings()), 0)

    lane = lax.broadcasted_iota(jnp.int32, (TILE, LANES), 1)
    sub = lax.broadcasted_iota(jnp.int32, (height, LANES), 0)
    level = lane[:1] % levels
    first_level = level == 0
    last_level = level == levels - 1

    def lower(x):
        return jnp.where(first_level, 0.0, pltpu.roll(x, 1, 1))

    def upper(x):
        return jnp.where(last_level, 0.0, pltpu.roll(x, LANES - 1, 1))

    def pick_tables(side):
        index = lane
        code = jnp.zeros_like(lane)
        for p in range(panels):
            here = lane // levels == p
            index = jnp.where(here, tables[0, side, p] * levels + lane % levels, index)
            code = jnp.where(here, tables[2, side, p] * 4 + tables[1, side, p], code)
        chunk = index // spare
        return index, code, jnp.where(lane < full, full + index - chunk * spare, lane), chunk

    def pack(value):
        filler = jnp.zeros((rows, cols, LANES - panels * levels), jnp.float32)
        return jnp.concatenate([value[p] for p in range(panels)] + [filler], axis=-1)

    def split(which, value):
        packed[which, :, :cols, :] = value
        if packed.shape[2] > cols:
            packed[which, :, cols:, :] = jnp.zeros(
                (rows, packed.shape[2] - cols, LANES), jnp.float32
            )
        return [
            [packed[which, y, pl.ds(b, height, stride=2), :] for b in range(2)]
            for y in range(rows)
        ]

    def fine(fun):
        return [[fun(y, b) for b in range(2)] for y in range(rows)]

    small = range(half_r)

    def block_mean(values, i):
        y = 2 * i
        return 0.25 * (values[y][0] + values[y][1] + values[y + 1][0] + values[y + 1][1])

    pltpu.make_async_copy(inp.at[0:2], inp.at[0:2], in_sem.at[0]).wait()
    gain = split(1, pack(inp[0]))
    vertical = split(2, pack(inp[1]))
    low_vert = fine(lambda y, b: lower(vertical[y][b]))
    inverse = fine(
        lambda y, b: relaxation / (gain[y][b] + 4.0 + vertical[y][b] + low_vert[y][b])
    )
    c_vert = [block_mean(vertical, i) for i in small]
    c_low = [lower(c_vert[i]) for i in small]
    c_inv = [relaxation / (block_mean(gain, i) + 1.0 + c_vert[i] + c_low[i]) for i in small]
    pltpu.make_async_copy(inp.at[2:4], inp.at[2:4], in_sem.at[1]).wait()
    right_side = split(0, pack(inp[2] * inp[3]))
    smoothed = fine(lambda y, b: inverse[y][b] * right_side[y][b])

    def inner(y, b):
        x = smoothed[y][b]
        return vertical[y][b] * upper(x) + low_vert[y][b] * lower(x)

    coupled = fine(inner)
    column = fine(lambda y, b: coupled[y][b] + (1.0 - relaxation) * right_side[y][b])
    north = [smoothed[2 * i][0] + smoothed[2 * i][1] for i in small]
    south = [smoothed[2 * i + 1][0] + smoothed[2 * i + 1][1] for i in small]
    west = [smoothed[2 * i][0] + smoothed[2 * i + 1][0] for i in small]
    east = [smoothed[2 * i][1] + smoothed[2 * i + 1][1] for i in small]
    from_w = [pltpu.roll(east[i], 1, 0) for i in small]
    from_e = [pltpu.roll(west[i], height - 1, 0) for i in small]
    start_w = sub % length == 0
    start_e = sub % length == last
    edge_w = sub == 0
    edge_e = sub == half_c - 1

    def bare(i):
        total = block_mean(column, i) + 0.5 * (north[i] + south[i])
        beside = None
        if i > 0:
            beside = south[i - 1]
        if i < half_r - 1:
            beside = north[i + 1] if beside is None else beside + north[i + 1]
        return total if beside is None else total + 0.25 * beside

    plain = [bare(i) for i in small]

    def partial_guess(i, mask_w, mask_e):
        beside = jnp.where(mask_w, 0.0, from_w[i]) + jnp.where(mask_e, 0.0, from_e[i])
        return c_inv[i] * (plain[i] + 0.25 * beside)

    by_tile = [partial_guess(i, edge_w, edge_e) for i in small]
    by_piece = by_tile if k == 1 else [partial_guess(i, start_w, start_e) for i in small]

    def put(ref, at, value):
        ref[at : at + value.shape[0], :] = value

    def press(ref, runs, singles):
        for at, run in enumerate(runs):
            put(ref, at * length, run)
        singles = jnp.concatenate(singles + [jnp.zeros((TILE - used, LANES), jnp.float32)], axis=0)
        for j in range(full // spare):
            moved = pltpu.roll(singles, full - spare * j, 1)
            ref[used * j : used * (j + 1), full:] = moved[:used, full:]

    for s in range(2):
        y = s * (rows - 1)
        i0, i1 = (0, 1) if s == 0 else (half_r - 1, half_r - 2)
        out = north[0] if s == 0 else south[half_r - 1]
        for p in range(k):
            lo, hi = p * length, p * length + last
            seg = slice(lo, hi + 1)
            one = lambda x, j: x[j : j + 1]
            a, b, g = (st_row.at[s, p, q] for q in range(3))
            put(a, 0, smoothed[y][0][seg])
            put(a, length, smoothed[y][1][seg])
            put(a, 2 * length, one(c_inv[i1], lo))
            put(a, 2 * length + 1, one(c_inv[i1], hi))
            put(b, 0, by_piece[i0][seg])
            put(b, length, by_piece[i1][seg])
            put(b, 2 * length, one(west[i0], lo))
            put(b, 2 * length + 1, one(east[i0], hi))
            put(g, 0, c_inv[i0][seg])
            put(g, length, c_vert[i0][seg])
            put(g, 2 * length, one(west[i1], lo))
            put(g, 2 * length + 1, one(east[i1], hi))
            parts = (smoothed[y][0], smoothed[y][1], by_piece[i0], by_piece[i1])
            press(
                sp_row.at[s, p],
                [x[seg] for x in parts + (c_inv[i0], c_vert[i0])],
                [one(c_inv[i1], lo), one(c_inv[i1], hi)]
                + [one(west[i0], lo), one(east[i0], hi), one(west[i1], lo), one(east[i1], hi)],
            )
    for s in range(2):
        j0, j1 = (0, 1) if s == 0 else (half_c - 1, half_c - 2)
        out = west if s == 0 else east
        a, b, g = (st_col.at[s, q] for q in range(3))
        at0 = lambda x: x[j0 : j0 + 1]
        at1 = lambda x: x[j1 : j1 + 1]
        for y in range(rows):
            put(a, (y % 2) * length + y // 2, at0(smoothed[y][s]))
        put(a, 2 * length, at1(c_inv[0]))
        put(a, 2 * length + 1, at1(c_inv[half_r - 1]))
        for i in small:
            put(b, i, at0(by_tile[i]))
            put(b, length + i, at1(by_tile[i]))
            put(g, i, at0(c_inv[i]))
            put(g, length + i, at0(c_vert[i]))
        put(b, 2 * length, at0(north[0]))
        put(b, 2 * length + 1, at0(south[half_r - 1]))
        put(g, 2 * length, at1(north[0]))
        put(g, 2 * length + 1, at1(south[half_r - 1]))
        parts = [
            [at0(smoothed[2 * i][s]) for i in small],
            [at0(smoothed[2 * i + 1][s]) for i in small],
            [at0(x) for x in by_tile],
            [at1(x) for x in by_tile],
            [at0(x) for x in c_inv],
            [at0(x) for x in c_vert],
        ]
        press(
            sp_col.at[s],
            [jnp.concatenate(x, axis=0) for x in parts],
            [at1(c_inv[0]), at1(c_inv[half_r - 1]), at0(north[0]), at0(south[half_r - 1])]
            + [at1(north[0]), at1(south[half_r - 1])],
        )

    def stage_ends():
        for s in range(2):
            i0, i1 = (0, 1) if s == 0 else (half_r - 1, half_r - 2)
            out = north[0] if s == 0 else south[half_r - 1]
            for p in range(k):
                lo, hi = p * length, p * length + last
                one = lambda x, j: x[j : j + 1]
                for h in range(2):
                    j, j1 = (lo, lo + 1) if h == 0 else (hi, hi - 1)
                    side = west if h == 0 else east
                    x = ex_row.at[s, p, h]
                    put(x, 0, one(by_piece[i0], j))
                    put(x, 1, one(c_inv[i0], j))
                    put(x, 2, one(side[i0], j))
                    put(x, 3, one(side[i1], j))
                    put(x, 4, one(out, j))
                    put(x, 5, one(out, j1))
        for s in range(2):
            j0, j1 = (0, 1) if s == 0 else (half_c - 1, half_c - 2)
            out = west if s == 0 else east
            at0 = lambda x: x[j0 : j0 + 1]
            at1 = lambda x: x[j1 : j1 + 1]
            for h in range(2):
                i0, i1 = (0, 1) if h == 0 else (half_r - 1, half_r - 2)
                side = north[0] if h == 0 else south[half_r - 1]
                x = ex_col.at[s, h]
                put(x, 0, at0(by_tile[i0]))
                put(x, 1, at0(c_inv[i0]))
                put(x, 2, at0(side))
                put(x, 3, at1(side))
                put(x, 4, at0(out[i0]))
                put(x, 5, at0(out[i1]))

    pl.semaphore_wait(barrier, expected)
    traffic(True)

    def beside(y, b):
        x = smoothed[y][b]
        total = coupled[y][b] + smoothed[y][1 - b]
        if y > 0:
            total = total + smoothed[y - 1][b]
        if y < rows - 1:
            total = total + smoothed[y + 1][b]
        return total

    partial = fine(beside)
    traffic(False)

    pltpu.make_async_copy(tables, tables, table_sem.at[0]).wait()
    row_pick = pick_tables(tr)
    col_pick = pick_tables(2 + tc)

    def arrived(ref, sem):
        pltpu.make_async_copy(ref, ref, sem).wait()

    for s in range(2):

        @pl.when(row_ok[s])
        def _():
            arrived(nb_row.at[s], nb_sem.at[s])

        @pl.when(col_ok[s])
        def _():
            arrived(nb_col.at[s], nb_sem.at[2 + s])

        for w in range(2):

            @pl.when(row_ok[s] & col_ok[w])
            def _():
                arrived(corner.at[2 * s + w, 0:used], corner_sem.at[2 * s + w])

    order = list(range(2 * length))[::-1] + [2 * length + 1, 2 * length]
    other = (
        list(range(length))[::-1]
        + list(range(length, 2 * length))[::-1]
        + [2 * length + 1, 2 * length]
    )
    sublane = lax.broadcasted_iota(jnp.int32, (block, LANES), 0)

    def flip_index(perm):
        index = sublane
        for at, source in enumerate(perm):
            index = jnp.where(sublane == at, source, index)
        return index

    flips = [flip_index(order), flip_index(other), flip_index(other)]

    def choose(read, pick, f, second=False):
        index, code = pick[2 if second else 0], pick[1]
        taken = None
        for t in range(4):
            moved = jnp.take_along_axis(read(4 * f + t), index, axis=1, mode="promise_in_bounds")
            taken = moved if taken is None else jnp.where(code == 4 * f + t, moved, taken)
        return taken

    def select(plainly, reverse, pick, group):
        straight = choose(plainly, pick, 0)
        turned = choose(reverse, pick, 1)
        if group is not None:
            turned = jnp.take_along_axis(turned, flips[group], axis=0, mode="promise_in_bounds")
        return jnp.where(pick[1] >= 4, turned, straight)

    def rows_of(tiles, first, final):
        parts = []
        for q, tile in enumerate(tiles):
            lo, hi = max(first, q * TILE), min(final, (q + 1) * TILE)
            if lo < hi:
                parts.append(tile[lo - q * TILE : hi - q * TILE])
        return parts

    def select_packed(plainly, reverse, pick):
        tiles = range(-(-packed_rows // TILE))
        results = []
        for f, read in ((0, plainly), (1, reverse)):
            main = [choose(lambda s: read(s, q), pick, f) for q in tiles]
            extra = [choose(lambda s: read(s, q), pick, f, True) for q in tiles]
            singles = None
            for j in range(full // spare):
                part = jnp.concatenate(rows_of(extra, used * j, used * (j + 1)), axis=0)
                same = pick[3][:used] == j
                singles = part if singles is None else jnp.where(same, part, singles)
            groups = []
            for q in range(3):
                lines = rows_of(main, 2 * length * q, 2 * length * (q + 1))
                lines.append(singles[2 * q : 2 * q + 2])
                if block > 2 * length + 2:
                    lines.append(jnp.zeros((block - 2 * length - 2, LANES), jnp.float32))
                groups.append(jnp.concatenate(lines, axis=0))
            results.append(groups)
        turned = [
            jnp.take_along_axis(x, flips[q], axis=0, mode="promise_in_bounds")
            for q, x in enumerate(results[1])
        ]
        return [jnp.where(pick[1] >= 4, x, y) for x, y in zip(turned, results[0])]

    @pl.when(is_row)
    def _():
        arrived(rx_row.at[:, :, 0:packed_rows], row_sem)
        for p in range(k):
            value = select_packed(
                lambda s, q: rx_row[s, p, q * TILE : (q + 1) * TILE],
                lambda s, q: rx_row[s, k - 1 - p, q * TILE : (q + 1) * TILE],
                row_pick,
            )
            for q in range(3):
                nb_row[tr, p, q] = value[q]
        for w in range(2):

            @pl.when(col_ok[w])
            def _():
                arrived(ry_row.at[w, :, 0:used], row_end_sem.at[w])
                read = lambda s: ry_row[w, s]
                corner[2 * tr + w] = select(read, read, row_pick, None)

    @pl.when(is_col & jnp.logical_not(is_row))
    def _():
        arrived(rx_col, col_sem)
        for q in range(3):
            read = lambda s: rx_col[s, q]
            nb_col[tc, q] = select(read, read, col_pick, q)

    @pl.when(is_col & is_row)
    def _():
        swap = (tr != tc).astype(jnp.int32)

        def read(s, q):
            f, t = s // 4, s % 4
            at = 4 * (1 - swap) + t if f == 1 else 4 * swap + t
            piece = (tr if f == 0 else 1 - tr) * (k - 1)
            return rx_row[at, piece, q * TILE : (q + 1) * TILE]

        value = select_packed(read, read, col_pick)
        for q in range(3):
            nb_col[tc, q] = value[q]

    @pl.when(is_col)
    def _():
        for s in range(2):

            @pl.when(row_ok[s])
            def _():
                arrived(ry_col.at[s, :, 0:used], col_end_sem.at[s])
                read = lambda slot: ry_col[s, slot]
                value = select(read, read, col_pick, None)
                corner[2 * s + tc, 0:2, :] = value[0:2]
                corner[2 * s + tc, 2:4, :] = value[4:6]
                corner[2 * s + tc, 4:6, :] = value[2:4]

    @pl.when(is_row & is_col)
    def _():
        at = 2 * tr + tc
        corner[at, 0:2, :] = jnp.zeros((2, LANES), jnp.float32)
        for q in range(2):
            rows_z = nb_col[tc, 1 + q]
            rows_x = nb_row[tr, tc * (k - 1), 1 + q]
            corner[at, 2 + q : 3 + q, :] = jnp.where(
                tr == 0, rows_z[2 * length : 2 * length + 1], rows_z[2 * length + 1 : 2 * length + 2]
            )
            corner[at, 4 + q : 5 + q, :] = jnp.where(
                tc == 0, rows_x[2 * length : 2 * length + 1], rows_x[2 * length + 1 : 2 * length + 2]
            )

    def zeros(count):
        return [jnp.zeros((count, LANES), jnp.float32)] if count else []

    def stack(lines, total):
        used = sum(x.shape[0] for x in lines)
        return jnp.concatenate(list(lines) + zeros(total - used), axis=0)

    tall_z = round_up(half_r, TILE)
    flat = 2 * length

    class Strip:
        pass

    def strip(read, pieces, ends, total, own):
        def gather(q, at):
            return stack([read(p, q, slice(at, at + length)) for p in range(pieces)], total)

        def sides(first, final):
            lines = []
            for p in range(pieces):
                lines += [first(p)] + zeros(length - 2) + [final(p)]
            return stack(lines, total)

        def lateral(q):
            return sides(
                lambda p: ends[0][q] if p == 0 else read(p - 1, 1 + q, slice(flat + 1, flat + 2)),
                lambda p: ends[1][q]
                if p == pieces - 1
                else read(p + 1, 1 + q, slice(flat, flat + 1)),
            )

        x = Strip()
        x.even, x.odd = gather(0, 0), gather(0, length)
        x.pair = x.even + x.odd
        inv1 = sides(
            lambda p: read(p, 0, slice(flat, flat + 1)),
            lambda p: read(p, 0, slice(flat + 1, flat + 2)),
        )
        x.inv, x.vert = gather(2, 0), gather(2, length)
        x.guess = gather(1, 0) + 0.25 * x.inv * (lateral(0) + own)
        x.inside = gather(1, length) + 0.25 * inv1 * lateral(1)
        return x

    def corner_row(s, w, at):
        return corner[2 * s + w, at : at + 1, :]

    row_strip = []
    for s in range(2):
        own = north[0] if s == 0 else south[half_r - 1]
        ends = [[corner_row(s, w, 2 + q) for q in range(2)] for w in range(2)]
        row_strip.append(
            strip(lambda p, q, rows_: nb_row[s, p, q, rows_, :], k, ends, height, own)
        )
    col_strip = []
    for w in range(2):
        j = w * (half_c - 1)
        faces = west if w == 0 else east
        own = stack([faces[i][j : j + 1] for i in small], tall_z)
        ends = [[corner_row(s, w, 4 + q) for q in range(2)] for s in range(2)]
        col_strip.append(
            strip(lambda p, q, rows_: nb_col[w, q, rows_, :], 1, ends, tall_z, own)
        )

    guess = []
    for i in small:
        lateral = jnp.where(edge_w, col_strip[0].pair[i : i + 1], 0.0)
        lateral = lateral + jnp.where(edge_e, col_strip[1].pair[i : i + 1], 0.0)
        if i == 0:
            lateral = lateral + row_strip[0].pair
        if i == half_r - 1:
            lateral = lateral + row_strip[1].pair
        guess.append(by_tile[i] + 0.25 * c_inv[i] * lateral)

    row_side = [[None] * 2 for _ in range(2)]
    col_side = [[None] * 2 for _ in range(2)]
    for s in range(2):
        for w in range(2):
            faces = nb_row[s, w * (k - 1), 1, flat + w : flat + w + 1, :]
            faces = faces + nb_col[w, 1, flat + s : flat + s + 1, :]
            there = corner_row(s, w, 0) + 0.25 * corner_row(s, w, 1) * faces
            tip = (r == s * (nr - 1)) & (c == w * (nc - 1))
            jr, jc = w * (half_c - 1), s * (half_r - 1)
            row_side[s][w] = jnp.where(tip, col_strip[w].guess[jc : jc + 1], there)
            col_side[w][s] = jnp.where(tip, row_strip[s].guess[jr : jr + 1], there)

    def relax(x, ends, own, count):
        total = x.guess.shape[0]
        at = lax.broadcasted_iota(jnp.int32, (total, LANES), 0)
        around = x.inside + own
        around = around + jnp.where(at == 0, ends[0], pltpu.roll(x.guess, 1, 0))
        around = around + jnp.where(at == count - 1, ends[1], pltpu.roll(x.guess, total - 1, 0))
        column = x.vert * upper(x.guess) + lower(x.vert) * lower(x.guess)
        return (2.0 - relaxation) * x.guess + x.inv * (0.25 * around + column)

    row_fix = [
        relax(row_strip[s], row_side[s], guess[s * (half_r - 1)], half_c) for s in range(2)
    ]
    col_fix = []
    for w in range(2):
        j = w * (half_c - 1)
        own = stack([guess[i][j : j + 1] for i in small], tall_z)
        col_fix.append(relax(col_strip[w], col_side[w], own, half_r))

    def from_left(x, line):
        return jnp.where(edge_w, line, pltpu.roll(x, 1, 0))

    def from_right(x, line):
        return jnp.where(edge_e, line, pltpu.roll(x, height - 1, 0))

    correction = []
    for i in small:
        x = guess[i]
        around = from_left(x, col_strip[0].guess[i : i + 1])
        around = around + from_right(x, col_strip[1].guess[i : i + 1])
        around = around + (guess[i - 1] if i > 0 else row_strip[0].guess)
        around = around + (guess[i + 1] if i < half_r - 1 else row_strip[1].guess)
        levels_part = c_vert[i] * upper(x) + c_low[i] * lower(x)
        correction.append((2.0 - relaxation) * x + c_inv[i] * (0.25 * around + levels_part))
        small_ref[i] = correction[i]

    def outer(y, b):
        at = (y % 2) * length + y // 2
        source = col_strip[b]
        line = (source.even if y % 2 == 0 else source.odd)[y // 2 : y // 2 + 1]
        if b == 0:
            total = partial[y][b] + from_left(smoothed[y][1], line)
        else:
            total = partial[y][b] + from_right(smoothed[y][0], line)
        if y == 0:
            total = total + (row_strip[0].even if b == 0 else row_strip[0].odd)
        if y == rows - 1:
            total = total + (row_strip[1].even if b == 0 else row_strip[1].odd)
        return total

    c_up = [upper(x) for x in correction]
    c_down = [lower(x) for x in correction]
    left = [from_left(correction[i], col_fix[0][i : i + 1]) for i in small]
    right = [from_right(correction[i], col_fix[1][i : i + 1]) for i in small]
    for y in range(rows):
        i = y // 2
        next_i = i - 1 if y % 2 == 0 else i + 1
        for b in range(2):
            total = outer(y, b) + 2.0 * correction[i]
            total = total + vertical[y][b] * c_up[i] + low_vert[y][b] * c_down[i]
            if next_i < 0:
                total = total + row_fix[0]
            elif next_i >= half_r:
                total = total + row_fix[1]
            else:
                total = total + correction[next_i]
            total = total + (left if b == 0 else right)[i]
            first = (2.0 - relaxation) * smoothed[y][b] + (1.0 - relaxation) * correction[i]
            spread[y, pl.ds(b, height, stride=2), :] = first + inverse[y][b] * total


def unpack(spread, small_ref, sol_hbm, corr_hbm, sol, corr, sem):
    panels, _, cols, levels = sol.shape
    half_c = corr.shape[2]
    for p in range(panels):
        lanes = slice(p * levels, (p + 1) * levels)
        sol[p] = spread[:, :cols, lanes]
        pltpu.make_async_copy(sol.at[p], sol_hbm.at[p], sem.at[0]).start()
    for p in range(panels):
        lanes = slice(p * levels, (p + 1) * levels)
        corr[p] = small_ref[:, :half_c, lanes]
    last = pltpu.make_async_copy(corr, corr_hbm, sem.at[1])
    last.start()
    pltpu.make_async_copy(sol, sol_hbm, sem.at[0]).wait()
    last.wait()


def solution(mesh):
    nr, nc = mesh.shape["tx"], mesh.shape["ty"]

    def shards(residual, density, gain, vertical, edge_panel, edge_side, edge_flip):
        panels, rows, cols, levels = residual.shape
        k = cols // rows
        assert cols == k * rows and rows % 2 == 0 and panels * levels <= LANES
        assert rows >= 6 and nr > 1 and nc > 1
        block = round_up(rows + 2, TILE)
        dense = round_up(3 * rows, TILE)
        spare = LANES - panels * levels
        assert spare % levels == 0 and panels * levels % spare == 0
        assert 2 * panels * levels <= rows * spare
        height = round_up(cols // 2, TILE)
        tall = 2 * height
        f32 = jnp.float32
        spread, small = pl.pallas_call(
            functools.partial(kernel, nr, nc),
            out_shape=(
                pltpu.VMEM((rows, tall, LANES), f32),
                pltpu.VMEM((rows // 2, height, LANES), f32),
            ),
            in_specs=[pl.BlockSpec(memory_space=pl.ANY)] * 7,
            out_specs=(pl.BlockSpec(memory_space=pltpu.VMEM),) * 2,
            scratch_shapes=[
                pltpu.VMEM((4, panels, rows, cols, levels), f32),
                pltpu.SMEM((3,) + edge_panel.T.shape, jnp.int32),
                pltpu.VMEM((3, rows, tall, LANES), f32),
                pltpu.VMEM((3, k, 3, block, LANES), f32),
                pltpu.VMEM((3, 3, block, LANES), f32),
                pltpu.VMEM((3, k, dense, LANES), f32),
                pltpu.VMEM((3, dense, LANES), f32),
                pltpu.VMEM((3, k, 2, TILE, LANES), f32),
                pltpu.VMEM((3, 2, TILE, LANES), f32),
                pltpu.VMEM((3, k, 3, block, LANES), f32),
                pltpu.VMEM((3, 3, block, LANES), f32),
                pltpu.VMEM((5, TILE, LANES), f32),
                pltpu.VMEM((8, k, dense, LANES), f32),
                pltpu.VMEM((8, 3, block, LANES), f32),
                pltpu.VMEM((2, 8, TILE, LANES), f32),
                pltpu.VMEM((2, 8, TILE, LANES), f32),
                pltpu.SemaphoreType.DMA((2,)),
                pltpu.SemaphoreType.DMA((1,)),
                pltpu.SemaphoreType.DMA((1,)),
                pltpu.SemaphoreType.DMA((4,)),
                pltpu.SemaphoreType.DMA((4,)),
                pltpu.SemaphoreType.DMA,
                pltpu.SemaphoreType.DMA,
                pltpu.SemaphoreType.DMA((2,)),
                pltpu.SemaphoreType.DMA((2,)),
            ],
            compiler_params=pltpu.CompilerParams(collective_id=0, has_side_effects=True),
        )(residual, density, gain, vertical, edge_panel.T, edge_side.T, edge_flip.T)
        spread = pltpu.with_memory_space_constraint(spread, pltpu.VMEM)
        small = pltpu.with_memory_space_constraint(small, pltpu.VMEM)
        return pl.pallas_call(
            unpack,
            out_shape=(
                jax.ShapeDtypeStruct(residual.shape, f32),
                jax.ShapeDtypeStruct((panels, rows // 2, cols // 2, levels), f32),
            ),
            in_specs=[pl.BlockSpec(memory_space=pltpu.VMEM)] * 2,
            out_specs=(pl.BlockSpec(memory_space=pl.ANY),) * 2,
            scratch_shapes=[
                pltpu.VMEM(residual.shape, f32),
                pltpu.VMEM((panels, rows // 2, cols // 2, levels), f32),
                pltpu.SemaphoreType.DMA((2,)),
            ],
        )(spread, small)

    fields = P(None, "tx", "ty", None)
    return jax.shard_map(
        shards,
        mesh=mesh,
        in_specs=(fields,) * 4 + (P(),) * 3,
        out_specs=(fields, fields),
        check_vma=False,
    )
```

```python
import functools

import jax
import jax.numpy as jnp
from jax import lax
from jax.experimental import pallas as pl
from jax.experimental.pallas import tpu as pltpu
from jax.sharding import PartitionSpec as P

MESH = pl.DeviceIdType.MESH
relaxation = 0.8
LANES = 128
TILE = 8


def round_up(value, unit):
    return (value + unit - 1) // unit * unit


def kernel(
    nr,
    nc,
    res_hbm,
    den_hbm,
    gain_hbm,
    vert_hbm,
    panel_hbm,
    side_hbm,
    flip_hbm,
    spread,
    small_ref,
    inp,
    tables,
    packed,
    st_row,
    st_col,
    sp_row,
    sp_col,
    ex_row,
    ex_col,
    nb_row,
    nb_col,
    corner,
    rx_row,
    rx_col,
    ry_row,
    ry_col,
    in_sem,
    table_sem,
    send_sem,
    nb_sem,
    corner_sem,
    row_sem,
    col_sem,
    row_end_sem,
    col_end_sem,
):
    _, panels, rows, cols, levels = inp.shape
    half_r, half_c = rows // 2, cols // 2
    k = cols // rows
    length = half_r
    last = length - 1
    height = spread.shape[1] // 2
    block = st_row.shape[3]
    r = lax.axis_index("tx")
    c = lax.axis_index("ty")
    is_row = (r == 0) | (r == nr - 1)
    is_col = (c == 0) | (c == nc - 1)
    tr = (r == nr - 1).astype(jnp.int32)
    tc = (c == nc - 1).astype(jnp.int32)
    row_ok = (r > 0, r < nr - 1)
    col_ok = (c > 0, c < nc - 1)

    def row_segment(f, p):
        return k * c + p if f == 0 else nr - 1 - k * c - p

    def col_segment(f):
        return r if f == 0 else nr - 1 - r

    def clamp(x, n):
        return jnp.minimum(jnp.maximum(x, 0), n - 1)

    used = 6
    full = panels * levels
    spare = LANES - full
    packed_rows = 3 * rows

    def traffic(sending):
        def remote(src, dst, sem, dest):
            if sending:
                pltpu.make_async_remote_copy(
                    src_ref=src,
                    dst_ref=dst,
                    send_sem=send_sem.at[0],
                    recv_sem=sem,
                    device_id=dest,
                    device_id_type=MESH,
                ).start()
            else:
                pltpu.make_async_copy(src, src, send_sem.at[0]).wait()

        def local(src, dst, sem):
            if sending:
                pltpu.make_async_copy(src, dst, sem).start()

        def either(src, dst, sem, dest, mine):
            @pl.when(jnp.logical_not(mine))
            def _():
                remote(src, dst, sem, dest)

            @pl.when(mine)
            def _():
                local(src, dst, sem)

        def at_row(e):
            return r == e * (nr - 1)

        def at_col(e):
            return c == e * (nc - 1)

        def strips_to_rows(e):
            row = e * (nr - 1)

            @pl.when(is_row)
            def _():
                src = sp_row.at[tr, :, 0:packed_rows]
                to = jnp.minimum(c, nc - 1 - c)
                f = (c > to).astype(jnp.int32)
                for to, f in ((to, f), (nc - 1 - to, 1 - f)):
                    either(src, rx_row.at[4 * f + tr, :, 0:packed_rows], row_sem, (row, to), at_row(e) & (to == c))

            @pl.when(is_col)
            def _():
                g = jnp.minimum(r, nr - 1 - r)
                f = (r > g).astype(jnp.int32)
                for g, f in ((g, f), (nr - 1 - g, 1 - f)):
                    dst = rx_row.at[4 * f + 2 + tc, lax.rem(r, k), 0:packed_rows]
                    to = lax.div(g, k)
                    either(sp_col.at[tc, 0:packed_rows], dst, row_sem, (row, to), at_row(e) & (to == c))

        def strips_to_columns(e):
            col = e * (nc - 1)

            @pl.when(is_row)
            def _():
                for p in range(k):
                    extreme = (c == 0) if p == 0 else (c == nc - 1)
                    if k == 1:
                        extreme = extreme | (c == nc - 1)

                    def to_columns(p=p):
                        for f in (1, 0):
                            to = row_segment(f, p)
                            remote(st_row.at[tr, p], rx_col.at[4 * f + tr], col_sem, (to, col))

                    if 0 < p < k - 1:
                        to_columns()
                    else:
                        pl.when(jnp.logical_not(extreme))(to_columns)

            @pl.when(is_col & jnp.logical_not(is_row))
            def _():
                src = st_col.at[tc]
                remote(src, rx_col.at[6 + tc], col_sem, (nr - 1 - r, col))
                either(src, rx_col.at[2 + tc], col_sem, (r, col), at_col(e))

        def ends(e):
            row, col = e * (nr - 1), e * (nc - 1)
            for f in (1, 0):
                for h in range(2):
                    d = 1 if h != f else -1
                    end = 0 if d == 1 else 1

                    @pl.when(is_row)
                    def _():
                        slot = 4 * f + tr
                        for p in range(k):
                            outer_end = p == (k - 1 if h == 1 else 0)

                            def one_end(p=p, outer_end=outer_end):
                                src = ex_row.at[tr, p, h, 0:used]
                                if outer_end:
                                    to = clamp((c if f == 0 else nc - 1 - c) + d, nc)
                                    dst = ry_row.at[end, slot, 0:used]
                                    sem = row_end_sem.at[end]
                                    if f == 0:
                                        remote(src, dst, sem, (row, to))
                                    else:
                                        either(src, dst, sem, (row, to), at_row(e) & (to == c))
                                to = clamp(row_segment(f, p) + d, nr)
                                dst = ry_col.at[end, slot, 0:used]
                                sem = col_end_sem.at[end]
                                either(src, dst, sem, (to, col), at_col(e) & (to == r))

                            if outer_end:
                                pl.when(col_ok[h])(one_end)
                            else:
                                one_end()

                    @pl.when(is_col & row_ok[h])
                    def _():
                        slot = 4 * f + 2 + tc
                        src = ex_col.at[tc, h, 0:used]
                        g = col_segment(f)

                        def crossing():
                            to = clamp(lax.div(g, k) + d, nc)
                            dst = ry_row.at[end, slot, 0:used]
                            sem = row_end_sem.at[end]
                            either(src, dst, sem, (row, to), at_row(e) & (to == c))

                        if k == 1:
                            crossing()
                        else:
                            pl.when(lax.rem(g, k) == (k - 1 if d == 1 else 0))(crossing)
                        to = clamp(g + d, nr)
                        dst = ry_col.at[end, slot, 0:used]
                        sem = col_end_sem.at[end]
                        if f == 0:
                            remote(src, dst, sem, (to, col))
                        else:
                            either(src, dst, sem, (to, col), at_col(e) & (to == r))

        def within(s):
            @pl.when(row_ok[s])
            def _():
                remote(st_row.at[s], nb_row.at[1 - s], nb_sem.at[1 - s], (r + 2 * s - 1, c))

            @pl.when(col_ok[s])
            def _():
                remote(st_col.at[s], nb_col.at[1 - s], nb_sem.at[3 - s], (r, c + 2 * s - 1))

            for w in range(2):
                at = 2 * (1 - s) + 1 - w

                @pl.when(row_ok[s] & col_ok[w])
                def _():
                    remote(
                        ex_row.at[s, w * (k - 1), w, 0:used],
                        corner.at[at, 0:used],
                        corner_sem.at[at],
                        (r + 2 * s - 1, c + 2 * w - 1),
                    )

        strips_to_rows(0)
        if sending:
            stage_ends()
        ends(0)
        within(0)
        strips_to_rows(1)
        strips_to_columns(0)
        strips_to_columns(1)
        ends(1)
        within(1)

    fields = (gain_hbm, vert_hbm, den_hbm, res_hbm)
    for pair in range(2):
        for p in range(panels):
            for i in (2 * pair, 2 * pair + 1):
                pltpu.make_async_copy(fields[i].at[p], inp.at[i, p], in_sem.at[pair]).start()
    table_loads = [
        pltpu.make_async_copy(source, tables.at[i], table_sem.at[0])
        for i, source in enumerate((panel_hbm, side_hbm, flip_hbm))
    ]
    for load in table_loads:
        load.start()

    barrier = pltpu.get_barrier_semaphore()
    far_r, near_r = (1 - tr) * (nr - 1), tr * (nr - 1)
    far_c, near_c = (1 - tc) * (nc - 1), tc * (nc - 1)

    def greet(dest):
        pl.semaphore_signal(barrier, inc=1, device_id=dest, device_id_type=MESH)

    def number(flag):
        return flag.astype(jnp.int32)

    def row_greetings():
        found = []
        for near in (False, True):
            for f in (1, 0):
                here = c if f == 0 else nc - 1 - c
                for d in (0, -1, 1):
                    if near and f == 0 and d == 0:
                        continue
                    ok = None if d == 0 else (here > 0) if d == -1 else (here < nc - 1)
                    mine = (here + d == c) if near and f == 1 and d else None
                    found.append((ok, mine, (near_r if near else far_r, clamp(here + d, nc))))
        for d in range(-1, k + 1):
            for f in (1, 0):
                low = row_segment(f, 0 if f == 0 else k - 1)
                for near in (False, True):
                    ok = None if 0 <= d < k else (low > 0) if d == -1 else (low + d < nr)
                    mine = (is_col & (low + d == r)) if near else None
                    found.append((ok, mine, (clamp(low + d, nr), near_c if near else far_c)))
        return found

    def col_greetings():
        found = []
        for near in (False, True):
            for f in (1, 0):
                g = col_segment(f)
                for d in (0, -1, 1):
                    inside = None if d == 0 else (g > 0) if d == -1 else (g < nr - 1)
                    if not (near and f == 0 and d == 0):
                        mine = (g + d == r) if near and f == 1 and d else None
                        found.append((inside, mine, (clamp(g + d, nr), near_c if near else far_c)))
                    cross = inside
                    if d and k > 1:
                        cross = inside & (lax.rem(g, k) == (k - 1 if d == 1 else 0))
                    to = lax.div(g, k) + d
                    mine = (is_row & (to == c)) if near else None
                    found.append((cross, mine, (near_r if near else far_r, clamp(to, nc))))
        return found

    def near_greetings():
        found = []
        for dr in (-1, 0, 1):
            for dc in (-1, 0, 1):
                if dr or dc:
                    ok = row_ok[(dr + 1) // 2] if dr else None
                    if dc:
                        side = col_ok[(dc + 1) // 2]
                        ok = side if ok is None else ok & side
                    found.append((ok, None, (r + dr, c + dc)))
        return found

    def announce(found):
        total = jnp.int32(0)
        for ok, mine, dest in found:
            go = ok
            if mine is not None:
                go = jnp.logical_not(mine) if go is None else go & jnp.logical_not(mine)
            if go is None:
                total = total + 1
            else:
                total = total + number(go)
        return total

    def tell(found):
        for ok, mine, dest in found:
            go = ok
            if mine is not None:
                go = jnp.logical_not(mine) if go is None else go & jnp.logical_not(mine)
            if go is None:
                greet(dest)
            else:
                pl.when(go)(functools.partial(greet, dest))

    pl.when(is_row)(lambda: tell(row_greetings()))
    pl.when(is_col)(lambda: tell(col_greetings()))
    tell(near_greetings())
    expected = announce(near_greetings())
    expected = expected + jnp.where(is_row, announce(row_greetings()), 0)
    expected = expected + jnp.where(is_col, announce(col_greetings()), 0)

    lane = lax.broadcasted_iota(jnp.int32, (TILE, LANES), 1)
    sub = lax.broadcasted_iota(jnp.int32, (height, LANES), 0)
    level = lane[:1] % levels
    first_level = level == 0
    last_level = level == levels - 1

    def lower(x):
        return jnp.where(first_level, 0.0, pltpu.roll(x, 1, 1))

    def upper(x):
        return jnp.where(last_level, 0.0, pltpu.roll(x, LANES - 1, 1))

    def pick_tables(side):
        index = lane
        code = jnp.zeros_like(lane)
        for p in range(panels):
            here = lane // levels == p
            index = jnp.where(here, tables[0, side, p] * levels + lane % levels, index)
            code = jnp.where(here, tables[2, side, p] * 4 + tables[1, side, p], code)
        chunk = index // spare
        return index, code, jnp.where(lane < full, full + index - chunk * spare, lane), chunk

    def pack(value):
        filler = jnp.zeros((rows, cols, LANES - panels * levels), jnp.float32)
        return jnp.concatenate([value[p] for p in range(panels)] + [filler], axis=-1)

    def split(which, value):
        packed[which, :, :cols, :] = value
        if packed.shape[2] > cols:
            packed[which, :, cols:, :] = jnp.zeros(
                (rows, packed.shape[2] - cols, LANES), jnp.float32
            )
        return [
            [packed[which, y, pl.ds(b, height, stride=2), :] for b in range(2)]
            for y in range(rows)
        ]

    def fine(fun):
        return [[fun(y, b) for b in range(2)] for y in range(rows)]

    small = range(half_r)

    def block_mean(values, i):
        y = 2 * i
        return 0.25 * (values[y][0] + values[y][1] + values[y + 1][0] + values[y + 1][1])

    pltpu.make_async_copy(inp.at[0:2], inp.at[0:2], in_sem.at[0]).wait()
    gain = split(1, pack(inp[0]))
    vertical = split(2, pack(inp[1]))
    low_vert = fine(lambda y, b: lower(vertical[y][b]))
    inverse = fine(
        lambda y, b: relaxation / (gain[y][b] + 4.0 + vertical[y][b] + low_vert[y][b])
    )
    c_vert = [block_mean(vertical, i) for i in small]
    c_low = [lower(c_vert[i]) for i in small]
    c_inv = [relaxation / (block_mean(gain, i) + 1.0 + c_vert[i] + c_low[i]) for i in small]
    pltpu.make_async_copy(inp.at[2:4], inp.at[2:4], in_sem.at[1]).wait()
    right_side = split(0, pack(inp[2] * inp[3]))
    smoothed = fine(lambda y, b: inverse[y][b] * right_side[y][b])

    def inner(y, b):
        x = smoothed[y][b]
        return vertical[y][b] * upper(x) + low_vert[y][b] * lower(x)

    coupled = fine(inner)
    column = fine(lambda y, b: coupled[y][b] + (1.0 - relaxation) * right_side[y][b])
    north = [smoothed[2 * i][0] + smoothed[2 * i][1] for i in small]
    south = [smoothed[2 * i + 1][0] + smoothed[2 * i + 1][1] for i in small]
    west = [smoothed[2 * i][0] + smoothed[2 * i + 1][0] for i in small]
    east = [smoothed[2 * i][1] + smoothed[2 * i + 1][1] for i in small]
    from_w = [pltpu.roll(east[i], 1, 0) for i in small]
    from_e = [pltpu.roll(west[i], height - 1, 0) for i in small]
    start_w = sub % length == 0
    start_e = sub % length == last
    edge_w = sub == 0
    edge_e = sub == half_c - 1

    def bare(i):
        total = block_mean(column, i) + 0.5 * (north[i] + south[i])
        beside = None
        if i > 0:
            beside = south[i - 1]
        if i < half_r - 1:
            beside = north[i + 1] if beside is None else beside + north[i + 1]
        return total if beside is None else total + 0.25 * beside

    plain = [bare(i) for i in small]

    def partial_guess(i, mask_w, mask_e):
        beside = jnp.where(mask_w, 0.0, from_w[i]) + jnp.where(mask_e, 0.0, from_e[i])
        return c_inv[i] * (plain[i] + 0.25 * beside)

    by_tile = [partial_guess(i, edge_w, edge_e) for i in small]
    by_piece = by_tile if k == 1 else [partial_guess(i, start_w, start_e) for i in small]

    def put(ref, at, value):
        ref[at : at + value.shape[0], :] = value

    def press(ref, runs, singles):
        for at, run in enumerate(runs):
            put(ref, at * length, run)
        singles = jnp.concatenate(singles + [jnp.zeros((TILE - used, LANES), jnp.float32)], axis=0)
        for j in range(full // spare):
            moved = pltpu.roll(singles, full - spare * j, 1)
            ref[used * j : used * (j + 1), full:] = moved[:used, full:]

    for s in range(2):
        y = s * (rows - 1)
        i0, i1 = (0, 1) if s == 0 else (half_r - 1, half_r - 2)
        out = north[0] if s == 0 else south[half_r - 1]
        for p in range(k):
            lo, hi = p * length, p * length + last
            seg = slice(lo, hi + 1)
            one = lambda x, j: x[j : j + 1]
            a, b, g = (st_row.at[s, p, q] for q in range(3))
            put(a, 0, smoothed[y][0][seg])
            put(a, length, smoothed[y][1][seg])
            put(a, 2 * length, one(c_inv[i1], lo))
            put(a, 2 * length + 1, one(c_inv[i1], hi))
            put(b, 0, by_piece[i0][seg])
            put(b, length, by_piece[i1][seg])
            put(b, 2 * length, one(west[i0], lo))
            put(b, 2 * length + 1, one(east[i0], hi))
            put(g, 0, c_inv[i0][seg])
            put(g, length, c_vert[i0][seg])
            put(g, 2 * length, one(west[i1], lo))
            put(g, 2 * length + 1, one(east[i1], hi))
            parts = (smoothed[y][0], smoothed[y][1], by_piece[i0], by_piece[i1])
            press(
                sp_row.at[s, p],
                [x[seg] for x in parts + (c_inv[i0], c_vert[i0])],
                [one(c_inv[i1], lo), one(c_inv[i1], hi)]
                + [one(west[i0], lo), one(east[i0], hi), one(west[i1], lo), one(east[i1], hi)],
            )
    for s in range(2):
        j0, j1 = (0, 1) if s == 0 else (half_c - 1, half_c - 2)
        out = west if s == 0 else east
        a, b, g = (st_col.at[s, q] for q in range(3))
        at0 = lambda x: x[j0 : j0 + 1]
        at1 = lambda x: x[j1 : j1 + 1]
        for y in range(rows):
            put(a, (y % 2) * length + y // 2, at0(smoothed[y][s]))
        put(a, 2 * length, at1(c_inv[0]))
        put(a, 2 * length + 1, at1(c_inv[half_r - 1]))
        for i in small:
            put(b, i, at0(by_tile[i]))
            put(b, length + i, at1(by_tile[i]))
            put(g, i, at0(c_inv[i]))
            put(g, length + i, at0(c_vert[i]))
        put(b, 2 * length, at0(north[0]))
        put(b, 2 * length + 1, at0(south[half_r - 1]))
        put(g, 2 * length, at1(north[0]))
        put(g, 2 * length + 1, at1(south[half_r - 1]))
        parts = [
            [at0(smoothed[2 * i][s]) for i in small],
            [at0(smoothed[2 * i + 1][s]) for i in small],
            [at0(x) for x in by_tile],
            [at1(x) for x in by_tile],
            [at0(x) for x in c_inv],
            [at0(x) for x in c_vert],
        ]
        press(
            sp_col.at[s],
            [jnp.concatenate(x, axis=0) for x in parts],
            [at1(c_inv[0]), at1(c_inv[half_r - 1]), at0(north[0]), at0(south[half_r - 1])]
            + [at1(north[0]), at1(south[half_r - 1])],
        )

    def stage_ends():
        for s in range(2):
            i0, i1 = (0, 1) if s == 0 else (half_r - 1, half_r - 2)
            out = north[0] if s == 0 else south[half_r - 1]
            for p in range(k):
                lo, hi = p * length, p * length + last
                one = lambda x, j: x[j : j + 1]
                for h in range(2):
                    j, j1 = (lo, lo + 1) if h == 0 else (hi, hi - 1)
                    side = west if h == 0 else east
                    x = ex_row.at[s, p, h]
                    put(x, 0, one(by_piece[i0], j))
                    put(x, 1, one(c_inv[i0], j))
                    put(x, 2, one(side[i0], j))
                    put(x, 3, one(side[i1], j))
                    put(x, 4, one(out, j))
                    put(x, 5, one(out, j1))
        for s in range(2):
            j0, j1 = (0, 1) if s == 0 else (half_c - 1, half_c - 2)
            out = west if s == 0 else east
            at0 = lambda x: x[j0 : j0 + 1]
            at1 = lambda x: x[j1 : j1 + 1]
            for h in range(2):
                i0, i1 = (0, 1) if h == 0 else (half_r - 1, half_r - 2)
                side = north[0] if h == 0 else south[half_r - 1]
                x = ex_col.at[s, h]
                put(x, 0, at0(by_tile[i0]))
                put(x, 1, at0(c_inv[i0]))
                put(x, 2, at0(side))
                put(x, 3, at1(side))
                put(x, 4, at0(out[i0]))
                put(x, 5, at0(out[i1]))

    pl.semaphore_wait(barrier, expected)
    traffic(True)

    def beside(y, b):
        x = smoothed[y][b]
        total = coupled[y][b] + smoothed[y][1 - b]
        if y > 0:
            total = total + smoothed[y - 1][b]
        if y < rows - 1:
            total = total + smoothed[y + 1][b]
        return total

    partial = fine(beside)
    traffic(False)

    pltpu.make_async_copy(tables, tables, table_sem.at[0]).wait()
    row_pick = pick_tables(tr)
    col_pick = pick_tables(2 + tc)

    def arrived(ref, sem):
        pltpu.make_async_copy(ref, ref, sem).wait()

    order = list(range(2 * length))[::-1] + [2 * length + 1, 2 * length]
    other = (
        list(range(length))[::-1]
        + list(range(length, 2 * length))[::-1]
        + [2 * length + 1, 2 * length]
    )
    sublane = lax.broadcasted_iota(jnp.int32, (block, LANES), 0)

    def flip_index(perm):
        index = sublane
        for at, source in enumerate(perm):
            index = jnp.where(sublane == at, source, index)
        return index

    flips = [flip_index(order), flip_index(other), flip_index(other)]

    def choose(read, pick, f, second=False):
        index, code = pick[2 if second else 0], pick[1]
        taken = None
        for t in range(4):
            moved = jnp.take_along_axis(read(4 * f + t), index, axis=1, mode="promise_in_bounds")
            taken = moved if taken is None else jnp.where(code == 4 * f + t, moved, taken)
        return taken

    def select(plainly, reverse, pick, group):
        straight = choose(plainly, pick, 0)
        turned = choose(reverse, pick, 1)
        if group is not None:
            turned = jnp.take_along_axis(turned, flips[group], axis=0, mode="promise_in_bounds")
        return jnp.where(pick[1] >= 4, turned, straight)

    def rows_of(tiles, first, final):
        parts = []
        for q, tile in enumerate(tiles):
            lo, hi = max(first, q * TILE), min(final, (q + 1) * TILE)
            if lo < hi:
                parts.append(tile[lo - q * TILE : hi - q * TILE])
        return parts

    def select_packed(plainly, reverse, pick):
        tiles = range(-(-packed_rows // TILE))
        results = []
        for f, read in ((0, plainly), (1, reverse)):
            main = [choose(lambda s: read(s, q), pick, f) for q in tiles]
            extra = [choose(lambda s: read(s, q), pick, f, True) for q in tiles]
            singles = None
            for j in range(full // spare):
                part = jnp.concatenate(rows_of(extra, used * j, used * (j + 1)), axis=0)
                same = pick[3][:used] == j
                singles = part if singles is None else jnp.where(same, part, singles)
            groups = []
            for q in range(3):
                lines = rows_of(main, 2 * length * q, 2 * length * (q + 1))
                lines.append(singles[2 * q : 2 * q + 2])
                if block > 2 * length + 2:
                    lines.append(jnp.zeros((block - 2 * length - 2, LANES), jnp.float32))
                groups.append(jnp.concatenate(lines, axis=0))
            results.append(groups)
        turned = [
            jnp.take_along_axis(x, flips[q], axis=0, mode="promise_in_bounds")
            for q, x in enumerate(results[1])
        ]
        return [jnp.where(pick[1] >= 4, x, y) for x, y in zip(turned, results[0])]

    @pl.when(is_row)
    def _():
        arrived(rx_row.at[:, :, 0:packed_rows], row_sem)
        for p in range(k):
            value = select_packed(
                lambda s, q: rx_row[s, p, q * TILE : (q + 1) * TILE],
                lambda s, q: rx_row[s, k - 1 - p, q * TILE : (q + 1) * TILE],
                row_pick,
            )
            for q in range(3):
                nb_row[tr, p, q] = value[q]
        for w in range(2):

            @pl.when(col_ok[w])
            def _():
                arrived(ry_row.at[w, :, 0:used], row_end_sem.at[w])
                read = lambda s: ry_row[w, s]
                corner[2 * tr + w] = select(read, read, row_pick, None)

    @pl.when(is_col & jnp.logical_not(is_row))
    def _():
        arrived(rx_col, col_sem)
        for q in range(3):
            read = lambda s: rx_col[s, q]
            nb_col[tc, q] = select(read, read, col_pick, q)

    @pl.when(is_col & is_row)
    def _():
        swap = (tr != tc).astype(jnp.int32)

        def read(s, q):
            f, t = s // 4, s % 4
            at = 4 * (1 - swap) + t if f == 1 else 4 * swap + t
            piece = (tr if f == 0 else 1 - tr) * (k - 1)
            return rx_row[at, piece, q * TILE : (q + 1) * TILE]

        value = select_packed(read, read, col_pick)
        for q in range(3):
            nb_col[tc, q] = value[q]

    @pl.when(is_col)
    def _():
        for s in range(2):

            @pl.when(row_ok[s])
            def _():
                arrived(ry_col.at[s, :, 0:used], col_end_sem.at[s])
                read = lambda slot: ry_col[s, slot]
                value = select(read, read, col_pick, None)
                corner[2 * s + tc, 0:2, :] = value[0:2]
                corner[2 * s + tc, 2:4, :] = value[4:6]
                corner[2 * s + tc, 4:6, :] = value[2:4]

    for s in range(2):

        @pl.when(row_ok[s])
        def _():
            arrived(nb_row.at[s], nb_sem.at[s])

        @pl.when(col_ok[s])
        def _():
            arrived(nb_col.at[s], nb_sem.at[2 + s])

        for w in range(2):

            @pl.when(row_ok[s] & col_ok[w])
            def _():
                arrived(corner.at[2 * s + w, 0:used], corner_sem.at[2 * s + w])

    @pl.when(is_row & is_col)
    def _():
        at = 2 * tr + tc
        corner[at, 0:2, :] = jnp.zeros((2, LANES), jnp.float32)
        for q in range(2):
            rows_z = nb_col[tc, 1 + q]
            rows_x = nb_row[tr, tc * (k - 1), 1 + q]
            corner[at, 2 + q : 3 + q, :] = jnp.where(
                tr == 0, rows_z[2 * length : 2 * length + 1], rows_z[2 * length + 1 : 2 * length + 2]
            )
            corner[at, 4 + q : 5 + q, :] = jnp.where(
                tc == 0, rows_x[2 * length : 2 * length + 1], rows_x[2 * length + 1 : 2 * length + 2]
            )

    def zeros(count):
        return [jnp.zeros((count, LANES), jnp.float32)] if count else []

    def stack(lines, total):
        used = sum(x.shape[0] for x in lines)
        return jnp.concatenate(list(lines) + zeros(total - used), axis=0)

    tall_z = round_up(half_r, TILE)
    flat = 2 * length

    class Strip:
        pass

    def strip(read, pieces, ends, total, own):
        def gather(q, at):
            return stack([read(p, q, slice(at, at + length)) for p in range(pieces)], total)

        def sides(first, final):
            lines = []
            for p in range(pieces):
                lines += [first(p)] + zeros(length - 2) + [final(p)]
            return stack(lines, total)

        def lateral(q):
            return sides(
                lambda p: ends[0][q] if p == 0 else read(p - 1, 1 + q, slice(flat + 1, flat + 2)),
                lambda p: ends[1][q]
                if p == pieces - 1
                else read(p + 1, 1 + q, slice(flat, flat + 1)),
            )

        x = Strip()
        x.even, x.odd = gather(0, 0), gather(0, length)
        x.pair = x.even + x.odd
        inv1 = sides(
            lambda p: read(p, 0, slice(flat, flat + 1)),
            lambda p: read(p, 0, slice(flat + 1, flat + 2)),
        )
        x.inv, x.vert = gather(2, 0), gather(2, length)
        x.guess = gather(1, 0) + 0.25 * x.inv * (lateral(0) + own)
        x.inside = gather(1, length) + 0.25 * inv1 * lateral(1)
        return x

    def corner_row(s, w, at):
        return corner[2 * s + w, at : at + 1, :]

    row_strip = []
    for s in range(2):
        own = north[0] if s == 0 else south[half_r - 1]
        ends = [[corner_row(s, w, 2 + q) for q in range(2)] for w in range(2)]
        row_strip.append(
            strip(lambda p, q, rows_: nb_row[s, p, q, rows_, :], k, ends, height, own)
        )
    col_strip = []
    for w in range(2):
        j = w * (half_c - 1)
        faces = west if w == 0 else east
        own = stack([faces[i][j : j + 1] for i in small], tall_z)
        ends = [[corner_row(s, w, 4 + q) for q in range(2)] for s in range(2)]
        col_strip.append(
            strip(lambda p, q, rows_: nb_col[w, q, rows_, :], 1, ends, tall_z, own)
        )

    guess = []
    for i in small:
        lateral = jnp.where(edge_w, col_strip[0].pair[i : i + 1], 0.0)
        lateral = lateral + jnp.where(edge_e, col_strip[1].pair[i : i + 1], 0.0)
        if i == 0:
            lateral = lateral + row_strip[0].pair
        if i == half_r - 1:
            lateral = lateral + row_strip[1].pair
        guess.append(by_tile[i] + 0.25 * c_inv[i] * lateral)

    row_side = [[None] * 2 for _ in range(2)]
    col_side = [[None] * 2 for _ in range(2)]
    for s in range(2):
        for w in range(2):
            faces = nb_row[s, w * (k - 1), 1, flat + w : flat + w + 1, :]
            faces = faces + nb_col[w, 1, flat + s : flat + s + 1, :]
            there = corner_row(s, w, 0) + 0.25 * corner_row(s, w, 1) * faces
            tip = (r == s * (nr - 1)) & (c == w * (nc - 1))
            jr, jc = w * (half_c - 1), s * (half_r - 1)
            row_side[s][w] = jnp.where(tip, col_strip[w].guess[jc : jc + 1], there)
            col_side[w][s] = jnp.where(tip, row_strip[s].guess[jr : jr + 1], there)

    def relax(x, ends, own, count):
        total = x.guess.shape[0]
        at = lax.broadcasted_iota(jnp.int32, (total, LANES), 0)
        around = x.inside + own
        around = around + jnp.where(at == 0, ends[0], pltpu.roll(x.guess, 1, 0))
        around = around + jnp.where(at == count - 1, ends[1], pltpu.roll(x.guess, total - 1, 0))
        column = x.vert * upper(x.guess) + lower(x.vert) * lower(x.guess)
        return (2.0 - relaxation) * x.guess + x.inv * (0.25 * around + column)

    row_fix = [
        relax(row_strip[s], row_side[s], guess[s * (half_r - 1)], half_c) for s in range(2)
    ]
    col_fix = []
    for w in range(2):
        j = w * (half_c - 1)
        own = stack([guess[i][j : j + 1] for i in small], tall_z)
        col_fix.append(relax(col_strip[w], col_side[w], own, half_r))

    def from_left(x, line):
        return jnp.where(edge_w, line, pltpu.roll(x, 1, 0))

    def from_right(x, line):
        return jnp.where(edge_e, line, pltpu.roll(x, height - 1, 0))

    correction = []
    for i in small:
        x = guess[i]
        around = from_left(x, col_strip[0].guess[i : i + 1])
        around = around + from_right(x, col_strip[1].guess[i : i + 1])
        around = around + (guess[i - 1] if i > 0 else row_strip[0].guess)
        around = around + (guess[i + 1] if i < half_r - 1 else row_strip[1].guess)
        levels_part = c_vert[i] * upper(x) + c_low[i] * lower(x)
        correction.append((2.0 - relaxation) * x + c_inv[i] * (0.25 * around + levels_part))
        small_ref[i] = correction[i]

    def outer(y, b):
        at = (y % 2) * length + y // 2
        source = col_strip[b]
        line = (source.even if y % 2 == 0 else source.odd)[y // 2 : y // 2 + 1]
        if b == 0:
            total = partial[y][b] + from_left(smoothed[y][1], line)
        else:
            total = partial[y][b] + from_right(smoothed[y][0], line)
        if y == 0:
            total = total + (row_strip[0].even if b == 0 else row_strip[0].odd)
        if y == rows - 1:
            total = total + (row_strip[1].even if b == 0 else row_strip[1].odd)
        return total

    c_up = [upper(x) for x in correction]
    c_down = [lower(x) for x in correction]
    left = [from_left(correction[i], col_fix[0][i : i + 1]) for i in small]
    right = [from_right(correction[i], col_fix[1][i : i + 1]) for i in small]
    for y in range(rows):
        i = y // 2
        next_i = i - 1 if y % 2 == 0 else i + 1
        for b in range(2):
            total = outer(y, b) + 2.0 * correction[i]
            total = total + vertical[y][b] * c_up[i] + low_vert[y][b] * c_down[i]
            if next_i < 0:
                total = total + row_fix[0]
            elif next_i >= half_r:
                total = total + row_fix[1]
            else:
                total = total + correction[next_i]
            total = total + (left if b == 0 else right)[i]
            first = (2.0 - relaxation) * smoothed[y][b] + (1.0 - relaxation) * correction[i]
            spread[y, pl.ds(b, height, stride=2), :] = first + inverse[y][b] * total


def unpack(spread, small_ref, sol_hbm, corr_hbm, sol, corr, sem):
    panels, _, cols, levels = sol.shape
    half_c = corr.shape[2]
    for p in range(panels):
        lanes = slice(p * levels, (p + 1) * levels)
        sol[p] = spread[:, :cols, lanes]
        pltpu.make_async_copy(sol.at[p], sol_hbm.at[p], sem.at[0]).start()
    for p in range(panels):
        lanes = slice(p * levels, (p + 1) * levels)
        corr[p] = small_ref[:, :half_c, lanes]
    last = pltpu.make_async_copy(corr, corr_hbm, sem.at[1])
    last.start()
    pltpu.make_async_copy(sol, sol_hbm, sem.at[0]).wait()
    last.wait()


def solution(mesh):
    nr, nc = mesh.shape["tx"], mesh.shape["ty"]

    def shards(residual, density, gain, vertical, edge_panel, edge_side, edge_flip):
        panels, rows, cols, levels = residual.shape
        k = cols // rows
        assert cols == k * rows and rows % 2 == 0 and panels * levels <= LANES
        assert rows >= 6 and nr > 1 and nc > 1
        block = round_up(rows + 2, TILE)
        dense = round_up(3 * rows, TILE)
        spare = LANES - panels * levels
        assert spare % levels == 0 and panels * levels % spare == 0
        assert 2 * panels * levels <= rows * spare
        height = round_up(cols // 2, TILE)
        tall = 2 * height
        f32 = jnp.float32
        spread, small = pl.pallas_call(
            functools.partial(kernel, nr, nc),
            out_shape=(
                pltpu.VMEM((rows, tall, LANES), f32),
                pltpu.VMEM((rows // 2, height, LANES), f32),
            ),
            in_specs=[pl.BlockSpec(memory_space=pl.ANY)] * 7,
            out_specs=(pl.BlockSpec(memory_space=pltpu.VMEM),) * 2,
            scratch_shapes=[
                pltpu.VMEM((4, panels, rows, cols, levels), f32),
                pltpu.SMEM((3,) + edge_panel.T.shape, jnp.int32),
                pltpu.VMEM((3, rows, tall, LANES), f32),
                pltpu.VMEM((3, k, 3, block, LANES), f32),
                pltpu.VMEM((3, 3, block, LANES), f32),
                pltpu.VMEM((3, k, dense, LANES), f32),
                pltpu.VMEM((3, dense, LANES), f32),
                pltpu.VMEM((3, k, 2, TILE, LANES), f32),
                pltpu.VMEM((3, 2, TILE, LANES), f32),
                pltpu.VMEM((3, k, 3, block, LANES), f32),
                pltpu.VMEM((3, 3, block, LANES), f32),
                pltpu.VMEM((5, TILE, LANES), f32),
                pltpu.VMEM((8, k, dense, LANES), f32),
                pltpu.VMEM((8, 3, block, LANES), f32),
                pltpu.VMEM((2, 8, TILE, LANES), f32),
                pltpu.VMEM((2, 8, TILE, LANES), f32),
                pltpu.SemaphoreType.DMA((2,)),
                pltpu.SemaphoreType.DMA((1,)),
                pltpu.SemaphoreType.DMA((1,)),
                pltpu.SemaphoreType.DMA((4,)),
                pltpu.SemaphoreType.DMA((4,)),
                pltpu.SemaphoreType.DMA,
                pltpu.SemaphoreType.DMA,
                pltpu.SemaphoreType.DMA((2,)),
                pltpu.SemaphoreType.DMA((2,)),
            ],
            compiler_params=pltpu.CompilerParams(collective_id=0, has_side_effects=True),
        )(residual, density, gain, vertical, edge_panel.T, edge_side.T, edge_flip.T)
        spread = pltpu.with_memory_space_constraint(spread, pltpu.VMEM)
        small = pltpu.with_memory_space_constraint(small, pltpu.VMEM)
        return pl.pallas_call(
            unpack,
            out_shape=(
                jax.ShapeDtypeStruct(residual.shape, f32),
                jax.ShapeDtypeStruct((panels, rows // 2, cols // 2, levels), f32),
            ),
            in_specs=[pl.BlockSpec(memory_space=pltpu.VMEM)] * 2,
            out_specs=(pl.BlockSpec(memory_space=pl.ANY),) * 2,
            scratch_shapes=[
                pltpu.VMEM(residual.shape, f32),
                pltpu.VMEM((panels, rows // 2, cols // 2, levels), f32),
                pltpu.SemaphoreType.DMA((2,)),
            ],
        )(spread, small)

    fields = P(None, "tx", "ty", None)
    return jax.shard_map(
        shards,
        mesh=mesh,
        in_specs=(fields,) * 4 + (P(),) * 3,
        out_specs=(fields, fields),
        check_vma=False,
    )
```

```python
import functools

import jax
import jax.numpy as jnp
from jax import lax
from jax.experimental import pallas as pl
from jax.experimental.pallas import tpu as pltpu
from jax.sharding import PartitionSpec as P

MESH = pl.DeviceIdType.MESH
relaxation = 0.8
LANES = 128
TILE = 8


def round_up(value, unit):
    return (value + unit - 1) // unit * unit


def kernel(
    nr,
    nc,
    res_hbm,
    den_hbm,
    gain_hbm,
    vert_hbm,
    panel_hbm,
    side_hbm,
    flip_hbm,
    spread,
    small_ref,
    inp,
    tables,
    packed,
    st_row,
    st_col,
    sp_row,
    sp_col,
    ex_row,
    ex_col,
    nb_row,
    nb_col,
    corner,
    rx_row,
    rx_col,
    ry_row,
    ry_col,
    in_sem,
    table_sem,
    send_sem,
    nb_sem,
    corner_sem,
    row_sem,
    col_sem,
    row_end_sem,
    col_end_sem,
):
    _, panels, rows, cols, levels = inp.shape
    half_r, half_c = rows // 2, cols // 2
    k = cols // rows
    length = half_r
    last = length - 1
    height = spread.shape[1] // 2
    block = st_row.shape[3]
    r = lax.axis_index("tx")
    c = lax.axis_index("ty")
    is_row = (r == 0) | (r == nr - 1)
    is_col = (c == 0) | (c == nc - 1)
    tr = (r == nr - 1).astype(jnp.int32)
    tc = (c == nc - 1).astype(jnp.int32)
    row_ok = (r > 0, r < nr - 1)
    col_ok = (c > 0, c < nc - 1)

    def row_segment(f, p):
        return k * c + p if f == 0 else nr - 1 - k * c - p

    def col_segment(f):
        return r if f == 0 else nr - 1 - r

    def clamp(x, n):
        return jnp.minimum(jnp.maximum(x, 0), n - 1)

    used = 6
    full = panels * levels
    spare = LANES - full
    packed_rows = 3 * rows

    def traffic(sending):
        def remote(src, dst, sem, dest):
            if sending:
                pltpu.make_async_remote_copy(
                    src_ref=src,
                    dst_ref=dst,
                    send_sem=send_sem.at[0],
                    recv_sem=sem,
                    device_id=dest,
                    device_id_type=MESH,
                ).start()
            else:
                pltpu.make_async_copy(src, src, send_sem.at[0]).wait()

        def local(src, dst, sem):
            if sending:
                pltpu.make_async_copy(src, dst, sem).start()

        def either(src, dst, sem, dest, mine):
            @pl.when(jnp.logical_not(mine))
            def _():
                remote(src, dst, sem, dest)

            @pl.when(mine)
            def _():
                local(src, dst, sem)

        def at_row(e):
            return r == e * (nr - 1)

        def at_col(e):
            return c == e * (nc - 1)

        def strips_to_rows(e):
            row = e * (nr - 1)

            @pl.when(is_row)
            def _():
                src = sp_row.at[tr, :, 0:packed_rows]
                to = jnp.minimum(c, nc - 1 - c)
                f = (c > to).astype(jnp.int32)
                for to, f in ((to, f), (nc - 1 - to, 1 - f)):
                    either(src, rx_row.at[4 * f + tr, :, 0:packed_rows], row_sem, (row, to), at_row(e) & (to == c))

            @pl.when(is_col)
            def _():
                g = jnp.minimum(r, nr - 1 - r)
                f = (r > g).astype(jnp.int32)
                for g, f in ((g, f), (nr - 1 - g, 1 - f)):
                    dst = rx_row.at[4 * f + 2 + tc, lax.rem(r, k), 0:packed_rows]
                    to = lax.div(g, k)
                    either(sp_col.at[tc, 0:packed_rows], dst, row_sem, (row, to), at_row(e) & (to == c))

        def strips_to_columns(e):
            col = e * (nc - 1)

            @pl.when(is_row)
            def _():
                for p in range(k):
                    extreme = (c == 0) if p == 0 else (c == nc - 1)
                    if k == 1:
                        extreme = extreme | (c == nc - 1)

                    def to_columns(p=p):
                        for f in (1, 0):
                            to = row_segment(f, p)
                            remote(st_row.at[tr, p], rx_col.at[4 * f + tr], col_sem, (to, col))

                    if 0 < p < k - 1:
                        to_columns()
                    else:
                        pl.when(jnp.logical_not(extreme))(to_columns)

            @pl.when(is_col & jnp.logical_not(is_row))
            def _():
                src = st_col.at[tc]
                remote(src, rx_col.at[6 + tc], col_sem, (nr - 1 - r, col))
                either(src, rx_col.at[2 + tc], col_sem, (r, col), at_col(e))

        def ends(e):
            row, col = e * (nr - 1), e * (nc - 1)
            for f in (1, 0):
                for h in range(2):
                    d = 1 if h != f else -1
                    end = 0 if d == 1 else 1

                    @pl.when(is_row)
                    def _():
                        slot = 4 * f + tr
                        for p in range(k):
                            outer_end = p == (k - 1 if h == 1 else 0)

                            def one_end(p=p, outer_end=outer_end):
                                src = ex_row.at[tr, p, h, 0:used]
                                if outer_end:
                                    to = clamp((c if f == 0 else nc - 1 - c) + d, nc)
                                    dst = ry_row.at[end, slot, 0:used]
                                    sem = row_end_sem.at[end]
                                    if f == 0:
                                        remote(src, dst, sem, (row, to))
                                    else:
                                        either(src, dst, sem, (row, to), at_row(e) & (to == c))
                                to = clamp(row_segment(f, p) + d, nr)
                                dst = ry_col.at[end, slot, 0:used]
                                sem = col_end_sem.at[end]
                                either(src, dst, sem, (to, col), at_col(e) & (to == r))

                            if outer_end:
                                pl.when(col_ok[h])(one_end)
                            else:
                                one_end()

                    @pl.when(is_col & row_ok[h])
                    def _():
                        slot = 4 * f + 2 + tc
                        src = ex_col.at[tc, h, 0:used]
                        g = col_segment(f)

                        def crossing():
                            to = clamp(lax.div(g, k) + d, nc)
                            dst = ry_row.at[end, slot, 0:used]
                            sem = row_end_sem.at[end]
                            either(src, dst, sem, (row, to), at_row(e) & (to == c))

                        if k == 1:
                            crossing()
                        else:
                            pl.when(lax.rem(g, k) == (k - 1 if d == 1 else 0))(crossing)
                        to = clamp(g + d, nr)
                        dst = ry_col.at[end, slot, 0:used]
                        sem = col_end_sem.at[end]
                        if f == 0:
                            remote(src, dst, sem, (to, col))
                        else:
                            either(src, dst, sem, (to, col), at_col(e) & (to == r))

        def within(s):
            @pl.when(row_ok[s])
            def _():
                remote(st_row.at[s], nb_row.at[1 - s], nb_sem.at[1 - s], (r + 2 * s - 1, c))

            @pl.when(col_ok[s])
            def _():
                remote(st_col.at[s], nb_col.at[1 - s], nb_sem.at[3 - s], (r, c + 2 * s - 1))

            for w in range(2):
                at = 2 * (1 - s) + 1 - w

                @pl.when(row_ok[s] & col_ok[w])
                def _():
                    remote(
                        ex_row.at[s, w * (k - 1), w, 0:used],
                        corner.at[at, 0:used],
                        corner_sem.at[at],
                        (r + 2 * s - 1, c + 2 * w - 1),
                    )

        strips_to_rows(0)
        if sending:
            stage_ends()
            stage_strips()
        ends(0)
        within(0)
        strips_to_rows(1)
        strips_to_columns(0)
        strips_to_columns(1)
        ends(1)
        within(1)

    fields = (gain_hbm, vert_hbm, den_hbm, res_hbm)
    for pair in range(2):
        for p in range(panels):
            for i in (2 * pair, 2 * pair + 1):
                pltpu.make_async_copy(fields[i].at[p], inp.at[i, p], in_sem.at[pair]).start()
    table_loads = [
        pltpu.make_async_copy(source, tables.at[i], table_sem.at[0])
        for i, source in enumerate((panel_hbm, side_hbm, flip_hbm))
    ]
    for load in table_loads:
        load.start()

    barrier = pltpu.get_barrier_semaphore()
    far_r, near_r = (1 - tr) * (nr - 1), tr * (nr - 1)
    far_c, near_c = (1 - tc) * (nc - 1), tc * (nc - 1)

    def greet(dest):
        pl.semaphore_signal(barrier, inc=1, device_id=dest, device_id_type=MESH)

    def number(flag):
        return flag.astype(jnp.int32)

    def row_greetings():
        found = []
        for near in (False, True):
            for f in (1, 0):
                here = c if f == 0 else nc - 1 - c
                for d in (0, -1, 1):
                    if near and f == 0 and d == 0:
                        continue
                    ok = None if d == 0 else (here > 0) if d == -1 else (here < nc - 1)
                    mine = (here + d == c) if near and f == 1 and d else None
                    found.append((ok, mine, (near_r if near else far_r, clamp(here + d, nc))))
        for d in range(-1, k + 1):
            for f in (1, 0):
                low = row_segment(f, 0 if f == 0 else k - 1)
                for near in (False, True):
                    ok = None if 0 <= d < k else (low > 0) if d == -1 else (low + d < nr)
                    mine = (is_col & (low + d == r)) if near else None
                    found.append((ok, mine, (clamp(low + d, nr), near_c if near else far_c)))
        return found

    def col_greetings():
        found = []
        for near in (False, True):
            for f in (1, 0):
                g = col_segment(f)
                for d in (0, -1, 1):
                    inside = None if d == 0 else (g > 0) if d == -1 else (g < nr - 1)
                    if not (near and f == 0 and d == 0):
                        mine = (g + d == r) if near and f == 1 and d else None
                        found.append((inside, mine, (clamp(g + d, nr), near_c if near else far_c)))
                    cross = inside
                    if d and k > 1:
                        cross = inside & (lax.rem(g, k) == (k - 1 if d == 1 else 0))
                    to = lax.div(g, k) + d
                    mine = (is_row & (to == c)) if near else None
                    found.append((cross, mine, (near_r if near else far_r, clamp(to, nc))))
        return found

    def near_greetings():
        found = []
        for dr in (-1, 0, 1):
            for dc in (-1, 0, 1):
                if dr or dc:
                    ok = row_ok[(dr + 1) // 2] if dr else None
                    if dc:
                        side = col_ok[(dc + 1) // 2]
                        ok = side if ok is None else ok & side
                    found.append((ok, None, (r + dr, c + dc)))
        return found

    def announce(found):
        total = jnp.int32(0)
        for ok, mine, dest in found:
            go = ok
            if mine is not None:
                go = jnp.logical_not(mine) if go is None else go & jnp.logical_not(mine)
            if go is None:
                total = total + 1
            else:
                total = total + number(go)
        return total

    def tell(found):
        for ok, mine, dest in found:
            go = ok
            if mine is not None:
                go = jnp.logical_not(mine) if go is None else go & jnp.logical_not(mine)
            if go is None:
                greet(dest)
            else:
                pl.when(go)(functools.partial(greet, dest))

    pl.when(is_row)(lambda: tell(row_greetings()))
    pl.when(is_col)(lambda: tell(col_greetings()))
    tell(near_greetings())
    expected = announce(near_greetings())
    expected = expected + jnp.where(is_row, announce(row_greetings()), 0)
    expected = expected + jnp.where(is_col, announce(col_greetings()), 0)

    lane = lax.broadcasted_iota(jnp.int32, (TILE, LANES), 1)
    sub = lax.broadcasted_iota(jnp.int32, (height, LANES), 0)
    level = lane[:1] % levels
    first_level = level == 0
    last_level = level == levels - 1

    def lower(x):
        return jnp.where(first_level, 0.0, pltpu.roll(x, 1, 1))

    def upper(x):
        return jnp.where(last_level, 0.0, pltpu.roll(x, LANES - 1, 1))

    def pick_tables(side):
        index = lane
        code = jnp.zeros_like(lane)
        for p in range(panels):
            here = lane // levels == p
            index = jnp.where(here, tables[0, side, p] * levels + lane % levels, index)
            code = jnp.where(here, tables[2, side, p] * 4 + tables[1, side, p], code)
        chunk = index // spare
        return index, code, jnp.where(lane < full, full + index - chunk * spare, lane), chunk

    def pack(value):
        filler = jnp.zeros((rows, cols, LANES - panels * levels), jnp.float32)
        return jnp.concatenate([value[p] for p in range(panels)] + [filler], axis=-1)

    def split(which, value):
        packed[which, :, :cols, :] = value
        if packed.shape[2] > cols:
            packed[which, :, cols:, :] = jnp.zeros(
                (rows, packed.shape[2] - cols, LANES), jnp.float32
            )
        return [
            [packed[which, y, pl.ds(b, height, stride=2), :] for b in range(2)]
            for y in range(rows)
        ]

    def fine(fun):
        return [[fun(y, b) for b in range(2)] for y in range(rows)]

    small = range(half_r)

    def block_mean(values, i):
        y = 2 * i
        return 0.25 * (values[y][0] + values[y][1] + values[y + 1][0] + values[y + 1][1])

    pltpu.make_async_copy(inp.at[0:2], inp.at[0:2], in_sem.at[0]).wait()
    gain = split(1, pack(inp[0]))
    vertical = split(2, pack(inp[1]))
    low_vert = fine(lambda y, b: lower(vertical[y][b]))
    inverse = fine(
        lambda y, b: relaxation / (gain[y][b] + 4.0 + vertical[y][b] + low_vert[y][b])
    )
    c_vert = [block_mean(vertical, i) for i in small]
    c_low = [lower(c_vert[i]) for i in small]
    c_inv = [relaxation / (block_mean(gain, i) + 1.0 + c_vert[i] + c_low[i]) for i in small]
    pltpu.make_async_copy(inp.at[2:4], inp.at[2:4], in_sem.at[1]).wait()
    right_side = split(0, pack(inp[2] * inp[3]))
    smoothed = fine(lambda y, b: inverse[y][b] * right_side[y][b])

    def inner(y, b):
        x = smoothed[y][b]
        return vertical[y][b] * upper(x) + low_vert[y][b] * lower(x)

    coupled = fine(inner)
    column = fine(lambda y, b: coupled[y][b] + (1.0 - relaxation) * right_side[y][b])
    north = [smoothed[2 * i][0] + smoothed[2 * i][1] for i in small]
    south = [smoothed[2 * i + 1][0] + smoothed[2 * i + 1][1] for i in small]
    west = [smoothed[2 * i][0] + smoothed[2 * i + 1][0] for i in small]
    east = [smoothed[2 * i][1] + smoothed[2 * i + 1][1] for i in small]
    from_w = [pltpu.roll(east[i], 1, 0) for i in small]
    from_e = [pltpu.roll(west[i], height - 1, 0) for i in small]
    start_w = sub % length == 0
    start_e = sub % length == last
    edge_w = sub == 0
    edge_e = sub == half_c - 1

    def bare(i):
        total = block_mean(column, i) + 0.5 * (north[i] + south[i])
        beside = None
        if i > 0:
            beside = south[i - 1]
        if i < half_r - 1:
            beside = north[i + 1] if beside is None else beside + north[i + 1]
        return total if beside is None else total + 0.25 * beside

    plain = [bare(i) for i in small]

    def partial_guess(i, mask_w, mask_e):
        beside = jnp.where(mask_w, 0.0, from_w[i]) + jnp.where(mask_e, 0.0, from_e[i])
        return c_inv[i] * (plain[i] + 0.25 * beside)

    by_tile = [partial_guess(i, edge_w, edge_e) for i in small]
    by_piece = by_tile if k == 1 else [partial_guess(i, start_w, start_e) for i in small]

    def put(ref, at, value):
        ref[at : at + value.shape[0], :] = value

    def press(ref, runs, singles):
        for at, run in enumerate(runs):
            put(ref, at * length, run)
        singles = jnp.concatenate(singles + [jnp.zeros((TILE - used, LANES), jnp.float32)], axis=0)
        for j in range(full // spare):
            moved = pltpu.roll(singles, full - spare * j, 1)
            ref[used * j : used * (j + 1), full:] = moved[:used, full:]

    for s in range(2):
        y = s * (rows - 1)
        i0, i1 = (0, 1) if s == 0 else (half_r - 1, half_r - 2)
        out = north[0] if s == 0 else south[half_r - 1]
        for p in range(k):
            lo, hi = p * length, p * length + last
            seg = slice(lo, hi + 1)
            one = lambda x, j: x[j : j + 1]
            parts = (smoothed[y][0], smoothed[y][1], by_piece[i0], by_piece[i1])
            press(
                sp_row.at[s, p],
                [x[seg] for x in parts + (c_inv[i0], c_vert[i0])],
                [one(c_inv[i1], lo), one(c_inv[i1], hi)]
                + [one(west[i0], lo), one(east[i0], hi), one(west[i1], lo), one(east[i1], hi)],
            )
    for s in range(2):
        j0, j1 = (0, 1) if s == 0 else (half_c - 1, half_c - 2)
        out = west if s == 0 else east
        at0 = lambda x: x[j0 : j0 + 1]
        at1 = lambda x: x[j1 : j1 + 1]
        parts = [
            [at0(smoothed[2 * i][s]) for i in small],
            [at0(smoothed[2 * i + 1][s]) for i in small],
            [at0(x) for x in by_tile],
            [at1(x) for x in by_tile],
            [at0(x) for x in c_inv],
            [at0(x) for x in c_vert],
        ]
        press(
            sp_col.at[s],
            [jnp.concatenate(x, axis=0) for x in parts],
            [at1(c_inv[0]), at1(c_inv[half_r - 1]), at0(north[0]), at0(south[half_r - 1])]
            + [at1(north[0]), at1(south[half_r - 1])],
        )

    def stage_strips():
        for s in range(2):
            y = s * (rows - 1)
            i0, i1 = (0, 1) if s == 0 else (half_r - 1, half_r - 2)
            out = north[0] if s == 0 else south[half_r - 1]
            for p in range(k):
                lo, hi = p * length, p * length + last
                seg = slice(lo, hi + 1)
                one = lambda x, j: x[j : j + 1]
                a, b, g = (st_row.at[s, p, q] for q in range(3))
                put(a, 0, smoothed[y][0][seg])
                put(a, length, smoothed[y][1][seg])
                put(a, 2 * length, one(c_inv[i1], lo))
                put(a, 2 * length + 1, one(c_inv[i1], hi))
                put(b, 0, by_piece[i0][seg])
                put(b, length, by_piece[i1][seg])
                put(b, 2 * length, one(west[i0], lo))
                put(b, 2 * length + 1, one(east[i0], hi))
                put(g, 0, c_inv[i0][seg])
                put(g, length, c_vert[i0][seg])
                put(g, 2 * length, one(west[i1], lo))
                put(g, 2 * length + 1, one(east[i1], hi))
        for s in range(2):
            j0, j1 = (0, 1) if s == 0 else (half_c - 1, half_c - 2)
            out = west if s == 0 else east
            a, b, g = (st_col.at[s, q] for q in range(3))
            at0 = lambda x: x[j0 : j0 + 1]
            at1 = lambda x: x[j1 : j1 + 1]
            for y in range(rows):
                put(a, (y % 2) * length + y // 2, at0(smoothed[y][s]))
            put(a, 2 * length, at1(c_inv[0]))
            put(a, 2 * length + 1, at1(c_inv[half_r - 1]))
            for i in small:
                put(b, i, at0(by_tile[i]))
                put(b, length + i, at1(by_tile[i]))
                put(g, i, at0(c_inv[i]))
                put(g, length + i, at0(c_vert[i]))
            put(b, 2 * length, at0(north[0]))
            put(b, 2 * length + 1, at0(south[half_r - 1]))
            put(g, 2 * length, at1(north[0]))
            put(g, 2 * length + 1, at1(south[half_r - 1]))

    def stage_ends():
        for s in range(2):
            i0, i1 = (0, 1) if s == 0 else (half_r - 1, half_r - 2)
            out = north[0] if s == 0 else south[half_r - 1]
            for p in range(k):
                lo, hi = p * length, p * length + last
                one = lambda x, j: x[j : j + 1]
                for h in range(2):
                    j, j1 = (lo, lo + 1) if h == 0 else (hi, hi - 1)
                    side = west if h == 0 else east
                    x = ex_row.at[s, p, h]
                    put(x, 0, one(by_piece[i0], j))
                    put(x, 1, one(c_inv[i0], j))
                    put(x, 2, one(side[i0], j))
                    put(x, 3, one(side[i1], j))
                    put(x, 4, one(out, j))
                    put(x, 5, one(out, j1))
        for s in range(2):
            j0, j1 = (0, 1) if s == 0 else (half_c - 1, half_c - 2)
            out = west if s == 0 else east
            at0 = lambda x: x[j0 : j0 + 1]
            at1 = lambda x: x[j1 : j1 + 1]
            for h in range(2):
                i0, i1 = (0, 1) if h == 0 else (half_r - 1, half_r - 2)
                side = north[0] if h == 0 else south[half_r - 1]
                x = ex_col.at[s, h]
                put(x, 0, at0(by_tile[i0]))
                put(x, 1, at0(c_inv[i0]))
                put(x, 2, at0(side))
                put(x, 3, at1(side))
                put(x, 4, at0(out[i0]))
                put(x, 5, at0(out[i1]))

    pl.semaphore_wait(barrier, expected)
    traffic(True)

    def beside(y, b):
        x = smoothed[y][b]
        total = coupled[y][b] + smoothed[y][1 - b]
        if y > 0:
            total = total + smoothed[y - 1][b]
        if y < rows - 1:
            total = total + smoothed[y + 1][b]
        return total

    partial = fine(beside)
    traffic(False)

    pltpu.make_async_copy(tables, tables, table_sem.at[0]).wait()
    row_pick = pick_tables(tr)
    col_pick = pick_tables(2 + tc)

    def arrived(ref, sem):
        pltpu.make_async_copy(ref, ref, sem).wait()

    order = list(range(2 * length))[::-1] + [2 * length + 1, 2 * length]
    other = (
        list(range(length))[::-1]
        + list(range(length, 2 * length))[::-1]
        + [2 * length + 1, 2 * length]
    )
    sublane = lax.broadcasted_iota(jnp.int32, (block, LANES), 0)

    def flip_index(perm):
        index = sublane
        for at, source in enumerate(perm):
            index = jnp.where(sublane == at, source, index)
        return index

    flips = [flip_index(order), flip_index(other), flip_index(other)]

    def choose(read, pick, f, second=False):
        index, code = pick[2 if second else 0], pick[1]
        taken = None
        for t in range(4):
            moved = jnp.take_along_axis(read(4 * f + t), index, axis=1, mode="promise_in_bounds")
            taken = moved if taken is None else jnp.where(code == 4 * f + t, moved, taken)
        return taken

    def select(plainly, reverse, pick, group):
        straight = choose(plainly, pick, 0)
        turned = choose(reverse, pick, 1)
        if group is not None:
            turned = jnp.take_along_axis(turned, flips[group], axis=0, mode="promise_in_bounds")
        return jnp.where(pick[1] >= 4, turned, straight)

    def rows_of(tiles, first, final):
        parts = []
        for q, tile in enumerate(tiles):
            lo, hi = max(first, q * TILE), min(final, (q + 1) * TILE)
            if lo < hi:
                parts.append(tile[lo - q * TILE : hi - q * TILE])
        return parts

    def select_packed(plainly, reverse, pick):
        tiles = range(-(-packed_rows // TILE))
        results = []
        for f, read in ((0, plainly), (1, reverse)):
            main = [choose(lambda s: read(s, q), pick, f) for q in tiles]
            extra = [choose(lambda s: read(s, q), pick, f, True) for q in tiles]
            singles = None
            for j in range(full // spare):
                part = jnp.concatenate(rows_of(extra, used * j, used * (j + 1)), axis=0)
                same = pick[3][:used] == j
                singles = part if singles is None else jnp.where(same, part, singles)
            groups = []
            for q in range(3):
                lines = rows_of(main, 2 * length * q, 2 * length * (q + 1))
                lines.append(singles[2 * q : 2 * q + 2])
                if block > 2 * length + 2:
                    lines.append(jnp.zeros((block - 2 * length - 2, LANES), jnp.float32))
                groups.append(jnp.concatenate(lines, axis=0))
            results.append(groups)
        turned = [
            jnp.take_along_axis(x, flips[q], axis=0, mode="promise_in_bounds")
            for q, x in enumerate(results[1])
        ]
        return [jnp.where(pick[1] >= 4, x, y) for x, y in zip(turned, results[0])]

    @pl.when(is_row)
    def _():
        arrived(rx_row.at[:, :, 0:packed_rows], row_sem)
        for p in range(k):
            value = select_packed(
                lambda s, q: rx_row[s, p, q * TILE : (q + 1) * TILE],
                lambda s, q: rx_row[s, k - 1 - p, q * TILE : (q + 1) * TILE],
                row_pick,
            )
            for q in range(3):
                nb_row[tr, p, q] = value[q]
        for w in range(2):

            @pl.when(col_ok[w])
            def _():
                arrived(ry_row.at[w, :, 0:used], row_end_sem.at[w])
                read = lambda s: ry_row[w, s]
                corner[2 * tr + w] = select(read, read, row_pick, None)

    @pl.when(is_col & jnp.logical_not(is_row))
    def _():
        arrived(rx_col, col_sem)
        for q in range(3):
            read = lambda s: rx_col[s, q]
            nb_col[tc, q] = select(read, read, col_pick, q)

    @pl.when(is_col & is_row)
    def _():
        swap = (tr != tc).astype(jnp.int32)

        def read(s, q):
            f, t = s // 4, s % 4
            at = 4 * (1 - swap) + t if f == 1 else 4 * swap + t
            piece = (tr if f == 0 else 1 - tr) * (k - 1)
            return rx_row[at, piece, q * TILE : (q + 1) * TILE]

        value = select_packed(read, read, col_pick)
        for q in range(3):
            nb_col[tc, q] = value[q]

    @pl.when(is_col)
    def _():
        for s in range(2):

            @pl.when(row_ok[s])
            def _():
                arrived(ry_col.at[s, :, 0:used], col_end_sem.at[s])
                read = lambda slot: ry_col[s, slot]
                value = select(read, read, col_pick, None)
                corner[2 * s + tc, 0:2, :] = value[0:2]
                corner[2 * s + tc, 2:4, :] = value[4:6]
                corner[2 * s + tc, 4:6, :] = value[2:4]

    for s in range(2):

        @pl.when(row_ok[s])
        def _():
            arrived(nb_row.at[s], nb_sem.at[s])

        @pl.when(col_ok[s])
        def _():
            arrived(nb_col.at[s], nb_sem.at[2 + s])

        for w in range(2):

            @pl.when(row_ok[s] & col_ok[w])
            def _():
                arrived(corner.at[2 * s + w, 0:used], corner_sem.at[2 * s + w])

    @pl.when(is_row & is_col)
    def _():
        at = 2 * tr + tc
        corner[at, 0:2, :] = jnp.zeros((2, LANES), jnp.float32)
        for q in range(2):
            rows_z = nb_col[tc, 1 + q]
            rows_x = nb_row[tr, tc * (k - 1), 1 + q]
            corner[at, 2 + q : 3 + q, :] = jnp.where(
                tr == 0, rows_z[2 * length : 2 * length + 1], rows_z[2 * length + 1 : 2 * length + 2]
            )
            corner[at, 4 + q : 5 + q, :] = jnp.where(
                tc == 0, rows_x[2 * length : 2 * length + 1], rows_x[2 * length + 1 : 2 * length + 2]
            )

    def zeros(count):
        return [jnp.zeros((count, LANES), jnp.float32)] if count else []

    def stack(lines, total):
        used = sum(x.shape[0] for x in lines)
        return jnp.concatenate(list(lines) + zeros(total - used), axis=0)

    tall_z = round_up(half_r, TILE)
    flat = 2 * length

    class Strip:
        pass

    def strip(read, pieces, ends, total, own):
        def gather(q, at):
            return stack([read(p, q, slice(at, at + length)) for p in range(pieces)], total)

        def sides(first, final):
            lines = []
            for p in range(pieces):
                lines += [first(p)] + zeros(length - 2) + [final(p)]
            return stack(lines, total)

        def lateral(q):
            return sides(
                lambda p: ends[0][q] if p == 0 else read(p - 1, 1 + q, slice(flat + 1, flat + 2)),
                lambda p: ends[1][q]
                if p == pieces - 1
                else read(p + 1, 1 + q, slice(flat, flat + 1)),
            )

        x = Strip()
        x.even, x.odd = gather(0, 0), gather(0, length)
        x.pair = x.even + x.odd
        inv1 = sides(
            lambda p: read(p, 0, slice(flat, flat + 1)),
            lambda p: read(p, 0, slice(flat + 1, flat + 2)),
        )
        x.inv, x.vert = gather(2, 0), gather(2, length)
        x.guess = gather(1, 0) + 0.25 * x.inv * (lateral(0) + own)
        x.inside = gather(1, length) + 0.25 * inv1 * lateral(1)
        return x

    def corner_row(s, w, at):
        return corner[2 * s + w, at : at + 1, :]

    row_strip = []
    for s in range(2):
        own = north[0] if s == 0 else south[half_r - 1]
        ends = [[corner_row(s, w, 2 + q) for q in range(2)] for w in range(2)]
        row_strip.append(
            strip(lambda p, q, rows_: nb_row[s, p, q, rows_, :], k, ends, height, own)
        )
    col_strip = []
    for w in range(2):
        j = w * (half_c - 1)
        faces = west if w == 0 else east
        own = stack([faces[i][j : j + 1] for i in small], tall_z)
        ends = [[corner_row(s, w, 4 + q) for q in range(2)] for s in range(2)]
        col_strip.append(
            strip(lambda p, q, rows_: nb_col[w, q, rows_, :], 1, ends, tall_z, own)
        )

    guess = []
    for i in small:
        lateral = jnp.where(edge_w, col_strip[0].pair[i : i + 1], 0.0)
        lateral = lateral + jnp.where(edge_e, col_strip[1].pair[i : i + 1], 0.0)
        if i == 0:
            lateral = lateral + row_strip[0].pair
        if i == half_r - 1:
            lateral = lateral + row_strip[1].pair
        guess.append(by_tile[i] + 0.25 * c_inv[i] * lateral)

    row_side = [[None] * 2 for _ in range(2)]
    col_side = [[None] * 2 for _ in range(2)]
    for s in range(2):
        for w in range(2):
            faces = nb_row[s, w * (k - 1), 1, flat + w : flat + w + 1, :]
            faces = faces + nb_col[w, 1, flat + s : flat + s + 1, :]
            there = corner_row(s, w, 0) + 0.25 * corner_row(s, w, 1) * faces
            tip = (r == s * (nr - 1)) & (c == w * (nc - 1))
            jr, jc = w * (half_c - 1), s * (half_r - 1)
            row_side[s][w] = jnp.where(tip, col_strip[w].guess[jc : jc + 1], there)
            col_side[w][s] = jnp.where(tip, row_strip[s].guess[jr : jr + 1], there)

    def relax(x, ends, own, count):
        total = x.guess.shape[0]
        at = lax.broadcasted_iota(jnp.int32, (total, LANES), 0)
        around = x.inside + own
        around = around + jnp.where(at == 0, ends[0], pltpu.roll(x.guess, 1, 0))
        around = around + jnp.where(at == count - 1, ends[1], pltpu.roll(x.guess, total - 1, 0))
        column = x.vert * upper(x.guess) + lower(x.vert) * lower(x.guess)
        return (2.0 - relaxation) * x.guess + x.inv * (0.25 * around + column)

    row_fix = [
        relax(row_strip[s], row_side[s], guess[s * (half_r - 1)], half_c) for s in range(2)
    ]
    col_fix = []
    for w in range(2):
        j = w * (half_c - 1)
        own = stack([guess[i][j : j + 1] for i in small], tall_z)
        col_fix.append(relax(col_strip[w], col_side[w], own, half_r))

    def from_left(x, line):
        return jnp.where(edge_w, line, pltpu.roll(x, 1, 0))

    def from_right(x, line):
        return jnp.where(edge_e, line, pltpu.roll(x, height - 1, 0))

    correction = []
    for i in small:
        x = guess[i]
        around = from_left(x, col_strip[0].guess[i : i + 1])
        around = around + from_right(x, col_strip[1].guess[i : i + 1])
        around = around + (guess[i - 1] if i > 0 else row_strip[0].guess)
        around = around + (guess[i + 1] if i < half_r - 1 else row_strip[1].guess)
        levels_part = c_vert[i] * upper(x) + c_low[i] * lower(x)
        correction.append((2.0 - relaxation) * x + c_inv[i] * (0.25 * around + levels_part))
        small_ref[i] = correction[i]

    def outer(y, b):
        at = (y % 2) * length + y // 2
        source = col_strip[b]
        line = (source.even if y % 2 == 0 else source.odd)[y // 2 : y // 2 + 1]
        if b == 0:
            total = partial[y][b] + from_left(smoothed[y][1], line)
        else:
            total = partial[y][b] + from_right(smoothed[y][0], line)
        if y == 0:
            total = total + (row_strip[0].even if b == 0 else row_strip[0].odd)
        if y == rows - 1:
            total = total + (row_strip[1].even if b == 0 else row_strip[1].odd)
        return total

    c_up = [upper(x) for x in correction]
    c_down = [lower(x) for x in correction]
    left = [from_left(correction[i], col_fix[0][i : i + 1]) for i in small]
    right = [from_right(correction[i], col_fix[1][i : i + 1]) for i in small]
    for y in range(rows):
        i = y // 2
        next_i = i - 1 if y % 2 == 0 else i + 1
        for b in range(2):
            total = outer(y, b) + 2.0 * correction[i]
            total = total + vertical[y][b] * c_up[i] + low_vert[y][b] * c_down[i]
            if next_i < 0:
                total = total + row_fix[0]
            elif next_i >= half_r:
                total = total + row_fix[1]
            else:
                total = total + correction[next_i]
            total = total + (left if b == 0 else right)[i]
            first = (2.0 - relaxation) * smoothed[y][b] + (1.0 - relaxation) * correction[i]
            spread[y, pl.ds(b, height, stride=2), :] = first + inverse[y][b] * total


def unpack(spread, small_ref, sol_hbm, corr_hbm, sol, corr, sem):
    panels, _, cols, levels = sol.shape
    half_c = corr.shape[2]
    for p in range(panels):
        lanes = slice(p * levels, (p + 1) * levels)
        sol[p] = spread[:, :cols, lanes]
        pltpu.make_async_copy(sol.at[p], sol_hbm.at[p], sem.at[0]).start()
    for p in range(panels):
        lanes = slice(p * levels, (p + 1) * levels)
        corr[p] = small_ref[:, :half_c, lanes]
    last = pltpu.make_async_copy(corr, corr_hbm, sem.at[1])
    last.start()
    pltpu.make_async_copy(sol, sol_hbm, sem.at[0]).wait()
    last.wait()


def solution(mesh):
    nr, nc = mesh.shape["tx"], mesh.shape["ty"]

    def shards(residual, density, gain, vertical, edge_panel, edge_side, edge_flip):
        panels, rows, cols, levels = residual.shape
        k = cols // rows
        assert cols == k * rows and rows % 2 == 0 and panels * levels <= LANES
        assert rows >= 6 and nr > 1 and nc > 1
        block = round_up(rows + 2, TILE)
        dense = round_up(3 * rows, TILE)
        spare = LANES - panels * levels
        assert spare % levels == 0 and panels * levels % spare == 0
        assert 2 * panels * levels <= rows * spare
        height = round_up(cols // 2, TILE)
        tall = 2 * height
        f32 = jnp.float32
        spread, small = pl.pallas_call(
            functools.partial(kernel, nr, nc),
            out_shape=(
                pltpu.VMEM((rows, tall, LANES), f32),
                pltpu.VMEM((rows // 2, height, LANES), f32),
            ),
            in_specs=[pl.BlockSpec(memory_space=pl.ANY)] * 7,
            out_specs=(pl.BlockSpec(memory_space=pltpu.VMEM),) * 2,
            scratch_shapes=[
                pltpu.VMEM((4, panels, rows, cols, levels), f32),
                pltpu.SMEM((3,) + edge_panel.T.shape, jnp.int32),
                pltpu.VMEM((3, rows, tall, LANES), f32),
                pltpu.VMEM((3, k, 3, block, LANES), f32),
                pltpu.VMEM((3, 3, block, LANES), f32),
                pltpu.VMEM((3, k, dense, LANES), f32),
                pltpu.VMEM((3, dense, LANES), f32),
                pltpu.VMEM((3, k, 2, TILE, LANES), f32),
                pltpu.VMEM((3, 2, TILE, LANES), f32),
                pltpu.VMEM((3, k, 3, block, LANES), f32),
                pltpu.VMEM((3, 3, block, LANES), f32),
                pltpu.VMEM((5, TILE, LANES), f32),
                pltpu.VMEM((8, k, dense, LANES), f32),
                pltpu.VMEM((8, 3, block, LANES), f32),
                pltpu.VMEM((2, 8, TILE, LANES), f32),
                pltpu.VMEM((2, 8, TILE, LANES), f32),
                pltpu.SemaphoreType.DMA((2,)),
                pltpu.SemaphoreType.DMA((1,)),
                pltpu.SemaphoreType.DMA((1,)),
                pltpu.SemaphoreType.DMA((4,)),
                pltpu.SemaphoreType.DMA((4,)),
                pltpu.SemaphoreType.DMA,
                pltpu.SemaphoreType.DMA,
                pltpu.SemaphoreType.DMA((2,)),
                pltpu.SemaphoreType.DMA((2,)),
            ],
            compiler_params=pltpu.CompilerParams(collective_id=0, has_side_effects=True),
        )(residual, density, gain, vertical, edge_panel.T, edge_side.T, edge_flip.T)
        spread = pltpu.with_memory_space_constraint(spread, pltpu.VMEM)
        small = pltpu.with_memory_space_constraint(small, pltpu.VMEM)
        return pl.pallas_call(
            unpack,
            out_shape=(
                jax.ShapeDtypeStruct(residual.shape, f32),
                jax.ShapeDtypeStruct((panels, rows // 2, cols // 2, levels), f32),
            ),
            in_specs=[pl.BlockSpec(memory_space=pltpu.VMEM)] * 2,
            out_specs=(pl.BlockSpec(memory_space=pl.ANY),) * 2,
            scratch_shapes=[
                pltpu.VMEM(residual.shape, f32),
                pltpu.VMEM((panels, rows // 2, cols // 2, levels), f32),
                pltpu.SemaphoreType.DMA((2,)),
            ],
        )(spread, small)

    fields = P(None, "tx", "ty", None)
    return jax.shard_map(
        shards,
        mesh=mesh,
        in_specs=(fields,) * 4 + (P(),) * 3,
        out_specs=(fields, fields),
        check_vma=False,
    )
```

```python
import functools

import jax
import jax.numpy as jnp
from jax import lax
from jax.experimental import pallas as pl
from jax.experimental.pallas import tpu as pltpu
from jax.sharding import PartitionSpec as P

MESH = pl.DeviceIdType.MESH
relaxation = 0.8
LANES = 128
TILE = 8


def round_up(value, unit):
    return (value + unit - 1) // unit * unit


def kernel(
    nr,
    nc,
    res_hbm,
    den_hbm,
    gain_hbm,
    vert_hbm,
    panel_hbm,
    side_hbm,
    flip_hbm,
    spread,
    small_ref,
    inp,
    tables,
    packed,
    st_row,
    st_col,
    sp_row,
    sp_col,
    ex_row,
    ex_col,
    nb_row,
    nb_col,
    corner,
    rx_row,
    rx_col,
    ry_row,
    ry_col,
    in_sem,
    table_sem,
    send_sem,
    nb_sem,
    corner_sem,
    row_sem,
    col_sem,
    row_end_sem,
    col_end_sem,
):
    _, panels, rows, cols, levels = inp.shape
    half_r, half_c = rows // 2, cols // 2
    k = cols // rows
    length = half_r
    last = length - 1
    height = spread.shape[1] // 2
    block = st_row.shape[3]
    r = lax.axis_index("tx")
    c = lax.axis_index("ty")
    is_row = (r == 0) | (r == nr - 1)
    is_col = (c == 0) | (c == nc - 1)
    tr = (r == nr - 1).astype(jnp.int32)
    tc = (c == nc - 1).astype(jnp.int32)
    row_ok = (r > 0, r < nr - 1)
    col_ok = (c > 0, c < nc - 1)

    def row_segment(f, p):
        return k * c + p if f == 0 else nr - 1 - k * c - p

    def col_segment(f):
        return r if f == 0 else nr - 1 - r

    def clamp(x, n):
        return jnp.minimum(jnp.maximum(x, 0), n - 1)

    used = 6
    full = panels * levels
    spare = LANES - full
    packed_rows = 3 * rows

    def traffic(sending):
        def remote(src, dst, sem, dest):
            if sending:
                pltpu.make_async_remote_copy(
                    src_ref=src,
                    dst_ref=dst,
                    send_sem=send_sem.at[0],
                    recv_sem=sem,
                    device_id=dest,
                    device_id_type=MESH,
                ).start()
            else:
                pltpu.make_async_copy(src, src, send_sem.at[0]).wait()

        def local(src, dst, sem):
            if sending:
                pltpu.make_async_copy(src, dst, sem).start()

        def either(src, dst, sem, dest, mine):
            @pl.when(jnp.logical_not(mine))
            def _():
                remote(src, dst, sem, dest)

            @pl.when(mine)
            def _():
                local(src, dst, sem)

        def at_row(e):
            return r == e * (nr - 1)

        def at_col(e):
            return c == e * (nc - 1)

        def strips_to_rows(e):
            row = e * (nr - 1)

            @pl.when(is_row)
            def _():
                src = sp_row.at[tr, :, 0:packed_rows]
                to = jnp.minimum(c, nc - 1 - c)
                f = (c > to).astype(jnp.int32)
                for to, f in ((to, f), (nc - 1 - to, 1 - f)):
                    either(src, rx_row.at[4 * f + tr, :, 0:packed_rows], row_sem, (row, to), at_row(e) & (to == c))

            @pl.when(is_col)
            def _():
                g = jnp.minimum(r, nr - 1 - r)
                f = (r > g).astype(jnp.int32)
                for g, f in ((g, f), (nr - 1 - g, 1 - f)):
                    dst = rx_row.at[4 * f + 2 + tc, lax.rem(r, k), 0:packed_rows]
                    to = lax.div(g, k)
                    either(sp_col.at[tc, 0:packed_rows], dst, row_sem, (row, to), at_row(e) & (to == c))

        def strips_to_columns(e):
            col = e * (nc - 1)

            @pl.when(is_row)
            def _():
                for p in range(k):
                    extreme = (c == 0) if p == 0 else (c == nc - 1)
                    if k == 1:
                        extreme = extreme | (c == nc - 1)

                    def to_columns(p=p):
                        for f in (1, 0):
                            to = row_segment(f, p)
                            remote(st_row.at[tr, p], rx_col.at[4 * f + tr], col_sem, (to, col))

                    if 0 < p < k - 1:
                        to_columns()
                    else:
                        pl.when(jnp.logical_not(extreme))(to_columns)

            @pl.when(is_col & jnp.logical_not(is_row))
            def _():
                src = st_col.at[tc]
                remote(src, rx_col.at[6 + tc], col_sem, (nr - 1 - r, col))
                either(src, rx_col.at[2 + tc], col_sem, (r, col), at_col(e))

        def ends(e):
            row, col = e * (nr - 1), e * (nc - 1)
            for f in (1, 0):
                for h in range(2):
                    d = 1 if h != f else -1
                    end = 0 if d == 1 else 1

                    @pl.when(is_row)
                    def _():
                        slot = 4 * f + tr
                        for p in range(k):
                            outer_end = p == (k - 1 if h == 1 else 0)

                            def one_end(p=p, outer_end=outer_end):
                                src = ex_row.at[tr, p, h, 0:used]
                                if outer_end:
                                    to = clamp((c if f == 0 else nc - 1 - c) + d, nc)
                                    dst = ry_row.at[end, slot, 0:used]
                                    sem = row_end_sem.at[end]
                                    if f == 0:
                                        remote(src, dst, sem, (row, to))
                                    else:
                                        either(src, dst, sem, (row, to), at_row(e) & (to == c))
                                to = clamp(row_segment(f, p) + d, nr)
                                dst = ry_col.at[end, slot, 0:used]
                                sem = col_end_sem.at[end]
                                either(src, dst, sem, (to, col), at_col(e) & (to == r))

                            if outer_end:
                                pl.when(col_ok[h])(one_end)
                            else:
                                one_end()

                    @pl.when(is_col & row_ok[h])
                    def _():
                        slot = 4 * f + 2 + tc
                        src = ex_col.at[tc, h, 0:used]
                        g = col_segment(f)

                        def crossing():
                            to = clamp(lax.div(g, k) + d, nc)
                            dst = ry_row.at[end, slot, 0:used]
                            sem = row_end_sem.at[end]
                            either(src, dst, sem, (row, to), at_row(e) & (to == c))

                        if k == 1:
                            crossing()
                        else:
                            pl.when(lax.rem(g, k) == (k - 1 if d == 1 else 0))(crossing)
                        to = clamp(g + d, nr)
                        dst = ry_col.at[end, slot, 0:used]
                        sem = col_end_sem.at[end]
                        if f == 0:
                            remote(src, dst, sem, (to, col))
                        else:
                            either(src, dst, sem, (to, col), at_col(e) & (to == r))

        def within(s):
            @pl.when(row_ok[s])
            def _():
                remote(st_row.at[s], nb_row.at[1 - s], nb_sem.at[1 - s], (r + 2 * s - 1, c))

            @pl.when(col_ok[s])
            def _():
                remote(st_col.at[s], nb_col.at[1 - s], nb_sem.at[3 - s], (r, c + 2 * s - 1))

            for w in range(2):
                at = 2 * (1 - s) + 1 - w

                @pl.when(row_ok[s] & col_ok[w])
                def _():
                    remote(
                        ex_row.at[s, w * (k - 1), w, 0:used],
                        corner.at[at, 0:used],
                        corner_sem.at[at],
                        (r + 2 * s - 1, c + 2 * w - 1),
                    )

        strips_to_rows(0)
        if sending:
            stage_ends()
        ends(0)
        within(0)
        strips_to_rows(1)
        strips_to_columns(0)
        strips_to_columns(1)
        ends(1)
        within(1)

    fields = (gain_hbm, vert_hbm, den_hbm, res_hbm)
    for pair in range(2):
        for p in range(panels):
            for i in (2 * pair, 2 * pair + 1):
                pltpu.make_async_copy(fields[i].at[p], inp.at[i, p], in_sem.at[pair]).start()
    table_loads = [
        pltpu.make_async_copy(source, tables.at[i], table_sem.at[0])
        for i, source in enumerate((panel_hbm, side_hbm, flip_hbm))
    ]
    for load in table_loads:
        load.start()

    barrier = pltpu.get_barrier_semaphore()
    far_r, near_r = (1 - tr) * (nr - 1), tr * (nr - 1)
    far_c, near_c = (1 - tc) * (nc - 1), tc * (nc - 1)

    def greet(dest):
        pl.semaphore_signal(barrier, inc=1, device_id=dest, device_id_type=MESH)

    def number(flag):
        return flag.astype(jnp.int32)

    def row_greetings():
        found = []
        for near in (False, True):
            for f in (1, 0):
                here = c if f == 0 else nc - 1 - c
                for d in (0, -1, 1):
                    if near and f == 0 and d == 0:
                        continue
                    ok = None if d == 0 else (here > 0) if d == -1 else (here < nc - 1)
                    mine = (here + d == c) if near and f == 1 and d else None
                    found.append((ok, mine, (near_r if near else far_r, clamp(here + d, nc))))
        for d in range(-1, k + 1):
            for f in (1, 0):
                low = row_segment(f, 0 if f == 0 else k - 1)
                for near in (False, True):
                    ok = None if 0 <= d < k else (low > 0) if d == -1 else (low + d < nr)
                    mine = (is_col & (low + d == r)) if near else None
                    found.append((ok, mine, (clamp(low + d, nr), near_c if near else far_c)))
        return found

    def col_greetings():
        found = []
        for near in (False, True):
            for f in (1, 0):
                g = col_segment(f)
                for d in (0, -1, 1):
                    inside = None if d == 0 else (g > 0) if d == -1 else (g < nr - 1)
                    if not (near and f == 0 and d == 0):
                        mine = (g + d == r) if near and f == 1 and d else None
                        found.append((inside, mine, (clamp(g + d, nr), near_c if near else far_c)))
                    cross = inside
                    if d and k > 1:
                        cross = inside & (lax.rem(g, k) == (k - 1 if d == 1 else 0))
                    to = lax.div(g, k) + d
                    mine = (is_row & (to == c)) if near else None
                    found.append((cross, mine, (near_r if near else far_r, clamp(to, nc))))
        return found

    def near_greetings():
        found = []
        for dr in (-1, 0, 1):
            for dc in (-1, 0, 1):
                if dr or dc:
                    ok = row_ok[(dr + 1) // 2] if dr else None
                    if dc:
                        side = col_ok[(dc + 1) // 2]
                        ok = side if ok is None else ok & side
                    found.append((ok, None, (r + dr, c + dc)))
        return found

    def announce(found):
        total = jnp.int32(0)
        for ok, mine, dest in found:
            go = ok
            if mine is not None:
                go = jnp.logical_not(mine) if go is None else go & jnp.logical_not(mine)
            if go is None:
                total = total + 1
            else:
                total = total + number(go)
        return total

    def tell(found):
        for ok, mine, dest in found:
            go = ok
            if mine is not None:
                go = jnp.logical_not(mine) if go is None else go & jnp.logical_not(mine)
            if go is None:
                greet(dest)
            else:
                pl.when(go)(functools.partial(greet, dest))

    pl.when(is_row)(lambda: tell(row_greetings()))
    pl.when(is_col)(lambda: tell(col_greetings()))
    tell(near_greetings())
    expected = announce(near_greetings())
    expected = expected + jnp.where(is_row, announce(row_greetings()), 0)
    expected = expected + jnp.where(is_col, announce(col_greetings()), 0)

    lane = lax.broadcasted_iota(jnp.int32, (TILE, LANES), 1)
    sub = lax.broadcasted_iota(jnp.int32, (height, LANES), 0)
    level = lane[:1] % levels
    first_level = level == 0
    last_level = level == levels - 1

    def lower(x):
        return jnp.where(first_level, 0.0, pltpu.roll(x, 1, 1))

    def upper(x):
        return jnp.where(last_level, 0.0, pltpu.roll(x, LANES - 1, 1))

    def pick_tables(side):
        index = lane
        code = jnp.zeros_like(lane)
        for p in range(panels):
            here = lane // levels == p
            index = jnp.where(here, tables[0, side, p] * levels + lane % levels, index)
            code = jnp.where(here, tables[2, side, p] * 4 + tables[1, side, p], code)
        chunk = index // spare
        return index, code, jnp.where(lane < full, full + index - chunk * spare, lane), chunk

    def pack(value):
        filler = jnp.zeros((rows, cols, LANES - panels * levels), jnp.float32)
        return jnp.concatenate([value[p] for p in range(panels)] + [filler], axis=-1)

    def split(which, value):
        packed[which, :, :cols, :] = value
        if packed.shape[2] > cols:
            packed[which, :, cols:, :] = jnp.zeros(
                (rows, packed.shape[2] - cols, LANES), jnp.float32
            )
        return [
            [packed[which, y, pl.ds(b, height, stride=2), :] for b in range(2)]
            for y in range(rows)
        ]

    def fine(fun):
        return [[fun(y, b) for b in range(2)] for y in range(rows)]

    small = range(half_r)

    def block_mean(values, i):
        y = 2 * i
        return 0.25 * (values[y][0] + values[y][1] + values[y + 1][0] + values[y + 1][1])

    pltpu.make_async_copy(inp.at[0:2], inp.at[0:2], in_sem.at[0]).wait()
    gain = split(1, pack(inp[0]))
    vertical = split(2, pack(inp[1]))
    low_vert = fine(lambda y, b: lower(vertical[y][b]))
    inverse = fine(
        lambda y, b: relaxation / (gain[y][b] + 4.0 + vertical[y][b] + low_vert[y][b])
    )
    c_vert = [block_mean(vertical, i) for i in small]
    c_low = [lower(c_vert[i]) for i in small]
    c_inv = [relaxation / (block_mean(gain, i) + 1.0 + c_vert[i] + c_low[i]) for i in small]
    pltpu.make_async_copy(inp.at[2:4], inp.at[2:4], in_sem.at[1]).wait()
    right_side = split(0, pack(inp[2] * inp[3]))
    smoothed = fine(lambda y, b: inverse[y][b] * right_side[y][b])

    def inner(y, b):
        x = smoothed[y][b]
        return vertical[y][b] * upper(x) + low_vert[y][b] * lower(x)

    coupled = fine(inner)
    column = fine(lambda y, b: coupled[y][b] + (1.0 - relaxation) * right_side[y][b])
    north = [smoothed[2 * i][0] + smoothed[2 * i][1] for i in small]
    south = [smoothed[2 * i + 1][0] + smoothed[2 * i + 1][1] for i in small]
    west = [smoothed[2 * i][0] + smoothed[2 * i + 1][0] for i in small]
    east = [smoothed[2 * i][1] + smoothed[2 * i + 1][1] for i in small]
    from_w = [pltpu.roll(east[i], 1, 0) for i in small]
    from_e = [pltpu.roll(west[i], height - 1, 0) for i in small]
    start_w = sub % length == 0
    start_e = sub % length == last
    edge_w = sub == 0
    edge_e = sub == half_c - 1

    def bare(i):
        total = block_mean(column, i) + 0.5 * (north[i] + south[i])
        beside = None
        if i > 0:
            beside = south[i - 1]
        if i < half_r - 1:
            beside = north[i + 1] if beside is None else beside + north[i + 1]
        return total if beside is None else total + 0.25 * beside

    plain = [bare(i) for i in small]

    def partial_guess(i, mask_w, mask_e):
        beside = jnp.where(mask_w, 0.0, from_w[i]) + jnp.where(mask_e, 0.0, from_e[i])
        return c_inv[i] * (plain[i] + 0.25 * beside)

    by_tile = [partial_guess(i, edge_w, edge_e) for i in small]
    by_piece = by_tile if k == 1 else [partial_guess(i, start_w, start_e) for i in small]

    def put(ref, at, value):
        ref[at : at + value.shape[0], :] = value

    def press(ref, runs, singles):
        for at, run in enumerate(runs):
            put(ref, at * length, run)
        singles = jnp.concatenate(singles + [jnp.zeros((TILE - used, LANES), jnp.float32)], axis=0)
        for j in range(full // spare):
            moved = pltpu.roll(singles, full - spare * j, 1)
            ref[used * j : used * (j + 1), full:] = moved[:used, full:]

    for s in range(2):
        y = s * (rows - 1)
        i0, i1 = (0, 1) if s == 0 else (half_r - 1, half_r - 2)
        out = north[0] if s == 0 else south[half_r - 1]
        for p in range(k):
            lo, hi = p * length, p * length + last
            seg = slice(lo, hi + 1)
            one = lambda x, j: x[j : j + 1]
            a, b, g = (st_row.at[s, p, q] for q in range(3))
            put(a, 0, smoothed[y][0][seg])
            put(a, length, smoothed[y][1][seg])
            put(a, 2 * length, one(c_inv[i1], lo))
            put(a, 2 * length + 1, one(c_inv[i1], hi))
            put(b, 0, by_piece[i0][seg])
            put(b, length, by_piece[i1][seg])
            put(b, 2 * length, one(west[i0], lo))
            put(b, 2 * length + 1, one(east[i0], hi))
            put(g, 0, c_inv[i0][seg])
            put(g, length, c_vert[i0][seg])
            put(g, 2 * length, one(west[i1], lo))
            put(g, 2 * length + 1, one(east[i1], hi))
            parts = (smoothed[y][0], smoothed[y][1], by_piece[i0], by_piece[i1])
            press(
                sp_row.at[s, p],
                [x[seg] for x in parts + (c_inv[i0], c_vert[i0])],
                [one(c_inv[i1], lo), one(c_inv[i1], hi)]
                + [one(west[i0], lo), one(east[i0], hi), one(west[i1], lo), one(east[i1], hi)],
            )
    for s in range(2):
        j0, j1 = (0, 1) if s == 0 else (half_c - 1, half_c - 2)
        out = west if s == 0 else east
        a, b, g = (st_col.at[s, q] for q in range(3))
        at0 = lambda x: x[j0 : j0 + 1]
        at1 = lambda x: x[j1 : j1 + 1]
        for y in range(rows):
            put(a, (y % 2) * length + y // 2, at0(smoothed[y][s]))
        put(a, 2 * length, at1(c_inv[0]))
        put(a, 2 * length + 1, at1(c_inv[half_r - 1]))
        for i in small:
            put(b, i, at0(by_tile[i]))
            put(b, length + i, at1(by_tile[i]))
            put(g, i, at0(c_inv[i]))
            put(g, length + i, at0(c_vert[i]))
        put(b, 2 * length, at0(north[0]))
        put(b, 2 * length + 1, at0(south[half_r - 1]))
        put(g, 2 * length, at1(north[0]))
        put(g, 2 * length + 1, at1(south[half_r - 1]))
        parts = [
            [at0(smoothed[2 * i][s]) for i in small],
            [at0(smoothed[2 * i + 1][s]) for i in small],
            [at0(x) for x in by_tile],
            [at1(x) for x in by_tile],
            [at0(x) for x in c_inv],
            [at0(x) for x in c_vert],
        ]
        press(
            sp_col.at[s],
            [jnp.concatenate(x, axis=0) for x in parts],
            [at1(c_inv[0]), at1(c_inv[half_r - 1]), at0(north[0]), at0(south[half_r - 1])]
            + [at1(north[0]), at1(south[half_r - 1])],
        )

    def stage_ends():
        for s in range(2):
            i0, i1 = (0, 1) if s == 0 else (half_r - 1, half_r - 2)
            out = north[0] if s == 0 else south[half_r - 1]
            for p in range(k):
                lo, hi = p * length, p * length + last
                one = lambda x, j: x[j : j + 1]
                for h in range(2):
                    j, j1 = (lo, lo + 1) if h == 0 else (hi, hi - 1)
                    side = west if h == 0 else east
                    x = ex_row.at[s, p, h]
                    put(x, 0, one(by_piece[i0], j))
                    put(x, 1, one(c_inv[i0], j))
                    put(x, 2, one(side[i0], j))
                    put(x, 3, one(side[i1], j))
                    put(x, 4, one(out, j))
                    put(x, 5, one(out, j1))
        for s in range(2):
            j0, j1 = (0, 1) if s == 0 else (half_c - 1, half_c - 2)
            out = west if s == 0 else east
            at0 = lambda x: x[j0 : j0 + 1]
            at1 = lambda x: x[j1 : j1 + 1]
            for h in range(2):
                i0, i1 = (0, 1) if h == 0 else (half_r - 1, half_r - 2)
                side = north[0] if h == 0 else south[half_r - 1]
                x = ex_col.at[s, h]
                put(x, 0, at0(by_tile[i0]))
                put(x, 1, at0(c_inv[i0]))
                put(x, 2, at0(side))
                put(x, 3, at1(side))
                put(x, 4, at0(out[i0]))
                put(x, 5, at0(out[i1]))

    pl.semaphore_wait(barrier, expected)
    traffic(True)

    def beside(y, b):
        x = smoothed[y][b]
        total = coupled[y][b] + smoothed[y][1 - b]
        if y > 0:
            total = total + smoothed[y - 1][b]
        if y < rows - 1:
            total = total + smoothed[y + 1][b]
        return total

    partial = fine(beside)
    traffic(False)

    pltpu.make_async_copy(tables, tables, table_sem.at[0]).wait()
    row_pick = pick_tables(tr)
    col_pick = pick_tables(2 + tc)

    def arrived(ref, sem):
        pltpu.make_async_copy(ref, ref, sem).wait()

    order = list(range(2 * length))[::-1] + [2 * length + 1, 2 * length]
    other = (
        list(range(length))[::-1]
        + list(range(length, 2 * length))[::-1]
        + [2 * length + 1, 2 * length]
    )
    sublane = lax.broadcasted_iota(jnp.int32, (block, LANES), 0)

    def flip_index(perm):
        index = sublane
        for at, source in enumerate(perm):
            index = jnp.where(sublane == at, source, index)
        return index

    flips = [flip_index(order), flip_index(other), flip_index(other)]

    def choose(read, pick, f, second=False):
        index, code = pick[2 if second else 0], pick[1]
        taken = None
        for t in range(4):
            moved = jnp.take_along_axis(read(4 * f + t), index, axis=1, mode="promise_in_bounds")
            taken = moved if taken is None else jnp.where(code == 4 * f + t, moved, taken)
        return taken

    def select(plainly, reverse, pick, group):
        straight = choose(plainly, pick, 0)
        turned = choose(reverse, pick, 1)
        if group is not None:
            turned = jnp.take_along_axis(turned, flips[group], axis=0, mode="promise_in_bounds")
        return jnp.where(pick[1] >= 4, turned, straight)

    def rows_of(tiles, first, final):
        parts = []
        for q, tile in enumerate(tiles):
            lo, hi = max(first, q * TILE), min(final, (q + 1) * TILE)
            if lo < hi:
                parts.append(tile[lo - q * TILE : hi - q * TILE])
        return parts

    def select_packed(plainly, reverse, pick):
        tiles = range(-(-packed_rows // TILE))
        results = []
        for f, read in ((0, plainly), (1, reverse)):
            main = [choose(lambda s: read(s, q), pick, f) for q in tiles]
            extra = [choose(lambda s: read(s, q), pick, f, True) for q in tiles]
            singles = None
            for j in range(full // spare):
                part = jnp.concatenate(rows_of(extra, used * j, used * (j + 1)), axis=0)
                same = pick[3][:used] == j
                singles = part if singles is None else jnp.where(same, part, singles)
            groups = []
            for q in range(3):
                lines = rows_of(main, 2 * length * q, 2 * length * (q + 1))
                lines.append(singles[2 * q : 2 * q + 2])
                if block > 2 * length + 2:
                    lines.append(jnp.zeros((block - 2 * length - 2, LANES), jnp.float32))
                groups.append(jnp.concatenate(lines, axis=0))
            results.append(groups)
        turned = [
            jnp.take_along_axis(x, flips[q], axis=0, mode="promise_in_bounds")
            for q, x in enumerate(results[1])
        ]
        return [jnp.where(pick[1] >= 4, x, y) for x, y in zip(turned, results[0])]

    @pl.when(is_row)
    def _():
        arrived(rx_row.at[:, :, 0:packed_rows], row_sem)
        for p in range(k):
            value = select_packed(
                lambda s, q: rx_row[s, p, q * TILE : (q + 1) * TILE],
                lambda s, q: rx_row[s, k - 1 - p, q * TILE : (q + 1) * TILE],
                row_pick,
            )
            for q in range(3):
                nb_row[tr, p, q] = value[q]
    @pl.when(is_col & jnp.logical_not(is_row))
    def _():
        arrived(rx_col, col_sem)
        for q in range(3):
            read = lambda s: rx_col[s, q]
            nb_col[tc, q] = select(read, read, col_pick, q)

    @pl.when(is_col & is_row)
    def _():
        swap = (tr != tc).astype(jnp.int32)

        def read(s, q):
            f, t = s // 4, s % 4
            at = 4 * (1 - swap) + t if f == 1 else 4 * swap + t
            piece = (tr if f == 0 else 1 - tr) * (k - 1)
            return rx_row[at, piece, q * TILE : (q + 1) * TILE]

        value = select_packed(read, read, col_pick)
        for q in range(3):
            nb_col[tc, q] = value[q]

    @pl.when(is_row)
    def _():
        for w in range(2):

            @pl.when(col_ok[w])
            def _():
                arrived(ry_row.at[w, :, 0:used], row_end_sem.at[w])
                read = lambda s: ry_row[w, s]
                corner[2 * tr + w] = select(read, read, row_pick, None)

    @pl.when(is_col)
    def _():
        for s in range(2):

            @pl.when(row_ok[s])
            def _():
                arrived(ry_col.at[s, :, 0:used], col_end_sem.at[s])
                read = lambda slot: ry_col[s, slot]
                value = select(read, read, col_pick, None)
                corner[2 * s + tc, 0:2, :] = value[0:2]
                corner[2 * s + tc, 2:4, :] = value[4:6]
                corner[2 * s + tc, 4:6, :] = value[2:4]

    for s in range(2):

        @pl.when(row_ok[s])
        def _():
            arrived(nb_row.at[s], nb_sem.at[s])

        @pl.when(col_ok[s])
        def _():
            arrived(nb_col.at[s], nb_sem.at[2 + s])

        for w in range(2):

            @pl.when(row_ok[s] & col_ok[w])
            def _():
                arrived(corner.at[2 * s + w, 0:used], corner_sem.at[2 * s + w])

    @pl.when(is_row & is_col)
    def _():
        at = 2 * tr + tc
        corner[at, 0:2, :] = jnp.zeros((2, LANES), jnp.float32)
        for q in range(2):
            rows_z = nb_col[tc, 1 + q]
            rows_x = nb_row[tr, tc * (k - 1), 1 + q]
            corner[at, 2 + q : 3 + q, :] = jnp.where(
                tr == 0, rows_z[2 * length : 2 * length + 1], rows_z[2 * length + 1 : 2 * length + 2]
            )
            corner[at, 4 + q : 5 + q, :] = jnp.where(
                tc == 0, rows_x[2 * length : 2 * length + 1], rows_x[2 * length + 1 : 2 * length + 2]
            )

    def zeros(count):
        return [jnp.zeros((count, LANES), jnp.float32)] if count else []

    def stack(lines, total):
        used = sum(x.shape[0] for x in lines)
        return jnp.concatenate(list(lines) + zeros(total - used), axis=0)

    tall_z = round_up(half_r, TILE)
    flat = 2 * length

    class Strip:
        pass

    def strip(read, pieces, ends, total, own):
        def gather(q, at):
            return stack([read(p, q, slice(at, at + length)) for p in range(pieces)], total)

        def sides(first, final):
            lines = []
            for p in range(pieces):
                lines += [first(p)] + zeros(length - 2) + [final(p)]
            return stack(lines, total)

        def lateral(q):
            return sides(
                lambda p: ends[0][q] if p == 0 else read(p - 1, 1 + q, slice(flat + 1, flat + 2)),
                lambda p: ends[1][q]
                if p == pieces - 1
                else read(p + 1, 1 + q, slice(flat, flat + 1)),
            )

        x = Strip()
        x.even, x.odd = gather(0, 0), gather(0, length)
        x.pair = x.even + x.odd
        inv1 = sides(
            lambda p: read(p, 0, slice(flat, flat + 1)),
            lambda p: read(p, 0, slice(flat + 1, flat + 2)),
        )
        x.inv, x.vert = gather(2, 0), gather(2, length)
        x.guess = gather(1, 0) + 0.25 * x.inv * (lateral(0) + own)
        x.inside = gather(1, length) + 0.25 * inv1 * lateral(1)
        return x

    def corner_row(s, w, at):
        return corner[2 * s + w, at : at + 1, :]

    row_strip = []
    for s in range(2):
        own = north[0] if s == 0 else south[half_r - 1]
        ends = [[corner_row(s, w, 2 + q) for q in range(2)] for w in range(2)]
        row_strip.append(
            strip(lambda p, q, rows_: nb_row[s, p, q, rows_, :], k, ends, height, own)
        )
    col_strip = []
    for w in range(2):
        j = w * (half_c - 1)
        faces = west if w == 0 else east
        own = stack([faces[i][j : j + 1] for i in small], tall_z)
        ends = [[corner_row(s, w, 4 + q) for q in range(2)] for s in range(2)]
        col_strip.append(
            strip(lambda p, q, rows_: nb_col[w, q, rows_, :], 1, ends, tall_z, own)
        )

    guess = []
    for i in small:
        lateral = jnp.where(edge_w, col_strip[0].pair[i : i + 1], 0.0)
        lateral = lateral + jnp.where(edge_e, col_strip[1].pair[i : i + 1], 0.0)
        if i == 0:
            lateral = lateral + row_strip[0].pair
        if i == half_r - 1:
            lateral = lateral + row_strip[1].pair
        guess.append(by_tile[i] + 0.25 * c_inv[i] * lateral)

    row_side = [[None] * 2 for _ in range(2)]
    col_side = [[None] * 2 for _ in range(2)]
    for s in range(2):
        for w in range(2):
            faces = nb_row[s, w * (k - 1), 1, flat + w : flat + w + 1, :]
            faces = faces + nb_col[w, 1, flat + s : flat + s + 1, :]
            there = corner_row(s, w, 0) + 0.25 * corner_row(s, w, 1) * faces
            tip = (r == s * (nr - 1)) & (c == w * (nc - 1))
            jr, jc = w * (half_c - 1), s * (half_r - 1)
            row_side[s][w] = jnp.where(tip, col_strip[w].guess[jc : jc + 1], there)
            col_side[w][s] = jnp.where(tip, row_strip[s].guess[jr : jr + 1], there)

    def relax(x, ends, own, count):
        total = x.guess.shape[0]
        at = lax.broadcasted_iota(jnp.int32, (total, LANES), 0)
        around = x.inside + own
        around = around + jnp.where(at == 0, ends[0], pltpu.roll(x.guess, 1, 0))
        around = around + jnp.where(at == count - 1, ends[1], pltpu.roll(x.guess, total - 1, 0))
        column = x.vert * upper(x.guess) + lower(x.vert) * lower(x.guess)
        return (2.0 - relaxation) * x.guess + x.inv * (0.25 * around + column)

    row_fix = [
        relax(row_strip[s], row_side[s], guess[s * (half_r - 1)], half_c) for s in range(2)
    ]
    col_fix = []
    for w in range(2):
        j = w * (half_c - 1)
        own = stack([guess[i][j : j + 1] for i in small], tall_z)
        col_fix.append(relax(col_strip[w], col_side[w], own, half_r))

    def from_left(x, line):
        return jnp.where(edge_w, line, pltpu.roll(x, 1, 0))

    def from_right(x, line):
        return jnp.where(edge_e, line, pltpu.roll(x, height - 1, 0))

    correction = []
    for i in small:
        x = guess[i]
        around = from_left(x, col_strip[0].guess[i : i + 1])
        around = around + from_right(x, col_strip[1].guess[i : i + 1])
        around = around + (guess[i - 1] if i > 0 else row_strip[0].guess)
        around = around + (guess[i + 1] if i < half_r - 1 else row_strip[1].guess)
        levels_part = c_vert[i] * upper(x) + c_low[i] * lower(x)
        correction.append((2.0 - relaxation) * x + c_inv[i] * (0.25 * around + levels_part))
        small_ref[i] = correction[i]

    def outer(y, b):
        at = (y % 2) * length + y // 2
        source = col_strip[b]
        line = (source.even if y % 2 == 0 else source.odd)[y // 2 : y // 2 + 1]
        if b == 0:
            total = partial[y][b] + from_left(smoothed[y][1], line)
        else:
            total = partial[y][b] + from_right(smoothed[y][0], line)
        if y == 0:
            total = total + (row_strip[0].even if b == 0 else row_strip[0].odd)
        if y == rows - 1:
            total = total + (row_strip[1].even if b == 0 else row_strip[1].odd)
        return total

    c_up = [upper(x) for x in correction]
    c_down = [lower(x) for x in correction]
    left = [from_left(correction[i], col_fix[0][i : i + 1]) for i in small]
    right = [from_right(correction[i], col_fix[1][i : i + 1]) for i in small]
    for y in range(rows):
        i = y // 2
        next_i = i - 1 if y % 2 == 0 else i + 1
        for b in range(2):
            total = outer(y, b) + 2.0 * correction[i]
            total = total + vertical[y][b] * c_up[i] + low_vert[y][b] * c_down[i]
            if next_i < 0:
                total = total + row_fix[0]
            elif next_i >= half_r:
                total = total + row_fix[1]
            else:
                total = total + correction[next_i]
            total = total + (left if b == 0 else right)[i]
            first = (2.0 - relaxation) * smoothed[y][b] + (1.0 - relaxation) * correction[i]
            spread[y, pl.ds(b, height, stride=2), :] = first + inverse[y][b] * total


def unpack(spread, small_ref, sol_hbm, corr_hbm, sol, corr, sem):
    panels, _, cols, levels = sol.shape
    half_c = corr.shape[2]
    for p in range(panels):
        lanes = slice(p * levels, (p + 1) * levels)
        sol[p] = spread[:, :cols, lanes]
        pltpu.make_async_copy(sol.at[p], sol_hbm.at[p], sem.at[0]).start()
    for p in range(panels):
        lanes = slice(p * levels, (p + 1) * levels)
        corr[p] = small_ref[:, :half_c, lanes]
    last = pltpu.make_async_copy(corr, corr_hbm, sem.at[1])
    last.start()
    pltpu.make_async_copy(sol, sol_hbm, sem.at[0]).wait()
    last.wait()


def solution(mesh):
    nr, nc = mesh.shape["tx"], mesh.shape["ty"]

    def shards(residual, density, gain, vertical, edge_panel, edge_side, edge_flip):
        panels, rows, cols, levels = residual.shape
        k = cols // rows
        assert cols == k * rows and rows % 2 == 0 and panels * levels <= LANES
        assert rows >= 6 and nr > 1 and nc > 1
        block = round_up(rows + 2, TILE)
        dense = round_up(3 * rows, TILE)
        spare = LANES - panels * levels
        assert spare % levels == 0 and panels * levels % spare == 0
        assert 2 * panels * levels <= rows * spare
        height = round_up(cols // 2, TILE)
        tall = 2 * height
        f32 = jnp.float32
        spread, small = pl.pallas_call(
            functools.partial(kernel, nr, nc),
            out_shape=(
                pltpu.VMEM((rows, tall, LANES), f32),
                pltpu.VMEM((rows // 2, height, LANES), f32),
            ),
            in_specs=[pl.BlockSpec(memory_space=pl.ANY)] * 7,
            out_specs=(pl.BlockSpec(memory_space=pltpu.VMEM),) * 2,
            scratch_shapes=[
                pltpu.VMEM((4, panels, rows, cols, levels), f32),
                pltpu.SMEM((3,) + edge_panel.T.shape, jnp.int32),
                pltpu.VMEM((3, rows, tall, LANES), f32),
                pltpu.VMEM((3, k, 3, block, LANES), f32),
                pltpu.VMEM((3, 3, block, LANES), f32),
                pltpu.VMEM((3, k, dense, LANES), f32),
                pltpu.VMEM((3, dense, LANES), f32),
                pltpu.VMEM((3, k, 2, TILE, LANES), f32),
                pltpu.VMEM((3, 2, TILE, LANES), f32),
                pltpu.VMEM((3, k, 3, block, LANES), f32),
                pltpu.VMEM((3, 3, block, LANES), f32),
                pltpu.VMEM((5, TILE, LANES), f32),
                pltpu.VMEM((8, k, dense, LANES), f32),
                pltpu.VMEM((8, 3, block, LANES), f32),
                pltpu.VMEM((2, 8, TILE, LANES), f32),
                pltpu.VMEM((2, 8, TILE, LANES), f32),
                pltpu.SemaphoreType.DMA((2,)),
                pltpu.SemaphoreType.DMA((1,)),
                pltpu.SemaphoreType.DMA((1,)),
                pltpu.SemaphoreType.DMA((4,)),
                pltpu.SemaphoreType.DMA((4,)),
                pltpu.SemaphoreType.DMA,
                pltpu.SemaphoreType.DMA,
                pltpu.SemaphoreType.DMA((2,)),
                pltpu.SemaphoreType.DMA((2,)),
            ],
            compiler_params=pltpu.CompilerParams(collective_id=0, has_side_effects=True),
        )(residual, density, gain, vertical, edge_panel.T, edge_side.T, edge_flip.T)
        spread = pltpu.with_memory_space_constraint(spread, pltpu.VMEM)
        small = pltpu.with_memory_space_constraint(small, pltpu.VMEM)
        return pl.pallas_call(
            unpack,
            out_shape=(
                jax.ShapeDtypeStruct(residual.shape, f32),
                jax.ShapeDtypeStruct((panels, rows // 2, cols // 2, levels), f32),
            ),
            in_specs=[pl.BlockSpec(memory_space=pltpu.VMEM)] * 2,
            out_specs=(pl.BlockSpec(memory_space=pl.ANY),) * 2,
            scratch_shapes=[
                pltpu.VMEM(residual.shape, f32),
                pltpu.VMEM((panels, rows // 2, cols // 2, levels), f32),
                pltpu.SemaphoreType.DMA((2,)),
            ],
        )(spread, small)

    fields = P(None, "tx", "ty", None)
    return jax.shard_map(
        shards,
        mesh=mesh,
        in_specs=(fields,) * 4 + (P(),) * 3,
        out_specs=(fields, fields),
        check_vma=False,
    )
```
